32 devices in a mesh: groups: 2 (over x), ctx: 16 (over z, y, core).
Axes of the slice: x: 2, y: 2, z: 4, core: 2. Of those that a mesh axis runs over, the one named last changes fastest.
Arguments:
- ssm_input: bfloat16 [8192, 4096], P(('groups', 'ctx')), parts along dimension 0, may hold values from -18 to 18
- gate_input: bfloat16 [8192, 4096], P(('groups', 'ctx')), parts along dimension 0, may hold values from -6 to 6
- bc_input: bfloat16 [8192, 1024], P(('groups', 'ctx')), parts along dimension 0, may hold values from -6 to 6
- dt_raw: float32 [8192, 64], P(('groups', 'ctx')), parts along dimension 0, may hold values from -4 to 16
- offsets: int32 [38], P('groups'), parts along dimension 0, may hold values from 0 to 4096, as said below
- owners: int32 [36], P('groups'), parts along dimension 0, may hold values from 0 to 15, as said below
- conv_weight: float32 [4, 5120], replicated, may hold values from -3 to 3
- convolution_bias: float32 [5120], replicated, may hold values from -3 to 3
- a_log: float32 [64], replicated, may hold values from -3.6 to 2.5
- dt_bias: float32 [64], replicated, may hold values from -6.2 to -5.2
- d_skip: float32 [64], replicated, may hold values from 0.5 to 1.5
- norm_weight: float32 [4096], replicated, may hold values from 0.25 to 1.75
Outputs:
- gated_out: bfloat16 [8192, 4096], P(('groups', 'ctx')), parts along dimension 0
- decode_states: float32 [64, 64, 64, 128], P(('groups', 'ctx')), parts along dimension 0
The draws below stay inside these ranges and needn't reach their ends.
There are 2 independent parts, one for each index of `groups`. The reference program is written for one: setup_inputs(seed, part) draws one part's arguments, and reference() takes and returns one part's arrays. A program takes and returns all parts, laid end to end along the dimension named above; an argument that names none is the same for every part. Nothing has to cross between parts.
Inputs may be any that keep to these rules, and one draw needn't show every extreme that they name: offsets[0] is 0, offsets[18] is 4096 and the offsets rise strictly; every document holds at most 512 tokens and one holds exactly 512; at most 4 documents end on the 256 tokens of one device, and exactly 4 on some device. `owners`: each device owns at most 2 documents, and some device exactly 2.
All inputs are finite; a program needn't handle non-finite values.
Results may differ from the reference program's by a relative error of at most 0.001.
The reference program's roundings to bfloat16 on the way (of `conv_out` and `weights`) count: a program that leaves them out, or rounds other values in their place, can miss the bound.
Values may be sent and summed in bfloat16 or wider, within the bound.
A program may use at most 128 MiB of HBM per device.

```python
import math
import jax
import jax.numpy as jnp
from jax import lax

HEAD_COUNT = 64
HEAD_DIM = 64
STATE_DIM = 128
KERNEL_WIDTH = 4
BLOCK_LEN = 256
END_SLOTS = 4
OWNER_SLOTS = 2
TOK_DEV = 256
GROUP_COUNT = 4
INNER_DIM = 4096
CHANNELS = 5120
GROUP_SEQUENCE = 4096
DOC_COUNT = 18
OWNER_ROWS = 32
N_CTX = 16


def draw_offsets(key, part):
    keys = jax.random.split(key, 4)
    span = N_CTX // 8
    cell_len = TOK_DEV // END_SLOTS
    first_dev = jax.random.randint(keys[0], (), 0, N_CTX - span - 1)
    picked = jax.random.randint(keys[1], (), 0, N_CTX - span - 2)
    dense_dev = jnp.where(picked < first_dev, picked, picked + span + 1)
    last_dev = first_dev + span
    devices = jnp.arange(N_CTX, dtype=jnp.int32)
    cells = jnp.arange(END_SLOTS, dtype=jnp.int32)
    cell_pick = jax.random.randint(keys[2], (N_CTX,), 0, END_SLOTS)
    jitter = jax.random.randint(keys[3], (N_CTX, END_SLOTS), 1, cell_len + 1)
    cell_pick = cell_pick.at[last_dev].set(cell_pick[first_dev])
    jitter = jitter.at[last_dev].set(jitter[first_dev])
    cell_pick = jnp.where(devices == N_CTX - 1, cell_pick % (END_SLOTS - 1), cell_pick)
    inside = (devices > first_dev) & (devices < last_dev)
    single = (cells[None, :] == cell_pick[:, None]) & jnp.logical_not(inside)[:, None]
    flagged = jnp.where((devices == dense_dev)[:, None], True, single)
    places = devices[:, None] * TOK_DEV + cells[None, :] * cell_len + jitter
    flat_flag = flagged.reshape(-1)
    flat_place = places.reshape(-1).astype(jnp.int32)
    order_rank = jnp.cumsum(flat_flag.astype(jnp.int32)) - 1
    target = jnp.where(flat_flag, order_rank, DOC_COUNT - 1)
    inner_cuts = jnp.zeros((DOC_COUNT - 1,), jnp.int32).at[target].set(flat_place, mode='drop')
    return jnp.concatenate([jnp.zeros((1,), jnp.int32), inner_cuts, jnp.full((1,), GROUP_SEQUENCE, jnp.int32)])


def draw_owners(key, part):
    keys = jax.random.split(key, 3)
    shuffled = jax.random.permutation(keys[0], N_CTX).astype(jnp.int32)
    first_pair = jax.random.randint(keys[1], (), 0, DOC_COUNT - 3)
    second_pair = first_pair + 2 + jax.random.randint(keys[2], (), 0, DOC_COUNT - 3 - first_pair)
    doc_ids = jnp.arange(DOC_COUNT, dtype=jnp.int32)
    position = doc_ids - (doc_ids > first_pair).astype(jnp.int32) - (doc_ids > second_pair).astype(jnp.int32)
    return shuffled[position].astype(jnp.int32)


def draw_a_log(key, part):
    keys = jax.random.split(key, 2)
    choose = jax.random.uniform(keys[0], (HEAD_COUNT,))
    level = jax.random.uniform(keys[1], (HEAD_COUNT,))
    share = 0.5
    slow_rate = math.log(0.03) + level * (math.log(0.09) - math.log(0.03))
    fast_rate = math.log(5.0) + level * (math.log(12.0) - math.log(5.0))
    return jnp.where(choose < share, fast_rate, slow_rate).astype(jnp.float32)


def draw_dt_raw(key, part):
    keys = jax.random.split(key, 3)
    block_len = TOK_DEV // 2
    gaussian_perturbation = 0.3 * jax.random.truncated_normal(keys[0], -6.0, 6.0, (GROUP_SEQUENCE, HEAD_COUNT))
    shifts = jax.random.uniform(keys[1], (GROUP_SEQUENCE // block_len,), minval=-0.7, maxval=0.7)
    displaced_lines = jnp.repeat(shifts, block_len)
    sequence_locations = jax.random.randint(keys[2], (max(N_CTX // 8, 1),), 0, GROUP_SEQUENCE)
    sequence_stretch = jnp.any(jnp.arange(GROUP_SEQUENCE)[:, None] == sequence_locations[None, :], 1)
    quantity_elements = gaussian_perturbation + displaced_lines[:, None] + jnp.where(sequence_stretch, 12.5, 0.0)[:, None]
    return quantity_elements.astype(jnp.float32)


def draw_ssm_input(key, part):
    keys = jax.random.split(key, 2)
    columns = jnp.exp(jax.random.uniform(keys[1], (INNER_DIM,), minval=math.log(0.3), maxval=math.log(3.0)))
    quantity_elements = jax.random.truncated_normal(keys[0], -6.0, 6.0, (GROUP_SEQUENCE, INNER_DIM))
    return (quantity_elements * columns[None, :]).astype(jnp.bfloat16)


def levels(own_key, shape, shards, low, top_value):
    loudness = 1.0
    for axis_at, blocks in shards:
        draws = jax.random.uniform(jax.random.fold_in(jax.random.fold_in(own_key, 6), axis_at), (blocks,), jnp.float32, low / len(shards), top_value / len(shards))
        loudness = loudness * jnp.repeat(jnp.exp(draws), shape[axis_at] // blocks).reshape((-1,) + (1,) * (len(shape) - 1 - axis_at))
    return loudness


def noise(own_key, shape, spread, bound, pieces=(), kind=jnp.bfloat16):
    loudness = levels(own_key, shape, pieces, -0.22, 0.18) if pieces else 1.0
    values = jax.random.normal(own_key, shape, jnp.float32) * spread * loudness
    return jnp.minimum(jnp.maximum(values, -bound), bound).astype(kind)


def setup_inputs(seed: int = 0, part: int = 0) -> dict:
    splits = jax.random.split(jax.random.key(seed), 13)
    part_keys = jax.random.split(jax.random.fold_in(splits[12], part), 13)
    return {
        "ssm_input": draw_ssm_input(jax.random.fold_in(jax.random.fold_in(splits[12], part), 71), part),
        "gate_input": noise(part_keys[1], (GROUP_SEQUENCE, INNER_DIM), 1.0, 6.0, ((0, 16),)),
        "bc_input": noise(part_keys[2], (GROUP_SEQUENCE, 2 * GROUP_COUNT * STATE_DIM), 1.0, 6.0, ((0, 16),)),
        "dt_raw": draw_dt_raw(jax.random.fold_in(jax.random.fold_in(splits[12], part), 71), part),
        "offsets": draw_offsets(jax.random.fold_in(jax.random.fold_in(splits[12], part), 71), part),
        "owners": draw_owners(jax.random.fold_in(jax.random.fold_in(splits[12], part), 71), part),
        "conv_weight": noise(splits[6], (KERNEL_WIDTH, CHANNELS), KERNEL_WIDTH ** -0.5, 3.0, (), jnp.float32),
        "convolution_bias": noise(splits[7], (CHANNELS,), 0.5, 3.0, (), jnp.float32),
        "a_log": draw_a_log(jax.random.fold_in(splits[12], 71), part),
        "dt_bias": jnp.clip(jax.random.uniform(splits[9], (HEAD_COUNT,), jnp.float32, -6.2, -5.2), -6.2, -5.2),
        "d_skip": jnp.clip(jax.random.uniform(splits[10], (HEAD_COUNT,), jnp.float32, 0.5, 1.5), 0.5, 1.5),
        "norm_weight": jnp.clip(1.0 + 0.15 * jax.random.normal(splits[11], (INNER_DIM,), jnp.float32), 0.25, 1.75),
    }


def conv_act(conv_in, rim_rows, tok_index, doc_start, conv_weight, convolution_bias):
    length = conv_in.shape[0]
    padded = jnp.concatenate([rim_rows, conv_in], 0)
    total = jnp.zeros(conv_in.shape, jnp.float32) + convolution_bias[None, :]
    for tap_index in range(KERNEL_WIDTH):
        source = tok_index - (KERNEL_WIDTH - 1) + tap_index
        admissible = jnp.where(source >= doc_start, 1.0, 0.0).astype(jnp.float32)
        total = total + admissible[:, None] * conv_weight[tap_index][None, :] * padded[tap_index:tap_index + length].astype(jnp.float32)
    return jax.nn.silu(total).astype(jnp.bfloat16)

def block_terms(ssm_x, b_proj, c_proj, dt_val, log_decay, positions, doc_index, doc_start, slot_end, slot_start, slot_live):
    length, heads, head_dim = ssm_x.shape
    groups = b_proj.shape[1]
    per_group = heads // groups
    slots = slot_end.shape[0]
    cum_decay = jnp.cumsum(log_decay, axis=0)
    scores = jnp.einsum('tgn,sgn->gts', c_proj.astype(jnp.float32), b_proj.astype(jnp.float32), precision=lax.Precision.HIGHEST)
    causal = (positions[None, :] <= positions[:, None]) & (doc_index[None, :] == doc_index[:, None])
    cum_heads = cum_decay.T
    gaps = cum_heads[:, :, None] - cum_heads[:, None, :]
    decay = jnp.exp(jnp.where(causal[None], gaps, -jnp.inf))
    weights = scores[:, None] * decay.reshape(groups, per_group, length, length) * dt_val.T.reshape(groups, per_group, 1, length)
    weights = weights.astype(jnp.bfloat16)
    grouped_x = ssm_x.reshape(length, groups, per_group, head_dim)
    intra = jnp.einsum('gjts,sgjp->tgjp', weights.astype(jnp.float32), grouped_x.astype(jnp.float32), precision=lax.Precision.HIGHEST)
    first_pos = positions[0]
    end_local = jnp.clip(slot_end - first_pos, 0, length - 1)
    cum_end = cum_decay[end_local]
    covered = slot_live[:, None] & (positions[None, :] >= slot_start[:, None]) & (positions[None, :] <= slot_end[:, None])
    slot_decay = jnp.exp(jnp.where(covered[:, :, None], cum_end[:, None, :] - cum_decay[None], -jnp.inf)) * dt_val[None]
    weighted_x = (slot_decay[..., None] * ssm_x[None].astype(jnp.float32)).astype(jnp.bfloat16)
    local = jnp.einsum('iqgjp,qgn->igjpn', weighted_x.reshape(slots, length, groups, per_group, head_dim).astype(jnp.float32), b_proj.astype(jnp.float32), precision=lax.Precision.HIGHEST)
    carried = jnp.where((slot_live & (slot_start < first_pos))[:, None], jnp.exp(cum_end), 0.0).reshape(slots, groups, per_group)
    cont = jnp.where((doc_start < first_pos)[:, None], jnp.exp(cum_decay), 0.0).reshape(length, groups, per_group)
    return (intra, local, carried, cont)

def gate_norm(y_sum, gate_rows, norm_weight):
    length = y_sum.shape[0]
    groups = y_sum.shape[1]
    gated = y_sum.reshape(length, -1) * jax.nn.silu(gate_rows.astype(jnp.float32))
    grouped = gated.reshape(length, groups, -1)
    normed = grouped * lax.rsqrt(lax.optimization_barrier(jnp.mean(grouped * grouped, axis=-1, keepdims=True)) + 1e-05)
    return (normed.reshape(length, -1) * norm_weight[None, :]).astype(jnp.bfloat16)

def reference(ssm_input, gate_input, bc_input, dt_raw, offsets, owners, conv_weight, convolution_bias, a_log, dt_bias, d_skip, norm_weight):
    tok_index = jnp.arange(GROUP_SEQUENCE, dtype=jnp.int32)
    below = offsets[None, :] <= tok_index[:, None]
    doc_index = (lax.optimization_barrier(jnp.sum(below.astype(jnp.int32), 1)) - 1).astype(jnp.int32)
    doc_start = lax.optimization_barrier(jnp.max(jnp.where(below, offsets[None, :], 0), 1)).astype(jnp.int32)
    conv_in = jnp.concatenate([ssm_input, bc_input], 1)
    rim_rows = jnp.zeros((KERNEL_WIDTH - 1, CHANNELS), jnp.bfloat16)
    conv_out = conv_act(conv_in, rim_rows, tok_index, doc_start, conv_weight, convolution_bias)
    group_state = GROUP_COUNT * STATE_DIM
    per_group = HEAD_COUNT // GROUP_COUNT
    ssm_x = conv_out[:, :INNER_DIM].reshape(GROUP_SEQUENCE, HEAD_COUNT, HEAD_DIM)
    b_proj = conv_out[:, INNER_DIM:INNER_DIM + group_state].reshape(GROUP_SEQUENCE, GROUP_COUNT, STATE_DIM)
    c_proj = conv_out[:, INNER_DIM + group_state:].reshape(GROUP_SEQUENCE, GROUP_COUNT, STATE_DIM)
    dt_val = jax.nn.softplus(dt_raw + dt_bias[None, :])
    log_decay = -dt_val * jnp.exp(a_log)[None, :]
    doc_ends = (offsets[1:] - 1).astype(jnp.int32)
    doc_ids = jnp.arange(DOC_COUNT, dtype=jnp.int32)
    earlier = doc_ids[None, :] < doc_ids[:, None]
    owner_rank = lax.optimization_barrier(jnp.sum(((owners[None, :] == owners[:, None]) & earlier).astype(jnp.int32), 1))
    dest_row = (owners * OWNER_SLOTS + owner_rank).astype(jnp.int32)
    slot_ids = jnp.arange(END_SLOTS, dtype=jnp.int32)

    def window_rows(quantity_elements, first):
        return lax.dynamic_slice_in_dim(quantity_elements, first, BLOCK_LEN, 0)

    def run_block(carry, block_index):
        state_in, store = carry
        first = (block_index * BLOCK_LEN).astype(jnp.int32)
        positions = first + jnp.arange(BLOCK_LEN, dtype=jnp.int32)
        in_block = (doc_ends >= first) & (doc_ends < first + BLOCK_LEN)
        order_rank = jnp.cumsum(in_block.astype(jnp.int32)) - 1
        match = (order_rank[None, :] == slot_ids[:, None]) & in_block[None, :]
        slot_live = jnp.any(match, 1)
        slot_doc = lax.optimization_barrier(jnp.sum(match.astype(jnp.int32) * doc_ids[None, :], 1)).astype(jnp.int32)
        slot_end = jnp.where(slot_live, doc_ends[slot_doc], first).astype(jnp.int32)
        slot_start = offsets[slot_doc]
        block_start = window_rows(doc_start, first)
        ext_end = jnp.concatenate([slot_end, jnp.reshape(first + BLOCK_LEN - 1, (1,)).astype(jnp.int32)])
        ext_start = jnp.concatenate([slot_start, block_start[-1:]])
        ext_live = jnp.concatenate([slot_live, jnp.ones((1,), jnp.bool_)])
        x_block = window_rows(ssm_x, first)
        c_block = window_rows(c_proj, first)
        intra, local, carried, cont = block_terms(x_block, window_rows(b_proj, first), c_block, window_rows(dt_val, first), window_rows(log_decay, first), positions, window_rows(doc_index, first), block_start, ext_end, ext_start, ext_live)
        states = local + carried[..., None, None] * state_in[None]
        inter = jnp.einsum('tgn,gjpn->tgjp', c_block.astype(jnp.float32), state_in, precision=lax.Precision.HIGHEST) * cont[..., None]
        skip = d_skip.reshape(GROUP_COUNT, per_group)[None, :, :, None] * x_block.reshape(BLOCK_LEN, GROUP_COUNT, per_group, HEAD_DIM).astype(jnp.float32)
        out_rows = gate_norm(intra + inter + skip, window_rows(gate_input, first), norm_weight)
        for slot_index in range(END_SLOTS):
            target = dest_row[slot_doc[slot_index]]
            current = lax.dynamic_index_in_dim(store, target, 0, keepdims=False)
            update = jnp.where(slot_live[slot_index], states[slot_index].reshape(HEAD_COUNT, HEAD_DIM, STATE_DIM), current)
            store = lax.dynamic_update_index_in_dim(store, update, target, 0)
        return ((states[END_SLOTS], store), out_rows)
    init_state = jnp.zeros((GROUP_COUNT, per_group, HEAD_DIM, STATE_DIM), jnp.float32)
    init_store = jnp.zeros((OWNER_ROWS, HEAD_COUNT, HEAD_DIM, STATE_DIM), jnp.float32)
    carry_out, out_blocks = lax.scan(run_block, (init_state, init_store), jnp.arange(GROUP_SEQUENCE // BLOCK_LEN, dtype=jnp.int32))
    gated_out = out_blocks.reshape(GROUP_SEQUENCE, INNER_DIM)
    return (gated_out, carry_out[1])
```

```python
import functools
import math
import jax
import jax.numpy as jnp
from jax import lax
from jax.experimental import pallas as pl
from jax.experimental.pallas import tpu as pltpu
from jax.sharding import PartitionSpec as P

GROUP_HEADS = 16
KERNEL_WIDTH = 4
OWNER_SLOTS = 2
BLOCK_HEADS = 4
RIM = 16
SCALE_ROWS = 16
LEVELS = 8.0
CODE_MAX = 32767.0
VMEM_LIMIT = 56 * 1024 * 1024
MESH = pl.DeviceIdType.MESH


def encode(value):
    rows, lanes = value.shape
    parts = value.reshape(rows // SCALE_ROWS, SCALE_ROWS, lanes)
    top = jnp.max(jnp.abs(parts), axis=1)
    level = jnp.ceil(jnp.log(jnp.maximum(top, 1e-30)) * (LEVELS / math.log(2.0)))
    unit = jnp.exp2(level * (-1.0 / LEVELS)) * CODE_MAX
    coded = jnp.clip(jnp.round(parts * unit[:, None, :]), -CODE_MAX, CODE_MAX).reshape(rows, lanes)
    if level.shape[0] < SCALE_ROWS:
        level = jnp.concatenate([level, jnp.zeros((SCALE_ROWS - level.shape[0], lanes), jnp.float32)], 0)
    return coded.astype(jnp.int32).astype(jnp.int16), level.astype(jnp.int32).astype(jnp.int16)


def decode(coded, level):
    rows, lanes = coded.shape
    unit = jnp.exp2(level.astype(jnp.int32).astype(jnp.float32) * (1.0 / LEVELS)) * (1.0 / CODE_MAX)
    unit = unit[:rows // SCALE_ROWS]
    parts = coded.astype(jnp.int32).astype(jnp.float32).reshape(rows // SCALE_ROWS, SCALE_ROWS, lanes)
    return (parts * unit[:, None, :]).reshape(rows, lanes)


def conv_silu(x, rim, mask, weight, bias):
    x = x.astype(jnp.float32)
    padded = jnp.concatenate([rim.astype(jnp.float32), x], 0)
    total = bias + weight[0:1] * (mask[:, 0:1] * pltpu.roll(padded, 3, 0)[RIM:])
    total = total + weight[1:2] * (mask[:, 1:2] * pltpu.roll(padded, 2, 0)[RIM:])
    total = total + weight[2:3] * (mask[:, 2:3] * pltpu.roll(padded, 1, 0)[RIM:])
    total = total + weight[3:4] * x
    return (total / (1.0 + jnp.exp(-total))).astype(jnp.bfloat16)


def spread(k, count):
    half = (k + 1) // 2
    return count // 2 + half * (1 - 2 * (k % 2))


def enter(axis, me, devices):
    barrier = pltpu.get_barrier_semaphore()

    @pl.loop(1, devices)
    def _(by):
        pl.semaphore_signal(barrier, inc=1, device_id={axis: (me + by) % devices}, device_id_type=MESH)

    return barrier


def front_kernel(devices, groups, relays, x_ref, bc_ref, mask_ref, wx_ref, wbc_ref, end_ref, factor_ref, last_ref,
                 through_ref, xs_ref, bconv_ref, c_ref, in_ref, gx_ref, gb_ref, gd_ref,
                 rimx_scr, rimbc_scr, wt_scr, blast_scr, local_scr, code_scr, rec_scr, bsend_scr,
                 rim_send, rim_recv, x_send, x_recv, b_send, b_recv, f_send, f_recv, d_send, d_recv, hand_send,
                 hand_recv, own_sem):
    me = lax.axis_index("ctx")
    length, inner = x_ref.shape
    blocks = wx_ref.shape[0]
    width = inner // blocks
    state_dim = blast_scr.shape[2]
    heads = width // (inner // (blocks * BLOCK_HEADS))
    per_block = devices // blocks
    slice_width = width // per_block
    per_group = devices // groups
    blocks_per_group = blocks // groups
    quarter = me // per_group
    place = me % per_group

    def remote(src, dst, send, recv, to):
        return pltpu.make_async_remote_copy(src_ref=src, dst_ref=dst, send_sem=send, recv_sem=recv,
                                            device_id={"ctx": to}, device_id_type=MESH)

    barrier = enter("ctx", me, devices)

    @pl.when(me == 0)
    def _():
        rimx_scr[...] = jnp.zeros_like(rimx_scr)
        rimbc_scr[...] = jnp.zeros_like(rimbc_scr)
        in_ref[...] = jnp.zeros_like(in_ref)
        rec_scr[...] = jnp.zeros_like(rec_scr)

    pl.semaphore_wait(barrier, devices - 1)

    right = (me + 1) % devices

    def rim_copies():
        return (remote(x_ref.at[pl.ds(length - RIM, RIM)], rimx_scr, rim_send.at[0], rim_recv.at[0], right),
                remote(bc_ref.at[pl.ds(length - RIM, RIM)], rimbc_scr, rim_send.at[1], rim_recv.at[1], right))

    @pl.when(me < devices - 1)
    def _():
        for copy in rim_copies():
            copy.start()

    def d_copy(to):
        return remote(factor_ref.at[to], gd_ref.at[me], d_send.at[to], d_recv.at[me], to)

    @pl.loop(0, devices)
    def _(k):
        to = (me + spread(k, devices)) % devices

        @pl.when(to != me)
        def _():
            d_copy(to).start()

    own_d = pltpu.make_async_copy(factor_ref.at[me], gd_ref.at[me], own_sem.at[0])
    own_d.start()

    @pl.when(me > 0)
    def _():
        for copy in rim_copies():
            copy.wait_recv()

    mask = mask_ref[...]
    last = last_ref[...]
    for part in range(2 * groups):
        cols = slice(part * state_dim, (part + 1) * state_dim)
        value = conv_silu(bc_ref[:, cols], rimbc_scr[:, cols], mask, wbc_ref[:KERNEL_WIDTH, cols],
                          wbc_ref[KERNEL_WIDTH:KERNEL_WIDTH + 1, cols])
        if part < groups:
            bconv_ref[:, cols] = value
            bsend_scr[part] = value
            blast_scr[part] = (value.astype(jnp.float32) * last).astype(jnp.bfloat16)
        else:
            c_ref[:, (part - groups) * state_dim:(part - groups + 1) * state_dim] = value

    def b_copy(group):
        return remote(bsend_scr.at[group], gb_ref.at[me], b_send.at[group], b_recv.at[me],
                      group * per_group + place)

    own_b = pltpu.make_async_copy(bsend_scr.at[quarter], gb_ref.at[me], own_sem.at[1])
    own_b.start()
    for group in range(groups):
        @pl.when(quarter != group)
        def _():
            b_copy(group).start()

    def x_copy(to):
        return remote(wt_scr.at[pl.ds(pl.multiple_of(to * slice_width, slice_width), slice_width)], gx_ref.at[me],
                      x_send.at[to], x_recv.at[me], to)

    def one_block(k):
        block = (me // per_block + spread(k, blocks)) % blocks
        cols = pl.ds(pl.multiple_of(block * width, width), width)
        weight = wx_ref[block]
        xs = conv_silu(x_ref[:, cols], rimx_scr[:, cols], mask, weight[:KERNEL_WIDTH],
                       weight[KERNEL_WIDTH:KERNEL_WIDTH + 1])
        xs_ref[:, cols] = xs
        x_t = xs.astype(jnp.float32).T.reshape(heads, width // heads, length)
        weighted = (x_t * end_ref[block][:heads][:, None, :]).astype(jnp.bfloat16).reshape(width, length)
        wt_scr[cols, :] = weighted

        @pl.loop(0, per_block)
        def _(part):
            to = block * per_block + part

            @pl.when(to != me)
            def _():
                x_copy(to).start()

        local = jnp.dot(weighted, blast_scr[block // blocks_per_group], preferred_element_type=jnp.float32)
        local_scr[block] = local
        code_scr[block, :width], code_scr[block, width:] = encode(local)

    half = blocks // 2

    @pl.loop(0, half)
    def _(k):
        one_block(k)

    def f_copy(src, frm, by):
        to = quarter * per_group + (place + by) % per_group
        return remote(src, gb_ref.at[frm], f_send.at[frm // per_group, by], f_recv.at[frm], to)

    own_b.wait()
    for frm_quarter in range(groups):
        frm = frm_quarter * per_group + place

        @pl.when(quarter != frm_quarter)
        def _():
            remote(bsend_scr.at[0], gb_ref.at[frm], b_send.at[0], b_recv.at[frm], me).wait_recv()

        for by in range(1, per_group):
            f_copy(gb_ref.at[frm], frm, by).start()

    @pl.loop(half, blocks)
    def _(k):
        one_block(k)

    own_x = pltpu.make_async_copy(wt_scr.at[pl.ds(pl.multiple_of(me * slice_width, slice_width), slice_width)],
                                  gx_ref.at[me], own_sem.at[2])
    own_x.start()

    def hand_copy(step):
        target = in_ref if step == relays else rec_scr.at[step]
        return remote(code_scr, target, hand_send.at[step], hand_recv.at[step], right)

    for step in range(relays + 1):
        @pl.when(me < devices - 1)
        def _():
            hand_copy(step).start()
            hand_copy(step).wait_send()

        @pl.when(me > 0)
        def _():
            hand_copy(step).wait_recv()

        if step < relays:
            @pl.loop(0, blocks)
            def _(block):
                factor = through_ref[block][:heads]
                factor = jnp.broadcast_to(factor[:, None, :], (heads, width // heads, state_dim))
                value = decode(rec_scr[step, block, :width], rec_scr[step, block, width:])
                value = factor.reshape(width, state_dim) * value + local_scr[block]
                code_scr[block, :width], code_scr[block, width:] = encode(value)

    @pl.when(me < devices - 1)
    def _():
        for copy in rim_copies():
            copy.wait_send()

    own_d.wait()
    own_x.wait()
    for group in range(groups):
        @pl.when(quarter != group)
        def _():
            b_copy(group).wait_send()

    for frm_quarter in range(groups):
        for by in range(1, per_group):
            frm = frm_quarter * per_group + place
            f_copy(gb_ref.at[frm], frm, by).wait_send()

    @pl.loop(0, devices)
    def _(other):
        @pl.when(other != me)
        def _():
            d_copy(other).wait_send()
            x_copy(other).wait_send()
            remote(factor_ref.at[0], gd_ref.at[other], d_send.at[other], d_recv.at[other], other).wait_recv()
            remote(wt_scr.at[pl.ds(0, slice_width)], gx_ref.at[other], x_send.at[other], x_recv.at[other],
                   other).wait_recv()

        @pl.when(other % per_group != place)
        def _():
            remote(gb_ref.at[other], gb_ref.at[other], f_send.at[0, 1], f_recv.at[other], other).wait_recv()


def swap_kernel(devices, states_ref, out_ref, send_sem, recv_sem, own_sem):
    me = lax.axis_index("ctx")
    barrier = enter("ctx", me, devices)
    own = pltpu.make_async_copy(states_ref.at[me], out_ref.at[me], own_sem)
    own.start()
    pl.semaphore_wait(barrier, devices - 1)

    def copy(to):
        return pltpu.make_async_remote_copy(
            src_ref=states_ref.at[to], dst_ref=out_ref.at[me], send_sem=send_sem.at[to], recv_sem=recv_sem.at[me],
            device_id={"ctx": to}, device_id_type=MESH)

    @pl.loop(0, devices)
    def _(k):
        to = (me + spread(k, devices)) % devices

        @pl.when(to != me)
        def _():
            copy(to).start()

    own.wait()

    @pl.loop(0, devices)
    def _(other):
        @pl.when(other != me)
        def _():
            copy(other).wait_send()
            pltpu.make_async_remote_copy(
                src_ref=states_ref.at[0], dst_ref=out_ref.at[other], send_sem=send_sem.at[other],
                recv_sem=recv_sem.at[other], device_id={"ctx": other}, device_id_type=MESH).wait_recv()


def deliver_kernel(code_ref, out_ref):
    sources, slots, _, state_dim = code_ref.shape
    heads, head_dim = out_ref.shape[1:3]
    slice_heads = heads // sources
    width = slice_heads * head_dim
    for source in range(sources):
        for slot in range(slots):
            value = decode(code_ref[source, slot, :width], code_ref[source, slot, width:])
            out_ref[slot, source * slice_heads:(source + 1) * slice_heads] = value.reshape(
                slice_heads, head_dim, state_dim)


def state_kernel(heads, offsets_ref, dest_ref, first_ref, last_ref, wt_ref, b_ref, grow_ref, out_ref):
    blocks, width, length = wt_ref.shape
    state_dim = out_ref.shape[2]
    head_dim = width // heads
    out_ref[...] = jnp.zeros_like(out_ref)
    row = lax.broadcasted_iota(jnp.int32, (length, state_dim), 0)
    lane = lax.broadcasted_iota(jnp.int32, (heads, length), 1)

    def one_block(block, carry):
        first = block * length
        weighted = wt_ref[block]
        b_val = b_ref[block]
        grow = grow_ref[block][:heads]

        def state_at(end, start):
            part = jnp.where((row >= start) & (row <= end), b_val, jnp.zeros_like(b_val))
            local = jnp.dot(weighted, part, preferred_element_type=jnp.float32)
            factor = jnp.sum(jnp.where((lane == end) & (start < 0), grow, 0.0), axis=1, keepdims=True)
            carried = factor[:, :, None] * carry.reshape(heads, head_dim, state_dim)
            return local + carried.reshape(width, state_dim)

        @pl.loop(first_ref[block], first_ref[block + 1])
        def _(doc):
            at = dest_ref[doc]
            state = state_at(offsets_ref[doc + 1] - 1 - first, offsets_ref[doc] - first)
            out_ref[at, :width], out_ref[at, width:] = encode(state)

        return state_at(jnp.int32(length - 1), last_ref[block] - first)

    lax.fori_loop(0, blocks, one_block, jnp.zeros((width, state_dim), jnp.float32))


def main_kernel(xs_ref, b_ref, c_ref, cum_row_ref, cum_col_ref, cont_ref, dt_row_ref, start_ref, skip_ref, in_ref,
                gate_ref, norm_ref, out_ref, v_scr):
    length = xs_ref.shape[0]
    blocks = in_ref.shape[0]
    width = skip_ref.shape[1] // blocks
    heads = cum_row_ref.shape[0] // blocks
    head_dim = width // heads
    c_val = c_ref[...]
    contract = (((1,), (1,)), ((), ()))
    scores = lax.dot_general(c_val, b_ref[...], contract, preferred_element_type=jnp.float32)
    row = lax.broadcasted_iota(jnp.int32, (length, length), 0)
    col = lax.broadcasted_iota(jnp.int32, (length, length), 1)
    causal = (col <= row) & (col >= start_ref[...])
    part = lax.broadcasted_iota(jnp.int32, (length, width), 1) // head_dim
    square = jnp.zeros((length, 1), jnp.float32)
    for block in range(blocks):
        cols = slice(block * width, (block + 1) * width)
        xs = xs_ref[:, cols]
        weights, split = [], []
        cont = jnp.zeros((length, width), jnp.float32)
        for head in range(heads):
            at = block * heads + head
            gap = cum_col_ref[0, :, at:at + 1] - cum_row_ref[at:at + 1, :]
            decay = jnp.exp(jnp.where(causal, gap, -jnp.inf))
            weights.append((scores * decay * dt_row_ref[at:at + 1, :]).astype(jnp.bfloat16))
            split.append(jnp.where(part == head, xs, jnp.zeros_like(xs)))
            cont = jnp.where(part == head, cont_ref[0, :, at:at + 1], cont)
        intra = jnp.dot(jnp.concatenate(weights, 1), jnp.concatenate(split, 0), preferred_element_type=jnp.float32)
        state = decode(in_ref[block, :width], in_ref[block, width:])
        high = state.astype(jnp.bfloat16)
        low = (state - high.astype(jnp.float32)).astype(jnp.bfloat16)
        inter = lax.dot_general(c_val, high, contract, preferred_element_type=jnp.float32)
        inter = inter + lax.dot_general(c_val, low, contract, preferred_element_type=jnp.float32)
        y_sum = intra + inter * cont + skip_ref[:, cols] * xs.astype(jnp.float32)
        gate = gate_ref[:, cols].astype(jnp.float32)
        value = y_sum * (gate / (1.0 + jnp.exp(-gate)))
        v_scr[:, cols] = value
        square = square + jnp.sum(value * value, axis=1, keepdims=True)
    scale = lax.rsqrt(square / (blocks * width) + 1e-05)
    out_ref[...] = (v_scr[...] * scale * norm_ref[...]).astype(jnp.bfloat16)


def per_device(
    ssm_input,
    gate_input,
    bc_input,
    dt_raw,
    offsets,
    owners,
    conv_weight,
    convolution_bias,
    a_log,
    dt_bias,
    d_skip,
    norm_weight,
):
    length, inner_dim = ssm_input.shape
    heads = a_log.shape[0]
    head_dim = inner_dim // heads
    groups = heads // GROUP_HEADS
    state_dim = bc_input.shape[1] // (2 * groups)
    docs = offsets.shape[0] - 1
    devices = lax.axis_size("ctx")
    relays = devices // 8 - 1
    blocks = heads // BLOCK_HEADS
    width = BLOCK_HEADS * head_dim
    group_state = groups * state_dim
    device_width = inner_dim // devices
    device_heads = heads // devices
    base = lax.axis_index("ctx") * length

    local_tok = jnp.arange(length, dtype=jnp.int32)
    taps = jnp.arange(KERNEL_WIDTH, dtype=jnp.int32) - (KERNEL_WIDTH - 1)
    tokens = base + local_tok
    start_local = jnp.max(jnp.where(offsets[None, :] <= tokens[:, None], offsets[None, :], 0), 1) - base
    end_local = jnp.min(jnp.where(offsets[None, :] > tokens[:, None], offsets[None, :] - base, length), 1) - 1
    end_local = jnp.minimum(end_local, length - 1)
    mask = jnp.where(local_tok[:, None] + taps[None, :] >= start_local[:, None], 1.0, 0.0).astype(jnp.float32)
    start_last = start_local[length - 1]
    last_mask = jnp.broadcast_to(
        jnp.where(local_tok >= start_last, 1.0, 0.0).astype(jnp.float32)[:, None], (length, state_dim))

    exact = functools.partial(jnp.dot, precision=lax.Precision.HIGHEST, preferred_element_type=jnp.float32)
    dt_rows = jax.nn.softplus(dt_raw.T + dt_bias[:, None])
    upto = (local_tok[:, None] <= local_tok[None, :]).astype(jnp.float32)
    cum_rows = exact(-dt_rows * jnp.exp(a_log)[:, None], upto)
    pick = (local_tok[:, None] == end_local[None, :]).astype(jnp.float32)
    cum_end = exact(cum_rows, pick)
    end_weight = jnp.exp(cum_end - cum_rows) * dt_rows
    grow = jnp.exp(cum_rows)
    through = jnp.where(start_last < 0, grow[:, length - 1:], 0.0)
    cum = cum_rows.T
    cont = jnp.where((start_local < 0)[:, None], jnp.exp(cum), 0.0)

    slice_rows = -(-device_heads // 8) * 8
    grow_send = jnp.pad(grow.reshape(devices, device_heads, length),
                        ((0, 0), (0, slice_rows - device_heads), (0, 0)))
    end_blocks = end_weight.reshape(blocks, BLOCK_HEADS, length)
    through_blocks = jnp.broadcast_to(through.reshape(blocks, BLOCK_HEADS, 1), (blocks, BLOCK_HEADS, state_dim))
    taps_bias = jnp.concatenate([conv_weight, convolution_bias[None, :]], 0)
    wx = taps_bias[:, :inner_dim].reshape(KERNEL_WIDTH + 1, blocks, width).transpose(1, 0, 2)
    wbc = taps_bias[:, inner_dim:]

    vmem = pl.BlockSpec(memory_space=pltpu.VMEM)
    anywhere = pl.BlockSpec(memory_space=pl.ANY)
    dma = pltpu.SemaphoreType.DMA
    code_rows = width + SCALE_ROWS
    per_group = devices // groups
    xs, b_conv, c_conv, incoming, got_x, got_b, got_grow = pl.pallas_call(
        functools.partial(front_kernel, devices, groups, relays),
        in_specs=[vmem] * 9,
        out_specs=[vmem] * 4 + [anywhere] * 3,
        out_shape=[
            jax.ShapeDtypeStruct((length, inner_dim), jnp.bfloat16),
            jax.ShapeDtypeStruct((length, group_state), jnp.bfloat16),
            jax.ShapeDtypeStruct((length, group_state), jnp.bfloat16),
            jax.ShapeDtypeStruct((blocks, code_rows, state_dim), jnp.int16),
            jax.ShapeDtypeStruct((devices, device_width, length), jnp.bfloat16),
            jax.ShapeDtypeStruct((devices, length, state_dim), jnp.bfloat16),
            jax.ShapeDtypeStruct((devices, slice_rows, length), jnp.float32),
        ],
        scratch_shapes=[
            pltpu.VMEM((RIM, inner_dim), jnp.bfloat16),
            pltpu.VMEM((RIM, 2 * group_state), jnp.bfloat16),
            pltpu.VMEM((inner_dim, length), jnp.bfloat16),
            pltpu.VMEM((groups, length, state_dim), jnp.bfloat16),
            pltpu.VMEM((blocks, width, state_dim), jnp.float32),
            pltpu.VMEM((blocks, code_rows, state_dim), jnp.int16),
            pltpu.VMEM((max(relays, 1), blocks, code_rows, state_dim), jnp.int16),
            pltpu.VMEM((groups, length, state_dim), jnp.bfloat16),
            dma((2,)), dma((2,)),
            dma((devices,)), dma((devices,)),
            dma((groups,)), dma((devices,)),
            dma((groups, per_group)), dma((devices,)),
            dma((devices,)), dma((devices,)),
            dma((relays + 1,)), dma((relays + 1,)),
            dma((3,)),
        ],
        compiler_params=pltpu.CompilerParams(
            collective_id=0, has_side_effects=True, vmem_limit_bytes=VMEM_LIMIT),
        name="front",
    )(ssm_input, bc_input, mask, wx, wbc, end_blocks, grow_send, last_mask, through_blocks)

    doc_ids = jnp.arange(docs, dtype=jnp.int32)
    earlier = doc_ids[None, :] < doc_ids[:, None]
    owner_rank = jnp.sum(((owners[None, :] == owners[:, None]) & earlier).astype(jnp.int32), 1)
    dest_row = owners * OWNER_SLOTS + owner_rank
    edges = jnp.arange(devices + 1, dtype=jnp.int32) * length
    first_doc = jnp.sum((offsets[None, 1:] <= edges[:, None]).astype(jnp.int32), 1)
    last_start = jnp.max(jnp.where(offsets[None, :] < edges[1:, None], offsets[None, :], 0), 1)
    rows = devices * OWNER_SLOTS
    state_rows = device_width + SCALE_ROWS
    smem = pl.BlockSpec(memory_space=pltpu.SMEM)
    states = pl.pallas_call(
        functools.partial(state_kernel, device_heads),
        in_specs=[smem] * 4 + [vmem] * 3,
        out_specs=vmem,
        out_shape=jax.ShapeDtypeStruct((rows, state_rows, state_dim), jnp.int16),
        compiler_params=pltpu.CompilerParams(vmem_limit_bytes=VMEM_LIMIT),
        name="doc_states",
    )(offsets, dest_row, first_doc, last_start, got_x, got_b, got_grow)

    delivered = pl.pallas_call(
        functools.partial(swap_kernel, devices),
        in_specs=[anywhere],
        out_specs=anywhere,
        out_shape=jax.ShapeDtypeStruct((devices, OWNER_SLOTS * state_rows, state_dim), jnp.int16),
        scratch_shapes=[dma((devices,)), dma((devices,)), dma],
        compiler_params=pltpu.CompilerParams(collective_id=1, has_side_effects=True),
        name="swap",
    )(states.reshape(devices, OWNER_SLOTS * state_rows, state_dim))

    sources = devices // 4
    decode_states = pl.pallas_call(
        deliver_kernel,
        grid=(4,),
        in_specs=[pl.BlockSpec((sources, OWNER_SLOTS, state_rows, state_dim), lambda j: (j, 0, 0, 0))],
        out_specs=pl.BlockSpec((OWNER_SLOTS, heads // 4, head_dim, state_dim), lambda j: (0, j, 0, 0)),
        out_shape=jax.ShapeDtypeStruct((OWNER_SLOTS, heads, head_dim, state_dim), jnp.float32),
        name="deliver",
    )(delivered.reshape(devices, OWNER_SLOTS, state_rows, state_dim))

    group_blocks = GROUP_HEADS // BLOCK_HEADS
    group_width = group_blocks * width
    per_column = lambda rows: pl.BlockSpec((rows, group_width), lambda g: (0, g))
    by_column = lambda a: a.reshape(length, groups, GROUP_HEADS).transpose(1, 0, 2)
    column_spec = pl.BlockSpec((1, length, GROUP_HEADS), lambda g: (g, 0, 0))
    row_spec = pl.BlockSpec((GROUP_HEADS, length), lambda g: (g, 0))
    state_spec = pl.BlockSpec((length, state_dim), lambda g: (0, g))
    gated_out = pl.pallas_call(
        main_kernel,
        grid=(groups,),
        in_specs=[
            per_column(length),
            state_spec,
            state_spec,
            row_spec,
            column_spec,
            column_spec,
            row_spec,
            pl.BlockSpec((length, 1), lambda g: (0, 0)),
            per_column(1),
            pl.BlockSpec((group_blocks, code_rows, state_dim), lambda g: (g, 0, 0)),
            per_column(length),
            per_column(1),
        ],
        out_specs=per_column(length),
        out_shape=jax.ShapeDtypeStruct((length, inner_dim), jnp.bfloat16),
        scratch_shapes=[pltpu.VMEM((length, group_width), jnp.float32)],
        compiler_params=pltpu.CompilerParams(vmem_limit_bytes=VMEM_LIMIT),
        name="scan_gate_norm",
    )(
        xs,
        b_conv,
        c_conv,
        cum_rows,
        by_column(cum),
        by_column(cont),
        dt_rows,
        start_local[:, None],
        jnp.repeat(d_skip, head_dim)[None, :],
        incoming,
        gate_input,
        norm_weight[None, :],
    )
    return (gated_out, decode_states)


def solution(mesh):
    in_specs = (
        P(("groups", "ctx"), None),
        P(("groups", "ctx"), None),
        P(("groups", "ctx"), None),
        P(("groups", "ctx"), None),
        P("groups"),
        P("groups"),
        P(),
        P(),
        P(),
        P(),
        P(),
        P(),
    )
    out_specs = (P(("groups", "ctx"), None), P(("groups", "ctx"), None, None, None))
    return jax.shard_map(
        per_device, mesh=mesh, in_specs=in_specs, out_specs=out_specs, check_vma=False
    )
```

```python
import functools
import math
import jax
import jax.numpy as jnp
from jax import lax
from jax.experimental import pallas as pl
from jax.experimental.pallas import tpu as pltpu
from jax.sharding import PartitionSpec as P

GROUP_HEADS = 16
KERNEL_WIDTH = 4
OWNER_SLOTS = 2
BLOCK_HEADS = 4
RIM = 16
SCALE_ROWS = 16
LEVELS = 8.0
CODE_MAX = 32767.0
HAND_CHUNKS = 4
VMEM_LIMIT = 56 * 1024 * 1024
MESH = pl.DeviceIdType.MESH


def encode(value):
    rows, lanes = value.shape
    parts = value.reshape(rows // SCALE_ROWS, SCALE_ROWS, lanes)
    top = jnp.max(jnp.abs(parts), axis=1)
    level = jnp.ceil(jnp.log(jnp.maximum(top, 1e-30)) * (LEVELS / math.log(2.0)))
    unit = jnp.exp2(level * (-1.0 / LEVELS)) * CODE_MAX
    coded = jnp.clip(jnp.round(parts * unit[:, None, :]), -CODE_MAX, CODE_MAX).reshape(rows, lanes)
    if level.shape[0] < SCALE_ROWS:
        level = jnp.concatenate([level, jnp.zeros((SCALE_ROWS - level.shape[0], lanes), jnp.float32)], 0)
    return coded.astype(jnp.int32).astype(jnp.int16), level.astype(jnp.int32).astype(jnp.int16)


def decode(coded, level):
    rows, lanes = coded.shape
    unit = jnp.exp2(level.astype(jnp.int32).astype(jnp.float32) * (1.0 / LEVELS)) * (1.0 / CODE_MAX)
    unit = unit[:rows // SCALE_ROWS]
    parts = coded.astype(jnp.int32).astype(jnp.float32).reshape(rows // SCALE_ROWS, SCALE_ROWS, lanes)
    return (parts * unit[:, None, :]).reshape(rows, lanes)


def conv_silu(x, rim, mask_ref, weight, bias):
    x = x.astype(jnp.float32)
    padded = jnp.concatenate([rim.astype(jnp.float32), x], 0)
    total = bias
    for tap in range(KERNEL_WIDTH - 1):
        mask = jnp.concatenate([mask_ref[tap]] * (x.shape[1] // mask_ref.shape[2]), 1)
        total = total + weight[tap:tap + 1] * (mask * pltpu.roll(padded, KERNEL_WIDTH - 1 - tap, 0)[RIM:])
    total = total + weight[KERNEL_WIDTH - 1:KERNEL_WIDTH] * x
    return (total / (1.0 + jnp.exp(-total))).astype(jnp.bfloat16)


def spread(k, count):
    half = (k + 1) // 2
    return count // 2 + half * (1 - 2 * (k % 2))


def enter(axis, me, devices):
    barrier = pltpu.get_barrier_semaphore()

    @pl.loop(1, devices)
    def _(by):
        pl.semaphore_signal(barrier, inc=1, device_id={axis: (me + by) % devices}, device_id_type=MESH)

    return barrier


def exact_dot(a, b):
    return jnp.dot(a, b, precision=lax.Precision.HIGHEST, preferred_element_type=jnp.float32)


def front_kernel(devices, groups, relays, offsets_ref, x_ref, bc_ref, dt_ref, taps_ref, bias_ref, a_ref, dt_bias_ref,
                 xs_ref, bconv_ref, c_ref, in_ref, rows_ref, cols_ref, start_ref, gx_ref, gb_ref, gd_ref,
                 rimx_scr, rimbc_scr, wt_scr, blast_scr, local_scr, code_scr, rec_scr, bsend_scr, mask_scr, end_scr,
                 grow_scr, through_scr,
                 rim_send, rim_recv, x_send, x_recv, b_send, b_recv, f_send, f_recv, d_send, d_recv, hand_send,
                 hand_recv, own_sem):
    me = lax.axis_index("ctx")
    length, inner = x_ref.shape
    blocks = local_scr.shape[0]
    width = inner // blocks
    state_dim = blast_scr.shape[2]
    all_heads = dt_ref.shape[1]
    head_dim = inner // all_heads
    per_block = devices // blocks
    slice_width = width // per_block
    slice_heads = all_heads // devices
    per_group = devices // groups
    blocks_per_group = blocks // groups
    group_heads = all_heads // groups
    quarter = me // per_group
    place = me % per_group
    steps = relays + 2
    chunks = hand_send.shape[1]
    chunk_blocks = blocks // chunks

    def remote(src, dst, send, recv, to):
        return pltpu.make_async_remote_copy(src_ref=src, dst_ref=dst, send_sem=send, recv_sem=recv,
                                            device_id={"ctx": to}, device_id_type=MESH)

    barrier = enter("ctx", me, devices)

    @pl.when(me == 0)
    def _():
        rimx_scr[...] = jnp.zeros_like(rimx_scr)
        rimbc_scr[...] = jnp.zeros_like(rimbc_scr)
        in_ref[...] = jnp.zeros_like(in_ref)
        rec_scr[...] = jnp.zeros_like(rec_scr)

    base = me * length
    docs = offsets_ref.shape[0] - 1
    token = lax.broadcasted_iota(jnp.int32, (length, state_dim), 0)
    along = lax.broadcasted_iota(jnp.int32, (8, length), 1)

    def bounds(k, carry):
        start, end = carry
        offset = offsets_ref[k] - base
        start = jnp.where(offset <= token, jnp.maximum(start, offset), start)
        end = jnp.where(offset > along, jnp.minimum(end, offset), end)
        return start, end

    start, end = lax.fori_loop(0, docs + 1, bounds, (jnp.full((length, state_dim), -base, jnp.int32),
                                                     jnp.full((8, length), length, jnp.int32)))
    end = end - 1
    start_ref[...] = start
    for tap in range(KERNEL_WIDTH - 1):
        mask_scr[tap] = jnp.where(token + (tap - KERNEL_WIDTH + 1) >= start, 1.0, 0.0).astype(jnp.float32)
    last_start = jnp.max(start, axis=0, keepdims=True)
    last = token >= last_start

    pre = dt_ref[...] + dt_bias_ref[...]
    dt = jnp.maximum(pre, 0.0) + jnp.log1p(jnp.exp(-jnp.abs(pre)))
    turned = jnp.concatenate([dt, -dt * jnp.exp(a_ref[...])], 1).T
    dt_rows = turned[:all_heads]
    one = lax.broadcasted_iota(jnp.int32, (length, length), 0)
    two = lax.broadcasted_iota(jnp.int32, (length, length), 1)
    cum_rows = exact_dot(turned[all_heads:], jnp.where(one <= two, 1.0, 0.0).astype(jnp.float32))
    cum_end = exact_dot(cum_rows, jnp.where(one == end[:1], 1.0, 0.0).astype(jnp.float32))
    grow = jnp.exp(cum_rows)
    rows_ref[:all_heads] = cum_rows
    rows_ref[all_heads:] = dt_rows
    weight = jnp.exp(cum_end - cum_rows) * dt_rows
    for block in range(blocks):
        end_scr[block] = weight[block * BLOCK_HEADS:(block + 1) * BLOCK_HEADS]
    for device in range(devices):
        grow_scr[device, :slice_heads] = grow[device * slice_heads:(device + 1) * slice_heads]
    grow_last = jnp.sum(jnp.where(lax.broadcasted_iota(jnp.int32, grow.shape, 1) == length - 1, grow, 0.0), axis=1,
                        keepdims=True)
    through = jnp.where(last_start < 0, jnp.broadcast_to(grow_last, (all_heads, state_dim)), 0.0)
    for block in range(blocks):
        through_scr[block] = through[block * BLOCK_HEADS:(block + 1) * BLOCK_HEADS]
    upright = jnp.concatenate([cum_rows, grow], 0).T
    begun = start[:, :group_heads] < 0
    for group in range(groups):
        at = group * group_heads
        cols_ref[group, :, :group_heads] = upright[:, at:at + group_heads]
        cols_ref[group, :, group_heads:] = jnp.where(begun, upright[:, all_heads + at:all_heads + at + group_heads], 0.0)

    pl.semaphore_wait(barrier, devices - 1)

    right = (me + 1) % devices

    def rim_copies():
        return (remote(x_ref.at[pl.ds(length - RIM, RIM)], rimx_scr, rim_send.at[0], rim_recv.at[0], right),
                remote(bc_ref.at[pl.ds(length - RIM, RIM)], rimbc_scr, rim_send.at[1], rim_recv.at[1], right))

    @pl.when(me < devices - 1)
    def _():
        for copy in rim_copies():
            copy.start()

    def d_copy(to):
        return remote(grow_scr.at[to], gd_ref.at[me], d_send.at[to], d_recv.at[me], to)

    @pl.loop(0, devices)
    def _(k):
        to = (me + spread(k, devices)) % devices

        @pl.when(to != me)
        def _():
            d_copy(to).start()

    own_d = pltpu.make_async_copy(grow_scr.at[me], gd_ref.at[me], own_sem.at[0])
    own_d.start()

    @pl.when(me > 0)
    def _():
        for copy in rim_copies():
            copy.wait_recv()

    for part in range(2 * groups):
        cols = slice(part * state_dim, (part + 1) * state_dim)
        after = slice(inner + part * state_dim, inner + (part + 1) * state_dim)
        value = conv_silu(bc_ref[:, cols], rimbc_scr[:, cols], mask_scr, taps_ref[:, after], bias_ref[:, after])
        if part < groups:
            bconv_ref[:, cols] = value
            bsend_scr[part] = value
            blast_scr[part] = jnp.where(last, value, jnp.zeros_like(value))
        else:
            c_ref[:, (part - groups) * state_dim:(part - groups + 1) * state_dim] = value

    def b_copy(group):
        return remote(bsend_scr.at[group], gb_ref.at[me], b_send.at[group], b_recv.at[me],
                      group * per_group + place)

    own_b = pltpu.make_async_copy(bsend_scr.at[quarter], gb_ref.at[me], own_sem.at[1])
    own_b.start()
    for group in range(groups):
        @pl.when(quarter != group)
        def _():
            b_copy(group).start()

    def x_copy(to):
        return remote(wt_scr.at[pl.ds(pl.multiple_of(to * slice_width, slice_width), slice_width)], gx_ref.at[me],
                      x_send.at[to], x_recv.at[me], to)

    def one_block(k):
        block = (me // per_block + spread(k, blocks)) % blocks
        cols = pl.ds(pl.multiple_of(block * width, width), width)
        xs = conv_silu(x_ref[:, cols], rimx_scr[:, cols], mask_scr, taps_ref[:, cols], bias_ref[:, cols])
        xs_ref[:, cols] = xs
        x_t = xs.astype(jnp.float32).T.reshape(BLOCK_HEADS, head_dim, length)
        weighted = (x_t * end_scr[block][:, None, :]).astype(jnp.bfloat16).reshape(width, length)
        wt_scr[cols, :] = weighted

        @pl.loop(0, per_block)
        def _(part):
            to = block * per_block + part

            @pl.when(to != me)
            def _():
                x_copy(to).start()

        local = jnp.dot(weighted, blast_scr[block // blocks_per_group], preferred_element_type=jnp.float32)
        local_scr[block] = local
        code_scr[block, :width], code_scr[block, width:] = encode(local)

    half = blocks // 2

    @pl.loop(0, half)
    def _(k):
        one_block(k)

    def f_copy(src, frm, by):
        to = quarter * per_group + (place + by) % per_group
        return remote(src, gb_ref.at[frm], f_send.at[frm // per_group, by], f_recv.at[frm], to)

    own_b.wait()
    for frm_quarter in range(groups):
        frm = frm_quarter * per_group + place

        @pl.when(quarter != frm_quarter)
        def _():
            remote(bsend_scr.at[0], gb_ref.at[frm], b_send.at[0], b_recv.at[frm], me).wait_recv()

        for by in range(1, per_group):
            f_copy(gb_ref.at[frm], frm, by).start()

    @pl.loop(half, blocks)
    def _(k):
        one_block(k)

    own_x = pltpu.make_async_copy(wt_scr.at[pl.ds(pl.multiple_of(me * slice_width, slice_width), slice_width)],
                                  gx_ref.at[me], own_sem.at[2])
    own_x.start()

    def landing(step):
        return in_ref if step >= steps - 2 else rec_scr.at[step]

    def hand_copy(step, chunk):
        part = pl.ds(chunk * chunk_blocks, chunk_blocks)
        return remote(code_scr.at[part], landing(step).at[part], hand_send.at[step, chunk],
                      hand_recv.at[step, chunk], right)

    for step in range(steps):
        @pl.when(me % 2 == step % 2)
        def _():
            @pl.loop(0, chunks)
            def _(chunk):
                if step >= 2:
                    @pl.when(me < devices - 1)
                    def _():
                        hand_copy(step - 2, chunk).wait_send()

                if step >= 1:
                    @pl.when(me > 0)
                    def _():
                        hand_copy(step - 1, chunk).wait_recv()

                    got = landing(step - 1)

                    @pl.loop(chunk * chunk_blocks, (chunk + 1) * chunk_blocks)
                    def _(block):
                        factor = jnp.broadcast_to(through_scr[block][:, None, :], (BLOCK_HEADS, head_dim, state_dim))
                        value = decode(got[block, :width], got[block, width:])
                        value = factor.reshape(width, state_dim) * value + local_scr[block]
                        code_scr[block, :width], code_scr[block, width:] = encode(value)

                @pl.when(me < devices - 1)
                def _():
                    hand_copy(step, chunk).start()

    @pl.when((me % 2 != (steps - 1) % 2) & (me > 0))
    def _():
        @pl.loop(0, chunks)
        def _(chunk):
            hand_copy(steps - 1, chunk).wait_recv()

    @pl.when(me < devices - 1)
    def _():
        for copy in rim_copies():
            copy.wait_send()

        for step in range(steps - 2, steps):
            @pl.when(me % 2 == step % 2)
            def _():
                @pl.loop(0, chunks)
                def _(chunk):
                    hand_copy(step, chunk).wait_send()

    own_d.wait()
    own_x.wait()
    for group in range(groups):
        @pl.when(quarter != group)
        def _():
            b_copy(group).wait_send()

    for frm_quarter in range(groups):
        for by in range(1, per_group):
            frm = frm_quarter * per_group + place
            f_copy(gb_ref.at[frm], frm, by).wait_send()

    @pl.loop(0, devices)
    def _(other):
        @pl.when(other != me)
        def _():
            d_copy(other).wait_send()
            x_copy(other).wait_send()
            remote(grow_scr.at[0], gd_ref.at[other], d_send.at[other], d_recv.at[other], other).wait_recv()
            remote(wt_scr.at[pl.ds(0, slice_width)], gx_ref.at[other], x_send.at[other], x_recv.at[other],
                   other).wait_recv()

        @pl.when(other % per_group != place)
        def _():
            remote(gb_ref.at[other], gb_ref.at[other], f_send.at[0, 1], f_recv.at[other], other).wait_recv()


def swap_kernel(devices, groups, skip_ref, states_ref, xs_hbm, gate_hbm, in_hbm, b_ref, c_ref, rows_ref, cols_ref,
                start_ref, norm_ref, out_ref, gated_ref, xs_scr, gate_scr, in_scr, v_scr, send_sem, recv_sem,
                own_sem):
    me = lax.axis_index("ctx")
    barrier = enter("ctx", me, devices)
    own = pltpu.make_async_copy(states_ref.at[me], out_ref.at[me], own_sem.at[0])
    own.start()
    loads = [pltpu.make_async_copy(src, dst, own_sem.at[1 + k])
             for k, (src, dst) in enumerate(((xs_hbm, xs_scr), (gate_hbm, gate_scr), (in_hbm, in_scr)))]
    pl.semaphore_wait(barrier, devices - 1)

    def copy(to):
        return pltpu.make_async_remote_copy(
            src_ref=states_ref.at[to], dst_ref=out_ref.at[me], send_sem=send_sem.at[to], recv_sem=recv_sem.at[me],
            device_id={"ctx": to}, device_id_type=MESH)

    @pl.loop(0, devices)
    def _(k):
        to = (me + spread(k, devices)) % devices

        @pl.when(to != me)
        def _():
            copy(to).start()

    for load in loads:
        load.start()
    for load in loads:
        load.wait()

    @pl.loop(0, groups)
    def _(group):
        scan_group(groups, group, skip_ref, xs_scr, gate_scr, in_scr, b_ref, c_ref, rows_ref, cols_ref, start_ref,
                   norm_ref, gated_ref, v_scr)

    own.wait()

    @pl.loop(0, devices)
    def _(other):
        @pl.when(other != me)
        def _():
            copy(other).wait_send()
            pltpu.make_async_remote_copy(
                src_ref=states_ref.at[0], dst_ref=out_ref.at[other], send_sem=send_sem.at[other],
                recv_sem=recv_sem.at[other], device_id={"ctx": other}, device_id_type=MESH).wait_recv()


def scan_group(groups, group, skip_ref, xs_ref, gate_ref, in_ref, b_ref, c_ref, rows_ref, cols_ref, start_ref,
               norm_ref, out_ref, v_scr):
    length, inner = xs_ref.shape
    state_dim = b_ref.shape[1] // groups
    all_heads = rows_ref.shape[0] // 2
    group_heads = all_heads // groups
    group_width = inner // groups
    blocks = group_heads // BLOCK_HEADS
    width = group_width // blocks
    head_dim = width // BLOCK_HEADS
    state_cols = pl.ds(pl.multiple_of(group * state_dim, state_dim), state_dim)
    c_val = c_ref[:, state_cols]
    contract = (((1,), (1,)), ((), ()))
    scores = lax.dot_general(c_val, b_ref[:, state_cols], contract, preferred_element_type=jnp.float32)
    row = lax.broadcasted_iota(jnp.int32, (length, length), 0)
    col = lax.broadcasted_iota(jnp.int32, (length, length), 1)
    causal = (col <= row) & (col >= start_ref[:, :1])
    part = lax.broadcasted_iota(jnp.int32, (length, width), 1) // head_dim
    part_row = lax.broadcasted_iota(jnp.int32, (1, width), 1) // head_dim
    cum_rows = rows_ref[pl.ds(pl.multiple_of(group * group_heads, group_heads), group_heads), :]
    dt_rows = rows_ref[pl.ds(pl.multiple_of(all_heads + group * group_heads, group_heads), group_heads), :]
    columns = cols_ref[group]
    square = jnp.zeros((length, 1), jnp.float32)
    for block in range(blocks):
        here = pl.ds(pl.multiple_of(group * group_width + block * width, width), width)
        xs = xs_ref[:, here]
        weights, split = [], []
        cont = jnp.zeros((length, width), jnp.float32)
        skip = jnp.zeros((1, width), jnp.float32)
        for head in range(BLOCK_HEADS):
            at = block * BLOCK_HEADS + head
            gap = columns[:, at:at + 1] - cum_rows[at:at + 1]
            decay = jnp.exp(jnp.where(causal, gap, -jnp.inf))
            weights.append((scores * decay * dt_rows[at:at + 1]).astype(jnp.bfloat16))
            split.append(jnp.where(part == head, xs, jnp.zeros_like(xs)))
            cont = jnp.where(part == head, columns[:, group_heads + at:group_heads + at + 1], cont)
            skip = jnp.where(part_row == head, skip_ref[group * group_heads + at], skip)
        intra = jnp.dot(jnp.concatenate(weights, 1), jnp.concatenate(split, 0), preferred_element_type=jnp.float32)
        state = decode(in_ref[group * blocks + block, :width], in_ref[group * blocks + block, width:])
        high = state.astype(jnp.bfloat16)
        low = (state - high.astype(jnp.float32)).astype(jnp.bfloat16)
        inter = lax.dot_general(c_val, high, contract, preferred_element_type=jnp.float32)
        inter = inter + lax.dot_general(c_val, low, contract, preferred_element_type=jnp.float32)
        y_sum = intra + inter * cont + skip * xs.astype(jnp.float32)
        gate = gate_ref[:, here].astype(jnp.float32)
        value = y_sum * (gate / (1.0 + jnp.exp(-gate)))
        v_scr[:, block * width:(block + 1) * width] = value
        square = square + jnp.sum(value * value, axis=1, keepdims=True)
    scale = lax.rsqrt(square / group_width + 1e-05)
    whole = pl.ds(pl.multiple_of(group * group_width, group_width), group_width)
    out_ref[:, whole] = (v_scr[...] * scale * norm_ref[:, whole]).astype(jnp.bfloat16)


def deliver_kernel(code_ref, out_ref):
    sources, slots, _, state_dim = code_ref.shape
    heads, head_dim = out_ref.shape[1:3]
    slice_heads = heads // sources
    width = slice_heads * head_dim
    for source in range(sources):
        for slot in range(slots):
            value = decode(code_ref[source, slot, :width], code_ref[source, slot, width:])
            out_ref[slot, source * slice_heads:(source + 1) * slice_heads] = value.reshape(
                slice_heads, head_dim, state_dim)


def state_kernel(heads, offsets_ref, owners_ref, wt_ref, b_ref, grow_ref, out_ref, held_scr):
    blocks, width, length = wt_ref.shape
    state_dim = out_ref.shape[2]
    head_dim = width // heads
    docs = owners_ref.shape[0]
    out_ref[...] = jnp.zeros_like(out_ref)
    row = lax.broadcasted_iota(jnp.int32, (length, state_dim), 0)
    lane = lax.broadcasted_iota(jnp.int32, (heads, length), 1)

    @pl.loop(0, blocks)
    def _(device):
        held_scr[device] = 0

    def one_block(block, carried):
        doc, carry = carried
        first = block * length
        weighted = wt_ref[block]
        b_val = b_ref[block]
        grow = grow_ref[block][:heads]

        def state_at(end, start):
            part = jnp.where((row >= start) & (row <= end), b_val, jnp.zeros_like(b_val))
            local = jnp.dot(weighted, part, preferred_element_type=jnp.float32)
            factor = jnp.sum(jnp.where((lane == end) & (start < 0), grow, 0.0), axis=1, keepdims=True)
            kept = factor[:, :, None] * carry.reshape(heads, head_dim, state_dim)
            return local + kept.reshape(width, state_dim)

        def ends_here(at):
            return (at < docs) & (offsets_ref[jnp.minimum(at + 1, docs)] <= first + length)

        def finish(at):
            owner = owners_ref[at]
            target = owner * OWNER_SLOTS + held_scr[owner]
            held_scr[owner] = held_scr[owner] + 1
            state = state_at(offsets_ref[at + 1] - 1 - first, offsets_ref[at] - first)
            out_ref[target, :width], out_ref[target, width:] = encode(state)
            return at + 1

        doc = lax.while_loop(ends_here, finish, doc)
        return doc, state_at(jnp.int32(length - 1), offsets_ref[doc] - first)

    lax.fori_loop(0, blocks, one_block, (jnp.int32(0), jnp.zeros((width, state_dim), jnp.float32)))


def per_device(
    ssm_input,
    gate_input,
    bc_input,
    dt_raw,
    offsets,
    owners,
    conv_weight,
    convolution_bias,
    a_log,
    dt_bias,
    d_skip,
    norm_weight,
):
    length, inner_dim = ssm_input.shape
    heads = a_log.shape[0]
    head_dim = inner_dim // heads
    groups = heads // GROUP_HEADS
    state_dim = bc_input.shape[1] // (2 * groups)
    devices = lax.axis_size("ctx")
    relays = devices // 8 - 1
    blocks = heads // BLOCK_HEADS
    width = BLOCK_HEADS * head_dim
    group_state = groups * state_dim
    group_width = inner_dim // groups
    device_width = inner_dim // devices
    device_heads = heads // devices
    slice_rows = -(-device_heads // 8) * 8

    vmem = pl.BlockSpec(memory_space=pltpu.VMEM)
    smem = pl.BlockSpec(memory_space=pltpu.SMEM)
    anywhere = pl.BlockSpec(memory_space=pl.ANY)
    dma = pltpu.SemaphoreType.DMA
    code_rows = width + SCALE_ROWS
    per_group = devices // groups
    steps = relays + 2
    code = lambda *lead: pltpu.VMEM(lead + (code_rows, state_dim), jnp.int16)
    xs, b_conv, c_conv, incoming, rows, cols, start, got_x, got_b, got_grow = pl.pallas_call(
        functools.partial(front_kernel, devices, groups, relays),
        in_specs=[smem] + [vmem] * 7,
        out_specs=[vmem] * 7 + [anywhere] * 3,
        out_shape=[
            jax.ShapeDtypeStruct((length, inner_dim), jnp.bfloat16),
            jax.ShapeDtypeStruct((length, group_state), jnp.bfloat16),
            jax.ShapeDtypeStruct((length, group_state), jnp.bfloat16),
            jax.ShapeDtypeStruct((blocks, code_rows, state_dim), jnp.int16),
            jax.ShapeDtypeStruct((2 * heads, length), jnp.float32),
            jax.ShapeDtypeStruct((groups, length, 2 * GROUP_HEADS), jnp.float32),
            jax.ShapeDtypeStruct((length, state_dim), jnp.int32),
            jax.ShapeDtypeStruct((devices, device_width, length), jnp.bfloat16),
            jax.ShapeDtypeStruct((devices, length, state_dim), jnp.bfloat16),
            jax.ShapeDtypeStruct((devices, slice_rows, length), jnp.float32),
        ],
        scratch_shapes=[
            pltpu.VMEM((RIM, inner_dim), jnp.bfloat16),
            pltpu.VMEM((RIM, 2 * group_state), jnp.bfloat16),
            pltpu.VMEM((inner_dim, length), jnp.bfloat16),
            pltpu.VMEM((groups, length, state_dim), jnp.bfloat16),
            pltpu.VMEM((blocks, width, state_dim), jnp.float32),
            code(blocks),
            code(max(relays, 1), blocks),
            pltpu.VMEM((groups, length, state_dim), jnp.bfloat16),
            pltpu.VMEM((KERNEL_WIDTH - 1, length, state_dim), jnp.float32),
            pltpu.VMEM((blocks, BLOCK_HEADS, length), jnp.float32),
            pltpu.VMEM((devices, slice_rows, length), jnp.float32),
            pltpu.VMEM((blocks, BLOCK_HEADS, state_dim), jnp.float32),
            dma((2,)), dma((2,)),
            dma((devices,)), dma((devices,)),
            dma((groups,)), dma((devices,)),
            dma((groups, per_group)), dma((devices,)),
            dma((devices,)), dma((devices,)),
            dma((steps, HAND_CHUNKS)), dma((steps, HAND_CHUNKS)),
            dma((3,)),
        ],
        compiler_params=pltpu.CompilerParams(
            collective_id=0, has_side_effects=True, vmem_limit_bytes=VMEM_LIMIT),
        name="front",
    )(offsets, ssm_input, bc_input, dt_raw, conv_weight, convolution_bias[None, :], a_log[None, :], dt_bias[None, :])

    rows_owned = devices * OWNER_SLOTS
    state_rows = device_width + SCALE_ROWS
    states = pl.pallas_call(
        functools.partial(state_kernel, device_heads),
        in_specs=[smem] * 2 + [vmem] * 3,
        out_specs=vmem,
        out_shape=jax.ShapeDtypeStruct((rows_owned, state_rows, state_dim), jnp.int16),
        scratch_shapes=[pltpu.SMEM((devices,), jnp.int32)],
        compiler_params=pltpu.CompilerParams(vmem_limit_bytes=VMEM_LIMIT),
        name="doc_states",
    )(offsets, owners, got_x, got_b, got_grow)

    delivered, gated_out = pl.pallas_call(
        functools.partial(swap_kernel, devices, groups),
        in_specs=[smem] + [anywhere] * 4 + [vmem] * 6,
        out_specs=[anywhere, vmem],
        out_shape=[
            jax.ShapeDtypeStruct((devices, OWNER_SLOTS * state_rows, state_dim), jnp.int16),
            jax.ShapeDtypeStruct((length, inner_dim), jnp.bfloat16),
        ],
        scratch_shapes=[
            pltpu.VMEM((length, inner_dim), jnp.bfloat16),
            pltpu.VMEM((length, inner_dim), jnp.bfloat16),
            code(blocks),
            pltpu.VMEM((length, group_width), jnp.float32),
            dma((devices,)), dma((devices,)), dma((4,)),
        ],
        compiler_params=pltpu.CompilerParams(
            collective_id=1, has_side_effects=True, vmem_limit_bytes=VMEM_LIMIT),
        name="swap_scan",
    )(d_skip, states.reshape(devices, OWNER_SLOTS * state_rows, state_dim), xs, gate_input, incoming, b_conv, c_conv,
      rows, cols, start, norm_weight[None, :])

    sources = devices // 4
    decode_states = pl.pallas_call(
        deliver_kernel,
        grid=(4,),
        in_specs=[pl.BlockSpec((sources, OWNER_SLOTS, state_rows, state_dim), lambda j: (j, 0, 0, 0))],
        out_specs=pl.BlockSpec((OWNER_SLOTS, heads // 4, head_dim, state_dim), lambda j: (0, j, 0, 0)),
        out_shape=jax.ShapeDtypeStruct((OWNER_SLOTS, heads, head_dim, state_dim), jnp.float32),
        name="deliver",
    )(delivered.reshape(devices, OWNER_SLOTS, state_rows, state_dim))
    return (gated_out, decode_states)


def solution(mesh):
    in_specs = (
        P(("groups", "ctx"), None),
        P(("groups", "ctx"), None),
        P(("groups", "ctx"), None),
        P(("groups", "ctx"), None),
        P("groups"),
        P("groups"),
        P(),
        P(),
        P(),
        P(),
        P(),
        P(),
    )
    out_specs = (P(("groups", "ctx"), None), P(("groups", "ctx"), None, None, None))
    return jax.shard_map(
        per_device, mesh=mesh, in_specs=in_specs, out_specs=out_specs, check_vma=False
    )
```

```python
import functools
import math
import jax
import jax.numpy as jnp
from jax import lax
from jax.experimental import pallas as pl
from jax.experimental.pallas import tpu as pltpu
from jax.sharding import PartitionSpec as P

GROUP_HEADS = 16
KERNEL_WIDTH = 4
OWNER_SLOTS = 2
BLOCK_HEADS = 4
RIM = 16
SCALE_ROWS = 16
LEVELS = 8.0
CODE_MAX = 32767.0
END_SLOTS = 4
CHUNKS = 2
VMEM_LIMIT = 56 * 1024 * 1024
MESH = pl.DeviceIdType.MESH


def encode(value):
    rows, lanes = value.shape
    parts = value.reshape(rows // SCALE_ROWS, SCALE_ROWS, lanes)
    top = jnp.max(jnp.abs(parts), axis=1)
    level = jnp.ceil(jnp.log(jnp.maximum(top, 1e-30)) * (LEVELS / math.log(2.0)))
    unit = jnp.exp2(level * (-1.0 / LEVELS)) * CODE_MAX
    coded = jnp.clip(jnp.round(parts * unit[:, None, :]), -CODE_MAX, CODE_MAX).reshape(rows, lanes)
    if level.shape[0] < SCALE_ROWS:
        level = jnp.concatenate([level, jnp.zeros((SCALE_ROWS - level.shape[0], lanes), jnp.float32)], 0)
    return coded.astype(jnp.int32).astype(jnp.int16), level.astype(jnp.int32).astype(jnp.int16)


def decode(coded, level):
    rows, lanes = coded.shape
    unit = jnp.exp2(level.astype(jnp.int32).astype(jnp.float32) * (1.0 / LEVELS)) * (1.0 / CODE_MAX)
    unit = unit[:rows // SCALE_ROWS]
    parts = coded.astype(jnp.int32).astype(jnp.float32).reshape(rows // SCALE_ROWS, SCALE_ROWS, lanes)
    return (parts * unit[:, None, :]).reshape(rows, lanes)


def conv_silu(x, rim, mask_ref, weight, bias):
    x = x.astype(jnp.float32)
    padded = jnp.concatenate([rim.astype(jnp.float32), x], 0)
    total = bias
    for tap in range(KERNEL_WIDTH - 1):
        mask = jnp.concatenate([mask_ref[tap]] * (x.shape[1] // mask_ref.shape[2]), 1)
        total = total + weight[tap:tap + 1] * (mask * pltpu.roll(padded, KERNEL_WIDTH - 1 - tap, 0)[RIM:])
    total = total + weight[KERNEL_WIDTH - 1:KERNEL_WIDTH] * x
    return (total / (1.0 + jnp.exp(-total))).astype(jnp.bfloat16)


def spread(k, count):
    half = (k + 1) // 2
    return count // 2 + half * (1 - 2 * (k % 2))


def enter(axis, me, devices):
    barrier = pltpu.get_barrier_semaphore()

    @pl.loop(1, devices)
    def _(by):
        pl.semaphore_signal(barrier, inc=1, device_id={axis: (me + by) % devices}, device_id_type=MESH)

    return barrier


def exact_dot(a, b):
    return jnp.dot(a, b, precision=lax.Precision.HIGHEST, preferred_element_type=jnp.float32)


def whole_kernel(devices, groups, relays, offsets_ref, owners_ref, skip_ref, x_ref, bc_ref, dt_ref, taps_ref, bias_ref,
                 a_ref, dt_bias_ref, norm_ref, gate_hbm, out_ref, gated_hbm,
                 rimx_scr, rimbc_scr, xs_scr, b_scr, c_scr, wt_scr, blast_scr, local_scr, code_scr, rec_scr, in_ref,
                 bsend_scr, mask_scr, end_scr, grow_scr, through_scr, rows_ref, cols_ref, start_ref, gx_scr, gb_scr,
                 gd_scr, slot_scr, table_scr, mid_scr, gate_scr, gated_scr, v_scr, first_scr, dest_scr, source_scr,
                 pick_scr,
                 rim_send, rim_recv, x_send, x_recv, b_send, b_recv, f_send, f_recv, d_send, d_recv, hand_send,
                 hand_recv, mid_send, mid_recv, out_send, out_recv, own_sem, gate_sem, gated_sem):
    me = lax.axis_index("ctx")
    length, inner = x_ref.shape
    blocks = end_scr.shape[0]
    width = inner // blocks
    state_dim = blast_scr.shape[2]
    all_heads = dt_ref.shape[1]
    head_dim = inner // all_heads
    per_block = devices // blocks
    slice_width = width // per_block
    slice_heads = all_heads // devices
    chunk = slice_width // CHUNKS
    chunk_heads = max(chunk // head_dim, 1)
    per_group = devices // groups
    blocks_per_group = blocks // groups
    group_heads = all_heads // groups
    quarter = me // per_group
    place = me % per_group
    steps = relays + 2
    middle = devices // 2

    def remote(src, dst, send, recv, to):
        return pltpu.make_async_remote_copy(src_ref=src, dst_ref=dst, send_sem=send, recv_sem=recv,
                                            device_id={"ctx": to}, device_id_type=MESH)

    barrier = enter("ctx", me, devices)

    @pl.when(me == 0)
    def _():
        rimx_scr[...] = jnp.zeros_like(rimx_scr)
        rimbc_scr[...] = jnp.zeros_like(rimbc_scr)
        in_ref[...] = jnp.zeros_like(in_ref)
        rec_scr[...] = jnp.zeros_like(rec_scr)

    base = me * length
    docs = offsets_ref.shape[0] - 1
    token = lax.broadcasted_iota(jnp.int32, (length, state_dim), 0)
    along = lax.broadcasted_iota(jnp.int32, (8, length), 1)

    def bounds(k, carry):
        start, end = carry
        offset = offsets_ref[k] - base
        start = jnp.where(offset <= token, jnp.maximum(start, offset), start)
        end = jnp.where(offset > along, jnp.minimum(end, offset), end)
        return start, end

    start, end = lax.fori_loop(0, docs + 1, bounds, (jnp.full((length, state_dim), -base, jnp.int32),
                                                     jnp.full((8, length), length, jnp.int32)))
    end = end - 1
    start_ref[...] = start
    for tap in range(KERNEL_WIDTH - 1):
        mask_scr[tap] = jnp.where(token + (tap - KERNEL_WIDTH + 1) >= start, 1.0, 0.0).astype(jnp.float32)
    last_start = jnp.max(start, axis=0, keepdims=True)
    last = token >= last_start

    pre = dt_ref[...] + dt_bias_ref[...]
    dt = jnp.maximum(pre, 0.0) + jnp.log1p(jnp.exp(-jnp.abs(pre)))
    turned = jnp.concatenate([dt, -dt * jnp.exp(a_ref[...])], 1).T
    dt_rows = turned[:all_heads]
    one = lax.broadcasted_iota(jnp.int32, (length, length), 0)
    two = lax.broadcasted_iota(jnp.int32, (length, length), 1)
    cum_rows = exact_dot(turned[all_heads:], jnp.where(one <= two, 1.0, 0.0).astype(jnp.float32))
    cum_end = exact_dot(cum_rows, jnp.where(one == end[:1], 1.0, 0.0).astype(jnp.float32))
    grow = jnp.exp(cum_rows)
    rows_ref[:all_heads] = cum_rows
    rows_ref[all_heads:] = dt_rows
    weight = jnp.exp(cum_end - cum_rows) * dt_rows
    for block in range(blocks):
        end_scr[block] = weight[block * BLOCK_HEADS:(block + 1) * BLOCK_HEADS]
    for device in range(devices):
        grow_scr[device, :slice_heads] = grow[device * slice_heads:(device + 1) * slice_heads]
    grow_last = jnp.sum(jnp.where(lax.broadcasted_iota(jnp.int32, grow.shape, 1) == length - 1, grow, 0.0), axis=1,
                        keepdims=True)
    through = jnp.where(last_start < 0, jnp.broadcast_to(grow_last, (all_heads, state_dim)), 0.0)
    for part in range(devices * CHUNKS):
        at = part * chunk // head_dim
        through_scr[part] = through[at:at + chunk_heads]
    upright = jnp.concatenate([cum_rows, grow], 0).T
    begun = start[:, :group_heads] < 0
    for group in range(groups):
        at = group * group_heads
        cols_ref[group, :, :group_heads] = upright[:, at:at + group_heads]
        cols_ref[group, :, group_heads:] = jnp.where(begun, upright[:, all_heads + at:all_heads + at + group_heads], 0.0)

    pl.semaphore_wait(barrier, devices - 1)

    right = (me + 1) % devices
    gate_copy = pltpu.make_async_copy(gate_hbm, gate_scr, gate_sem)
    gate_copy.start()

    def rim_copies():
        return (remote(x_ref.at[pl.ds(length - RIM, RIM)], rimx_scr, rim_send.at[0], rim_recv.at[0], right),
                remote(bc_ref.at[pl.ds(length - RIM, RIM)], rimbc_scr, rim_send.at[1], rim_recv.at[1], right))

    @pl.when(me < devices - 1)
    def _():
        for copy in rim_copies():
            copy.start()

    def others(act):
        @pl.loop(0, devices)
        def _(k):
            to = (me + spread(k, devices)) % devices

            @pl.when(to != me)
            def _():
                act(to)

    def d_copy(to):
        return remote(grow_scr.at[to], gd_scr.at[me], d_send.at[to], d_recv.at[me], to)

    others(lambda to: d_copy(to).start())
    own_d = pltpu.make_async_copy(grow_scr.at[me], gd_scr.at[me], own_sem.at[0])
    own_d.start()

    @pl.when(me > 0)
    def _():
        for copy in rim_copies():
            copy.wait_recv()

    for part in range(2 * groups):
        cols = slice(part * state_dim, (part + 1) * state_dim)
        after = slice(inner + part * state_dim, inner + (part + 1) * state_dim)
        value = conv_silu(bc_ref[:, cols], rimbc_scr[:, cols], mask_scr, taps_ref[:, after], bias_ref[:, after])
        if part < groups:
            b_scr[:, cols] = value
            bsend_scr[part] = value
            blast_scr[part] = jnp.where(last, value, jnp.zeros_like(value))
        else:
            c_scr[:, (part - groups) * state_dim:(part - groups + 1) * state_dim] = value

    def b_copy(group):
        return remote(bsend_scr.at[group], gb_scr.at[me], b_send.at[group], b_recv.at[me],
                      group * per_group + place)

    own_b = pltpu.make_async_copy(bsend_scr.at[quarter], gb_scr.at[me], own_sem.at[1])
    own_b.start()
    for group in range(groups):
        @pl.when(quarter != group)
        def _():
            b_copy(group).start()

    def slice_rows(to, part):
        return pl.ds(pl.multiple_of(to * slice_width + part * chunk, chunk), chunk)

    def x_copy(part, to):
        return remote(wt_scr.at[slice_rows(to, part)], gx_scr.at[part, me], x_send.at[part, to], x_recv.at[part, me],
                      to)

    def one_block(k):
        block = (me // per_block + spread(k, blocks)) % blocks
        cols = pl.ds(pl.multiple_of(block * width, width), width)
        xs = conv_silu(x_ref[:, cols], rimx_scr[:, cols], mask_scr, taps_ref[:, cols], bias_ref[:, cols])
        xs_scr[:, cols] = xs
        x_t = xs.astype(jnp.float32).T.reshape(BLOCK_HEADS, head_dim, length)
        weighted = (x_t * end_scr[block][:, None, :]).astype(jnp.bfloat16).reshape(width, length)
        wt_scr[cols, :] = weighted

        @pl.loop(0, per_block)
        def _(part):
            to = block * per_block + part

            @pl.when(to != me)
            def _():
                x_copy(0, to).start()

        local = jnp.dot(weighted, blast_scr[block // blocks_per_group], preferred_element_type=jnp.float32)
        for part in range(per_block * CHUNKS):
            local_scr[block * per_block * CHUNKS + part] = local[part * chunk:(part + 1) * chunk]

        @pl.when(me % 2 == 0)
        def _():
            for part in range(per_block * CHUNKS):
                at = block * per_block + part // CHUNKS
                coded = encode(local[part * chunk:(part + 1) * chunk])
                code_scr[part % CHUNKS, at, :chunk], code_scr[part % CHUNKS, at, chunk:] = coded

    half = blocks // 2

    @pl.loop(0, half)
    def _(k):
        one_block(k)

    def f_copy(frm, by):
        to = quarter * per_group + (place + by) % per_group
        return remote(gb_scr.at[frm], gb_scr.at[frm], f_send.at[frm // per_group, by], f_recv.at[frm], to)

    own_b.wait()
    for frm_quarter in range(groups):
        frm = frm_quarter * per_group + place

        @pl.when(quarter != frm_quarter)
        def _():
            remote(bsend_scr.at[0], gb_scr.at[frm], b_send.at[0], b_recv.at[frm], me).wait_recv()

        for by in range(1, per_group):
            f_copy(frm, by).start()

    @pl.loop(half, blocks)
    def _(k):
        one_block(k)

    for part in range(1, CHUNKS):
        others(lambda to: x_copy(part, to).start())

    own_x = [pltpu.make_async_copy(wt_scr.at[slice_rows(me, part)], gx_scr.at[part, me], own_sem.at[2 + part])
             for part in range(CHUNKS)]
    for copy in own_x:
        copy.start()

    sends = (me < devices - 1) & (me != middle - 1)
    receives = (me > 0) & (me != middle)

    def landing(step):
        return in_ref if step >= steps - 2 else rec_scr.at[step]

    def hand_copy(step, part):
        return remote(code_scr.at[part], landing(step).at[part], hand_send.at[step, part], hand_recv.at[step, part],
                      right)

    def hand_over(step):
        @pl.when(me % 2 == step % 2)
        def _():
            for part in range(CHUNKS):
                if step >= 2:
                    @pl.when(sends)
                    def _():
                        hand_copy(step - 2, part).wait_send()

                if step >= 1:
                    @pl.when(receives)
                    def _():
                        hand_copy(step - 1, part).wait_recv()

                    got = landing(step - 1)

                    @pl.loop(0, devices)
                    def _(at):
                        factor = through_scr[at * CHUNKS + part]
                        factor = jnp.broadcast_to(factor[:, None, :],
                                                  (chunk_heads, chunk // chunk_heads, state_dim))
                        value = decode(got[part, at, :chunk], got[part, at, chunk:])
                        value = factor.reshape(chunk, state_dim) * value + local_scr[at * CHUNKS + part]
                        code_scr[part, at, :chunk], code_scr[part, at, chunk:] = encode(value)

                @pl.when(sends)
                def _():
                    hand_copy(step, part).start()

    for step in range(2):
        hand_over(step)

    docs_here = owners_ref.shape[0]

    @pl.loop(0, devices)
    def _(block):
        first_scr[block] = lax.fori_loop(
            0, docs_here + 1, lambda k, n: n + (offsets_ref[k] <= block * length).astype(jnp.int32), jnp.int32(0))

    @pl.loop(0, docs_here)
    def _(doc):
        owner = owners_ref[doc]
        rank = lax.fori_loop(
            0, docs_here, lambda k, n: n + ((owners_ref[k] == owner) & (k < doc)).astype(jnp.int32), jnp.int32(0))
        end_at = offsets_ref[doc + 1] - 1
        block = lax.fori_loop(
            1, devices, lambda k, n: n + (end_at >= k * length).astype(jnp.int32), jnp.int32(0))
        dest_scr[doc] = owner * OWNER_SLOTS + rank
        slot = jnp.clip(doc + 1 - first_scr[block], 0, END_SLOTS - 1)
        source_scr[doc] = block * END_SLOTS + slot

    @pl.loop(0, devices * OWNER_SLOTS)
    def _(at):
        pick_scr[at] = lax.fori_loop(
            0, docs_here, lambda k, n: jnp.where(dest_scr[k] == at, source_scr[k], n),
            jnp.int32(devices * END_SLOTS))

    for part in range(CHUNKS):
        slot_scr[part, devices * END_SLOTS] = jnp.zeros(slot_scr.shape[2:], jnp.int16)

    row = lax.broadcasted_iota(jnp.int32, (length, state_dim), 0)
    lane = lax.broadcasted_iota(jnp.int32, (slice_heads, length), 1)

    def mid_copy(part):
        return remote(mid_scr.at[part], in_ref.at[part, me], mid_send.at[part], mid_recv.at[part, me], middle)

    own_mid = [pltpu.make_async_copy(mid_scr.at[part], in_ref.at[part, middle], own_sem.at[2 + CHUNKS + part])
               for part in range(CHUNKS)]

    def states(part):
        def one(block, carry):
            first = block * length
            b_val = gb_scr[block].astype(jnp.float32)
            at = first_scr[block]
            cuts = [offsets_ref[jnp.minimum(at + k, docs_here)] - first for k in range(END_SLOTS)]
            last_cut = jnp.int32(0)
            for cut in cuts:
                last_cut = jnp.where(cut < length, cut, last_cut)
            begin, masked = jnp.int32(0), []
            for cut in cuts:
                masked.append(jnp.where((row >= begin) & (row < cut), b_val, 0.0).astype(jnp.bfloat16))
                begin = cut
            masked.append(jnp.where(row >= last_cut, b_val, 0.0).astype(jnp.bfloat16))
            local = jnp.dot(gx_scr[part, block], jnp.concatenate(masked, 1), preferred_element_type=jnp.float32)
            end_at = jnp.minimum(cuts[0], length) - 1
            begun = offsets_ref[jnp.maximum(at - 1, 0)] < first
            factor = jnp.sum(jnp.where((lane == end_at) & begun, gd_scr[block][:slice_heads], 0.0), axis=1, keepdims=True)
            head = part * chunk // head_dim
            factor = jnp.broadcast_to(factor[head:head + chunk_heads][:, :, None],
                                      (chunk_heads, chunk // chunk_heads, state_dim)).reshape(chunk, state_dim)
            kept = factor * carry
            for k in range(END_SLOTS):
                value = local[:, k * state_dim:(k + 1) * state_dim]
                coded = encode(value + kept if k == 0 else value)
                at_slot = block * END_SLOTS + k
                slot_scr[part, at_slot, :chunk], slot_scr[part, at_slot, chunk:] = coded
            carry = local[:, END_SLOTS * state_dim:] + jnp.where(cuts[0] >= length, kept, 0.0)

            @pl.when(block == middle - 1)
            def _():
                mid_scr[part, :chunk], mid_scr[part, chunk:] = encode(carry)

                @pl.when(me != middle)
                def _():
                    mid_copy(part).start()

                @pl.when(me == middle)
                def _():
                    own_mid[part].start()

            return carry

        lax.fori_loop(0, devices, one, jnp.zeros((chunk, state_dim), jnp.float32))

    def out_copy(part, to):
        return remote(table_scr.at[part, to], out_ref.at[part, me], out_send.at[part, to], out_recv.at[part, me], to)

    own_out = [pltpu.make_async_copy(table_scr.at[part, me], out_ref.at[part, me], own_sem.at[2 + 2 * CHUNKS + part])
               for part in range(CHUNKS)]

    own_d.wait()

    @pl.loop(0, devices)
    def _(other):
        @pl.when(other != me)
        def _():
            remote(grow_scr.at[0], gd_scr.at[other], d_send.at[other], d_recv.at[other], other).wait_recv()

        @pl.when(other % per_group != place)
        def _():
            remote(gb_scr.at[other], gb_scr.at[other], f_send.at[0, 1], f_recv.at[other], other).wait_recv()

    for part in range(CHUNKS):
        own_x[part].wait()

        @pl.loop(0, devices)
        def _(other):
            @pl.when(other != me)
            def _():
                remote(wt_scr.at[pl.ds(0, chunk)], gx_scr.at[part, other], x_send.at[part, other],
                       x_recv.at[part, other], other).wait_recv()

        states(part)

        @pl.loop(0, devices)
        def _(k):
            to = (me + spread(k, devices)) % devices
            levels = []
            for slot in range(OWNER_SLOTS):
                source = pick_scr[to * OWNER_SLOTS + slot]
                table_scr[part, to, slot * chunk:(slot + 1) * chunk] = slot_scr[part, source, :chunk]
                levels.append(slot_scr[part, source, chunk:].astype(jnp.int32)[:SCALE_ROWS // OWNER_SLOTS])
            table_scr[part, to, OWNER_SLOTS * chunk:] = jnp.concatenate(levels, 0).astype(jnp.int16)

            @pl.when(to != me)
            def _():
                out_copy(part, to).start()

        own_out[part].start()

    @pl.when(me == middle)
    def _():
        for part in range(CHUNKS):
            own_mid[part].wait()

            @pl.loop(0, devices)
            def _(other):
                @pl.when(other != me)
                def _():
                    remote(mid_scr.at[part], in_ref.at[part, other], mid_send.at[part], mid_recv.at[part, other],
                           other).wait_recv()

        for step in range(1, steps - 2, 2):
            rec_scr[step] = in_ref[...]

    for step in range(2, steps):
        hand_over(step)

    @pl.when((me % 2 != (steps - 1) % 2) & receives)
    def _():
        for part in range(CHUNKS):
            hand_copy(steps - 1, part).wait_recv()

    gate_copy.wait()

    def gated_copy(group):
        cols = pl.ds(pl.multiple_of(group * (inner // groups), inner // groups), inner // groups)
        return pltpu.make_async_copy(gated_scr.at[:, cols], gated_hbm.at[:, cols], gated_sem.at[group])

    @pl.loop(0, groups)
    def _(group):
        scan_group(groups, group, skip_ref, xs_scr, gate_scr, in_ref, b_scr, c_scr, rows_ref, cols_ref, start_ref,
                   norm_ref, gated_scr, v_scr)
        gated_copy(group).start()

    @pl.when(me < devices - 1)
    def _():
        for copy in rim_copies():
            copy.wait_send()

    @pl.when(sends)
    def _():
        for step in range(steps - 2, steps):
            @pl.when(me % 2 == step % 2)
            def _():
                for part in range(CHUNKS):
                    hand_copy(step, part).wait_send()

    @pl.when(me != middle)
    def _():
        for part in range(CHUNKS):
            mid_copy(part).wait_send()

    for group in range(groups):
        @pl.when(quarter != group)
        def _():
            b_copy(group).wait_send()

    for frm_quarter in range(groups):
        for by in range(1, per_group):
            f_copy(frm_quarter * per_group + place, by).wait_send()

    @pl.loop(0, groups)
    def _(group):
        gated_copy(group).wait()

    for part in range(CHUNKS):
        own_out[part].wait()

    @pl.loop(0, devices)
    def _(other):
        @pl.when(other != me)
        def _():
            d_copy(other).wait_send()
            for part in range(CHUNKS):
                x_copy(part, other).wait_send()
                out_copy(part, other).wait_send()
                remote(table_scr.at[part, 0], out_ref.at[part, other], out_send.at[part, other],
                       out_recv.at[part, other], other).wait_recv()


def scan_group(groups, group, skip_ref, xs_ref, gate_ref, in_ref, b_ref, c_ref, rows_ref, cols_ref, start_ref,
               norm_ref, out_ref, v_scr):
    length, inner = xs_ref.shape
    state_dim = b_ref.shape[1] // groups
    all_heads = rows_ref.shape[0] // 2
    group_heads = all_heads // groups
    group_width = inner // groups
    blocks = group_heads // BLOCK_HEADS
    width = group_width // blocks
    head_dim = width // BLOCK_HEADS
    per_block = in_ref.shape[1] // (groups * blocks)
    chunk = in_ref.shape[2] - SCALE_ROWS
    state_cols = pl.ds(pl.multiple_of(group * state_dim, state_dim), state_dim)
    c_val = c_ref[:, state_cols]
    contract = (((1,), (1,)), ((), ()))
    scores = lax.dot_general(c_val, b_ref[:, state_cols], contract, preferred_element_type=jnp.float32)
    row = lax.broadcasted_iota(jnp.int32, (length, length), 0)
    col = lax.broadcasted_iota(jnp.int32, (length, length), 1)
    causal = (col <= row) & (col >= start_ref[:, :1])
    part = lax.broadcasted_iota(jnp.int32, (length, width), 1) // head_dim
    part_row = lax.broadcasted_iota(jnp.int32, (1, width), 1) // head_dim
    cum_rows = rows_ref[pl.ds(pl.multiple_of(group * group_heads, group_heads), group_heads), :]
    dt_rows = rows_ref[pl.ds(pl.multiple_of(all_heads + group * group_heads, group_heads), group_heads), :]
    columns = cols_ref[group]
    square = jnp.zeros((length, 1), jnp.float32)
    for block in range(blocks):
        here = pl.ds(pl.multiple_of(group * group_width + block * width, width), width)
        xs = xs_ref[:, here]
        weights, split = [], []
        cont = jnp.zeros((length, width), jnp.float32)
        skip = jnp.zeros((1, width), jnp.float32)
        for head in range(BLOCK_HEADS):
            at = block * BLOCK_HEADS + head
            gap = columns[:, at:at + 1] - cum_rows[at:at + 1]
            decay = jnp.exp(jnp.where(causal, gap, -jnp.inf))
            weights.append((scores * decay * dt_rows[at:at + 1]).astype(jnp.bfloat16))
            split.append(jnp.where(part == head, xs, jnp.zeros_like(xs)))
            cont = jnp.where(part == head, columns[:, group_heads + at:group_heads + at + 1], cont)
            skip = jnp.where(part_row == head, skip_ref[group * group_heads + at], skip)
        intra = jnp.dot(jnp.concatenate(weights, 1), jnp.concatenate(split, 0), preferred_element_type=jnp.float32)
        pieces = []
        for piece in range(per_block * CHUNKS):
            at = (group * blocks + block) * per_block + piece // CHUNKS
            pieces.append(decode(in_ref[piece % CHUNKS, at, :chunk], in_ref[piece % CHUNKS, at, chunk:]))
        state = jnp.concatenate(pieces, 0)
        high = state.astype(jnp.bfloat16)
        low = (state - high.astype(jnp.float32)).astype(jnp.bfloat16)
        inter = lax.dot_general(c_val, high, contract, preferred_element_type=jnp.float32)
        inter = inter + lax.dot_general(c_val, low, contract, preferred_element_type=jnp.float32)
        y_sum = intra + inter * cont + skip * xs.astype(jnp.float32)
        gate = gate_ref[:, here].astype(jnp.float32)
        value = y_sum * (gate / (1.0 + jnp.exp(-gate)))
        v_scr[:, block * width:(block + 1) * width] = value
        square = square + jnp.sum(value * value, axis=1, keepdims=True)
    scale = lax.rsqrt(square / group_width + 1e-05)
    whole = pl.ds(pl.multiple_of(group * group_width, group_width), group_width)
    out_ref[:, whole] = (v_scr[...] * scale * norm_ref[:, whole]).astype(jnp.bfloat16)


def deliver_kernel(code_ref, out_ref):
    sources = code_ref.shape[1]
    slots, heads, head_dim, state_dim = out_ref.shape
    chunk = (code_ref.shape[2] - SCALE_ROWS) // slots
    for source in range(sources):
        for part in range(CHUNKS):
            level = code_ref[part, source, slots * chunk:].astype(jnp.int32)
            for slot in range(slots):
                at = slot * (SCALE_ROWS // slots)
                value = decode(code_ref[part, source, slot * chunk:(slot + 1) * chunk], level[at:])
                first = (source * CHUNKS + part) * chunk
                head, row = first // head_dim, first % head_dim
                if chunk >= head_dim:
                    value = value.reshape(chunk // head_dim, head_dim, state_dim)
                    out_ref[slot, head:head + chunk // head_dim] = value
                else:
                    out_ref[slot, head, row:row + chunk] = value


def per_device(
    ssm_input,
    gate_input,
    bc_input,
    dt_raw,
    offsets,
    owners,
    conv_weight,
    convolution_bias,
    a_log,
    dt_bias,
    d_skip,
    norm_weight,
):
    length, inner_dim = ssm_input.shape
    heads = a_log.shape[0]
    head_dim = inner_dim // heads
    groups = heads // GROUP_HEADS
    state_dim = bc_input.shape[1] // (2 * groups)
    devices = lax.axis_size("ctx")
    relays = devices // 8 - 1
    blocks = heads // BLOCK_HEADS
    width = BLOCK_HEADS * head_dim
    group_state = groups * state_dim
    group_width = inner_dim // groups
    device_width = inner_dim // devices
    device_heads = heads // devices
    slice_rows = -(-device_heads // 8) * 8

    vmem = pl.BlockSpec(memory_space=pltpu.VMEM)
    smem = pl.BlockSpec(memory_space=pltpu.SMEM)
    anywhere = pl.BlockSpec(memory_space=pl.ANY)
    dma = pltpu.SemaphoreType.DMA
    per_group = devices // groups
    steps = relays + 2
    docs = owners.shape[0]
    chunk = device_width // CHUNKS
    chunk_heads = max(chunk // head_dim, 1)
    table_rows = OWNER_SLOTS * chunk + SCALE_ROWS
    code = lambda *lead: pltpu.VMEM(lead + (chunk + SCALE_ROWS, state_dim), jnp.int16)
    half = lambda *shape: pltpu.VMEM(shape, jnp.bfloat16)
    full = lambda *shape: pltpu.VMEM(shape, jnp.float32)
    delivered, gated_out = pl.pallas_call(
        functools.partial(whole_kernel, devices, groups, relays),
        in_specs=[smem] * 3 + [vmem] * 8 + [anywhere],
        out_specs=[anywhere] * 2,
        out_shape=[
            jax.ShapeDtypeStruct((CHUNKS, devices, table_rows, state_dim), jnp.int16),
            jax.ShapeDtypeStruct((length, inner_dim), jnp.bfloat16),
        ],
        scratch_shapes=[
            half(RIM, inner_dim),
            half(RIM, 2 * group_state),
            half(length, inner_dim),
            half(length, group_state),
            half(length, group_state),
            half(inner_dim, length),
            half(groups, length, state_dim),
            full(devices * CHUNKS, chunk, state_dim),
            code(CHUNKS, devices),
            code(max(relays, 1), CHUNKS, devices),
            code(CHUNKS, devices),
            half(groups, length, state_dim),
            full(KERNEL_WIDTH - 1, length, state_dim),
            full(blocks, BLOCK_HEADS, length),
            full(devices, slice_rows, length),
            full(devices * CHUNKS, chunk_heads, state_dim),
            full(2 * heads, length),
            full(groups, length, 2 * GROUP_HEADS),
            pltpu.VMEM((length, state_dim), jnp.int32),
            half(CHUNKS, devices, chunk, length),
            half(devices, length, state_dim),
            full(devices, slice_rows, length),
            code(CHUNKS, devices * END_SLOTS + 1),
            pltpu.VMEM((CHUNKS, devices, table_rows, state_dim), jnp.int16),
            code(CHUNKS),
            half(length, inner_dim),
            half(length, inner_dim),
            full(length, group_width),
            pltpu.SMEM((devices,), jnp.int32),
            pltpu.SMEM((docs,), jnp.int32),
            pltpu.SMEM((docs,), jnp.int32),
            pltpu.SMEM((devices * OWNER_SLOTS,), jnp.int32),
            dma((2,)), dma((2,)),
            dma((CHUNKS, devices)), dma((CHUNKS, devices)),
            dma((groups,)), dma((devices,)),
            dma((groups, per_group)), dma((devices,)),
            dma((devices,)), dma((devices,)),
            dma((steps, CHUNKS)), dma((steps, CHUNKS)),
            dma((CHUNKS,)), dma((CHUNKS, devices)),
            dma((CHUNKS, devices)), dma((CHUNKS, devices)),
            dma((2 + 3 * CHUNKS,)), dma, dma((groups,)),
        ],
        compiler_params=pltpu.CompilerParams(
            collective_id=0, has_side_effects=True, vmem_limit_bytes=VMEM_LIMIT),
        name="layer",
    )(offsets, owners, d_skip, ssm_input, bc_input, dt_raw, conv_weight, convolution_bias[None, :], a_log[None, :],
      dt_bias[None, :], norm_weight[None, :], gate_input)

    sources = devices // 4
    decode_states = pl.pallas_call(
        deliver_kernel,
        grid=(4,),
        in_specs=[pl.BlockSpec((CHUNKS, sources, table_rows, state_dim), lambda j: (0, j, 0, 0))],
        out_specs=pl.BlockSpec((OWNER_SLOTS, heads // 4, head_dim, state_dim), lambda j: (0, j, 0, 0)),
        out_shape=jax.ShapeDtypeStruct((OWNER_SLOTS, heads, head_dim, state_dim), jnp.float32),
        name="deliver",
    )(delivered)
    return (gated_out, decode_states)


def solution(mesh):
    in_specs = (
        P(("groups", "ctx"), None),
        P(("groups", "ctx"), None),
        P(("groups", "ctx"), None),
        P(("groups", "ctx"), None),
        P("groups"),
        P("groups"),
        P(),
        P(),
        P(),
        P(),
        P(),
        P(),
    )
    out_specs = (P(("groups", "ctx"), None), P(("groups", "ctx"), None, None, None))
    return jax.shard_map(
        per_device, mesh=mesh, in_specs=in_specs, out_specs=out_specs, check_vma=False
    )
```

```python
import functools
import math
import jax
import jax.numpy as jnp
from jax import lax
from jax.experimental import pallas as pl
from jax.experimental.pallas import tpu as pltpu
from jax.sharding import PartitionSpec as P

GROUP_HEADS = 16
KERNEL_WIDTH = 4
OWNER_SLOTS = 2
BLOCK_HEADS = 4
RIM = 16
SCALE_ROWS = 16
LEVELS = 8.0
CODE_MAX = 32767.0
END_SLOTS = 4
CHUNKS = 2
VMEM_LIMIT = 56 * 1024 * 1024
MESH = pl.DeviceIdType.MESH


def encode(value):
    rows, lanes = value.shape
    parts = value.reshape(rows // SCALE_ROWS, SCALE_ROWS, lanes)
    top = jnp.max(jnp.abs(parts), axis=1)
    level = jnp.ceil(jnp.log(jnp.maximum(top, 1e-30)) * (LEVELS / math.log(2.0)))
    unit = jnp.exp2(level * (-1.0 / LEVELS)) * CODE_MAX
    coded = jnp.clip(jnp.round(parts * unit[:, None, :]), -CODE_MAX, CODE_MAX).reshape(rows, lanes)
    if level.shape[0] < SCALE_ROWS:
        level = jnp.concatenate([level, jnp.zeros((SCALE_ROWS - level.shape[0], lanes), jnp.float32)], 0)
    return coded.astype(jnp.int32).astype(jnp.int16), level.astype(jnp.int32).astype(jnp.int16)


def decode(coded, level):
    rows, lanes = coded.shape
    unit = jnp.exp2(level.astype(jnp.int32).astype(jnp.float32) * (1.0 / LEVELS)) * (1.0 / CODE_MAX)
    unit = unit[:rows // SCALE_ROWS]
    parts = coded.astype(jnp.int32).astype(jnp.float32).reshape(rows // SCALE_ROWS, SCALE_ROWS, lanes)
    return (parts * unit[:, None, :]).reshape(rows, lanes)


def conv_silu(x, rim, mask_ref, weight, bias):
    x = x.astype(jnp.float32)
    padded = jnp.concatenate([rim.astype(jnp.float32), x], 0)
    total = bias
    for tap in range(KERNEL_WIDTH - 1):
        mask = jnp.concatenate([mask_ref[tap]] * (x.shape[1] // mask_ref.shape[2]), 1)
        total = total + weight[tap:tap + 1] * (mask * pltpu.roll(padded, KERNEL_WIDTH - 1 - tap, 0)[RIM:])
    total = total + weight[KERNEL_WIDTH - 1:KERNEL_WIDTH] * x
    return (total / (1.0 + jnp.exp(-total))).astype(jnp.bfloat16)


def spread(k, count):
    half = (k + 1) // 2
    return count // 2 + half * (1 - 2 * (k % 2))


def enter(axis, me, devices):
    barrier = pltpu.get_barrier_semaphore()

    @pl.loop(1, devices)
    def _(by):
        pl.semaphore_signal(barrier, inc=1, device_id={axis: (me + by) % devices}, device_id_type=MESH)

    return barrier


def exact_dot(a, b):
    return jnp.dot(a, b, precision=lax.Precision.HIGHEST, preferred_element_type=jnp.float32)


def whole_kernel(devices, groups, relays, offsets_ref, owners_ref, skip_ref, dt_ref, bias_ref, a_ref, dt_bias_ref,
                 norm_ref, x_hbm, bc_hbm, taps_hbm, gate_hbm, out_ref, gated_hbm,
                 x_ref, bc_ref, taps_ref, rimx_scr, rimbc_scr, xs_scr, b_scr, c_scr, wt_scr, blast_scr, local_scr, code_scr, rec_scr, in_ref,
                 bsend_scr, mask_scr, end_scr, grow_scr, through_scr, rows_ref, cols_ref, start_ref, gx_scr, gb_scr,
                 gd_scr, slot_scr, table_scr, mid_scr, gate_scr, gated_scr, v_scr, first_scr, dest_scr, source_scr,
                 pick_scr,
                 rim_send, rim_recv, x_send, x_recv, b_send, b_recv, f_send, f_recv, d_send, d_recv, hand_send,
                 hand_recv, mid_send, mid_recv, out_send, out_recv, own_sem, load_sem, gated_sem):
    me = lax.axis_index("ctx")
    length, inner = x_ref.shape
    blocks = end_scr.shape[0]
    width = inner // blocks
    state_dim = blast_scr.shape[2]
    all_heads = dt_ref.shape[0]
    head_dim = inner // all_heads
    per_block = devices // blocks
    slice_width = width // per_block
    slice_heads = all_heads // devices
    chunk = slice_width // CHUNKS
    chunk_heads = max(chunk // head_dim, 1)
    per_group = devices // groups
    blocks_per_group = blocks // groups
    group_heads = all_heads // groups
    quarter = me // per_group
    place = me % per_group
    steps = relays + 2
    middle = devices // 2

    def remote(src, dst, send, recv, to):
        return pltpu.make_async_remote_copy(src_ref=src, dst_ref=dst, send_sem=send, recv_sem=recv,
                                            device_id={"ctx": to}, device_id_type=MESH)

    barrier = enter("ctx", me, devices)
    loads = [pltpu.make_async_copy(src, dst, load_sem.at[k]) for k, (src, dst) in enumerate(
        ((bc_hbm, bc_ref), (taps_hbm, taps_ref), (x_hbm, x_ref), (gate_hbm, gate_scr)))]
    for load in loads:
        load.start()

    @pl.when(me == 0)
    def _():
        rimx_scr[...] = jnp.zeros_like(rimx_scr)
        rimbc_scr[...] = jnp.zeros_like(rimbc_scr)
        in_ref[...] = jnp.zeros_like(in_ref)
        rec_scr[...] = jnp.zeros_like(rec_scr)

    base = me * length
    docs = offsets_ref.shape[0] - 1
    token = lax.broadcasted_iota(jnp.int32, (length, state_dim), 0)
    along = lax.broadcasted_iota(jnp.int32, (8, length), 1)

    def bounds(k, carry):
        start, end = carry
        offset = offsets_ref[k] - base
        start = jnp.where(offset <= token, jnp.maximum(start, offset), start)
        end = jnp.where(offset > along, jnp.minimum(end, offset), end)
        return start, end

    start, end = lax.fori_loop(0, docs + 1, bounds, (jnp.full((length, state_dim), -base, jnp.int32),
                                                     jnp.full((8, length), length, jnp.int32)))
    end = end - 1
    start_ref[...] = start
    for tap in range(KERNEL_WIDTH - 1):
        mask_scr[tap] = jnp.where(token + (tap - KERNEL_WIDTH + 1) >= start, 1.0, 0.0).astype(jnp.float32)
    last_start = jnp.max(start, axis=0, keepdims=True)
    last = token >= last_start

    pair = jnp.concatenate([dt_bias_ref[...], a_ref[...]], 1)
    pair = jnp.broadcast_to(pair, (8, 2 * all_heads)).T
    pre = dt_ref[...] + pair[:all_heads, :1]
    dt_rows = jnp.maximum(pre, 0.0) + jnp.log1p(jnp.exp(-jnp.abs(pre)))
    logdec = -dt_rows * jnp.exp(pair[all_heads:, :1])
    one = lax.broadcasted_iota(jnp.int32, (length, length), 0)
    two = lax.broadcasted_iota(jnp.int32, (length, length), 1)
    cum_rows = exact_dot(logdec, jnp.where(one <= two, 1.0, 0.0).astype(jnp.float32))
    cum_end = exact_dot(cum_rows, jnp.where(one == end[:1], 1.0, 0.0).astype(jnp.float32))
    grow = jnp.exp(cum_rows)
    rows_ref[:all_heads] = cum_rows
    rows_ref[all_heads:] = dt_rows
    weight = jnp.exp(cum_end - cum_rows) * dt_rows
    for block in range(blocks):
        end_scr[block] = weight[block * BLOCK_HEADS:(block + 1) * BLOCK_HEADS]
    first_end = jnp.min(end, axis=1, keepdims=True)[:1]
    grow_first = jnp.sum(jnp.where(lax.broadcasted_iota(jnp.int32, grow.shape, 1) == first_end, grow, 0.0), axis=1,
                         keepdims=True)
    carried = jnp.where(start[:1] < 0, jnp.broadcast_to(grow_first, (all_heads, state_dim)), 0.0)
    for device in range(devices):
        grow_scr[device, :slice_heads] = carried[device * slice_heads:(device + 1) * slice_heads]
    grow_last = jnp.sum(jnp.where(lax.broadcasted_iota(jnp.int32, grow.shape, 1) == length - 1, grow, 0.0), axis=1,
                        keepdims=True)
    through = jnp.where(last_start < 0, jnp.broadcast_to(grow_last, (all_heads, state_dim)), 0.0)
    for part in range(devices * CHUNKS):
        at = part * chunk // head_dim
        through_scr[part] = through[at:at + chunk_heads]
    upright = jnp.concatenate([cum_rows, grow], 0).T
    begun = start[:, :group_heads] < 0
    for group in range(groups):
        at = group * group_heads
        cols_ref[group, :, :group_heads] = upright[:, at:at + group_heads]
        cols_ref[group, :, group_heads:] = jnp.where(begun, upright[:, all_heads + at:all_heads + at + group_heads], 0.0)

    pl.semaphore_wait(barrier, devices - 1)

    right = (me + 1) % devices

    def rim_copy(k):
        src, dst = ((bc_hbm, rimbc_scr), (x_hbm, rimx_scr))[k]
        return remote(src.at[pl.ds(length - RIM, RIM)], dst, rim_send.at[k], rim_recv.at[k], right)

    @pl.when(me < devices - 1)
    def _():
        for k in range(2):
            rim_copy(k).start()

    def others(act):
        @pl.loop(0, devices)
        def _(k):
            to = (me + spread(k, devices)) % devices

            @pl.when(to != me)
            def _():
                act(to)

    def d_copy(to):
        return remote(grow_scr.at[to], gd_scr.at[me], d_send.at[to], d_recv.at[me], to)

    others(lambda to: d_copy(to).start())
    own_d = pltpu.make_async_copy(grow_scr.at[me], gd_scr.at[me], own_sem.at[0])
    own_d.start()

    loads[0].wait()
    loads[1].wait()

    @pl.when(me > 0)
    def _():
        rim_copy(0).wait_recv()

    for part in range(2 * groups):
        cols = slice(part * state_dim, (part + 1) * state_dim)
        after = slice(inner + part * state_dim, inner + (part + 1) * state_dim)
        value = conv_silu(bc_ref[:, cols], rimbc_scr[:, cols], mask_scr, taps_ref[:, after], bias_ref[:, after])
        if part < groups:
            b_scr[:, cols] = value
            bsend_scr[part] = value
            blast_scr[part] = jnp.where(last, value, jnp.zeros_like(value))
        else:
            c_scr[:, (part - groups) * state_dim:(part - groups + 1) * state_dim] = value

    def b_copy(group):
        return remote(bsend_scr.at[group], gb_scr.at[me], b_send.at[group], b_recv.at[me],
                      group * per_group + place)

    own_b = pltpu.make_async_copy(bsend_scr.at[quarter], gb_scr.at[me], own_sem.at[1])
    own_b.start()
    for group in range(groups):
        @pl.when(quarter != group)
        def _():
            b_copy(group).start()

    def slice_rows(to, part):
        return pl.ds(pl.multiple_of(to * slice_width + part * chunk, chunk), chunk)

    def x_copy(part, to):
        return remote(wt_scr.at[slice_rows(to, part)], gx_scr.at[part, me], x_send.at[part, to], x_recv.at[part, me],
                      to)

    def near(device):
        return (device >= middle - 1 - relays) & (device < middle)

    def one_block(k):
        block = (me // per_block + spread(k, blocks)) % blocks
        cols = pl.ds(pl.multiple_of(block * width, width), width)
        xs = conv_silu(x_ref[:, cols], rimx_scr[:, cols], mask_scr, taps_ref[:, cols], bias_ref[:, cols])
        xs_scr[:, cols] = xs
        x_t = xs.astype(jnp.float32).T.reshape(BLOCK_HEADS, head_dim, length)
        weighted = (x_t * end_scr[block][:, None, :]).astype(jnp.bfloat16).reshape(width, length)
        wt_scr[cols, :] = weighted

        @pl.loop(0, per_block)
        def _(part):
            to = block * per_block + part

            @pl.when(to != me)
            def _():
                x_copy(0, to).start()

                @pl.when(near(me))
                def _():
                    for later in range(1, CHUNKS):
                        x_copy(later, to).start()

        local = jnp.dot(weighted, blast_scr[block // blocks_per_group], preferred_element_type=jnp.float32)
        for part in range(per_block * CHUNKS):
            local_scr[block * per_block * CHUNKS + part] = local[part * chunk:(part + 1) * chunk]

        @pl.when(me % 2 == 0)
        def _():
            for part in range(per_block * CHUNKS):
                at = block * per_block + part // CHUNKS
                coded = encode(local[part * chunk:(part + 1) * chunk])
                code_scr[part % CHUNKS, at, :chunk], code_scr[part % CHUNKS, at, chunk:] = coded

    loads[2].wait()

    @pl.when(me > 0)
    def _():
        rim_copy(1).wait_recv()

    half = blocks // 2

    @pl.loop(0, half)
    def _(k):
        one_block(k)

    def f_copy(frm, by):
        to = quarter * per_group + (place + by) % per_group
        return remote(gb_scr.at[frm], gb_scr.at[frm], f_send.at[frm // per_group, by], f_recv.at[frm], to)

    own_b.wait()
    for frm_quarter in range(groups):
        frm = frm_quarter * per_group + place

        @pl.when(quarter != frm_quarter)
        def _():
            remote(bsend_scr.at[0], gb_scr.at[frm], b_send.at[0], b_recv.at[frm], me).wait_recv()

        for by in range(1, per_group):
            f_copy(frm, by).start()

    @pl.loop(half, blocks)
    def _(k):
        one_block(k)

    for part in range(1, CHUNKS):
        @pl.when(jnp.logical_not(near(me)))
        def _():
            others(lambda to: x_copy(part, to).start())

    own_x = [pltpu.make_async_copy(wt_scr.at[slice_rows(me, part)], gx_scr.at[part, me], own_sem.at[2 + part])
             for part in range(CHUNKS)]
    for copy in own_x:
        copy.start()

    sends = (me < devices - 1) & (me != middle - 1)
    receives = (me > 0) & (me != middle)

    def landing(step):
        return in_ref if step >= steps - 2 else rec_scr.at[step]

    def hand_copy(step, part):
        return remote(code_scr.at[part], landing(step).at[part], hand_send.at[step, part], hand_recv.at[step, part],
                      right)

    def hand_over(step):
        @pl.when(me % 2 == step % 2)
        def _():
            for part in range(CHUNKS):
                if step >= 2:
                    @pl.when(sends)
                    def _():
                        hand_copy(step - 2, part).wait_send()

                if step >= 1:
                    @pl.when(receives)
                    def _():
                        hand_copy(step - 1, part).wait_recv()

                    got = landing(step - 1)

                    @pl.loop(0, devices)
                    def _(at):
                        factor = through_scr[at * CHUNKS + part]
                        factor = jnp.broadcast_to(factor[:, None, :],
                                                  (chunk_heads, chunk // chunk_heads, state_dim))
                        value = decode(got[part, at, :chunk], got[part, at, chunk:])
                        value = factor.reshape(chunk, state_dim) * value + local_scr[at * CHUNKS + part]
                        code_scr[part, at, :chunk], code_scr[part, at, chunk:] = encode(value)

                @pl.when(sends)
                def _():
                    hand_copy(step, part).start()

    for step in range(2):
        hand_over(step)

    docs_here = owners_ref.shape[0]

    @pl.loop(0, devices)
    def _(block):
        first_scr[block] = lax.fori_loop(
            0, docs_here + 1, lambda k, n: n + (offsets_ref[k] <= block * length).astype(jnp.int32), jnp.int32(0))

    @pl.loop(0, docs_here)
    def _(doc):
        owner = owners_ref[doc]
        rank = lax.fori_loop(
            0, docs_here, lambda k, n: n + ((owners_ref[k] == owner) & (k < doc)).astype(jnp.int32), jnp.int32(0))
        end_at = offsets_ref[doc + 1] - 1
        block = lax.fori_loop(
            1, devices, lambda k, n: n + (end_at >= k * length).astype(jnp.int32), jnp.int32(0))
        dest_scr[doc] = owner * OWNER_SLOTS + rank
        slot = jnp.clip(doc + 1 - first_scr[block], 0, END_SLOTS - 1)
        source_scr[doc] = block * END_SLOTS + slot

    @pl.loop(0, devices * OWNER_SLOTS)
    def _(at):
        pick_scr[at] = lax.fori_loop(
            0, docs_here, lambda k, n: jnp.where(dest_scr[k] == at, source_scr[k], n),
            jnp.int32(devices * END_SLOTS))

    for part in range(CHUNKS):
        slot_scr[part, devices * END_SLOTS] = jnp.zeros(slot_scr.shape[2:], jnp.int16)

    row = lax.broadcasted_iota(jnp.int32, (length, state_dim), 0)
    def mid_copy(part):
        return remote(mid_scr.at[part], in_ref.at[part, me], mid_send.at[part], mid_recv.at[part, me], middle)

    own_mid = [pltpu.make_async_copy(mid_scr.at[part], in_ref.at[part, middle], own_sem.at[2 + CHUNKS + part])
               for part in range(CHUNKS)]

    def factor_rows(part, block):
        head = part * chunk // head_dim
        factor = gd_scr[block][head:head + chunk_heads]
        return jnp.broadcast_to(factor[:, None, :],
                                (chunk_heads, chunk // chunk_heads, state_dim)).reshape(chunk, state_dim)

    def block_cuts(block):
        first = block * length
        cuts = [offsets_ref[jnp.minimum(first_scr[block] + k, docs_here)] - first for k in range(END_SLOTS)]
        last_cut = jnp.int32(0)
        for cut in cuts:
            last_cut = jnp.where(cut < length, cut, last_cut)
        return cuts, last_cut

    def state_at_middle(part):
        carry = jnp.zeros((chunk, state_dim), jnp.float32)
        for block in range(middle - 1 - relays, middle):
            cuts, last_cut = block_cuts(block)
            masked = jnp.where(row >= last_cut, gb_scr[block].astype(jnp.float32), 0.0).astype(jnp.bfloat16)
            local = jnp.dot(gx_scr[part, block], masked, preferred_element_type=jnp.float32)
            carry = local + jnp.where(cuts[0] >= length, factor_rows(part, block) * carry, 0.0)
        mid_scr[part, :chunk], mid_scr[part, chunk:] = encode(carry)

        @pl.when(me != middle)
        def _():
            mid_copy(part).start()

        @pl.when(me == middle)
        def _():
            own_mid[part].start()

    def arrived(part, other):
        @pl.when(other != me)
        def _():
            remote(wt_scr.at[pl.ds(0, chunk)], gx_scr.at[part, other], x_send.at[part, other],
                   x_recv.at[part, other], other).wait_recv()

    def states(part):
        def one(block, carry):
            b_val = gb_scr[block].astype(jnp.float32)
            cuts, last_cut = block_cuts(block)
            begin, masked = jnp.int32(0), []
            for cut in cuts:
                masked.append(jnp.where((row >= begin) & (row < cut), b_val, 0.0).astype(jnp.bfloat16))
                begin = cut
            masked.append(jnp.where(row >= last_cut, b_val, 0.0).astype(jnp.bfloat16))
            local = jnp.dot(gx_scr[part, block], jnp.concatenate(masked, 1), preferred_element_type=jnp.float32)
            kept = factor_rows(part, block) * carry
            for k in range(END_SLOTS):
                value = local[:, k * state_dim:(k + 1) * state_dim]
                coded = encode(value + kept if k == 0 else value)
                at_slot = block * END_SLOTS + k
                slot_scr[part, at_slot, :chunk], slot_scr[part, at_slot, chunk:] = coded
            carry = local[:, END_SLOTS * state_dim:] + jnp.where(cuts[0] >= length, kept, 0.0)

            return carry

        lax.fori_loop(0, devices, one, jnp.zeros((chunk, state_dim), jnp.float32))

    def out_copy(part, to):
        return remote(table_scr.at[part, to], out_ref.at[part, me], out_send.at[part, to], out_recv.at[part, me], to)

    own_out = [pltpu.make_async_copy(table_scr.at[part, me], out_ref.at[part, me], own_sem.at[2 + 2 * CHUNKS + part])
               for part in range(CHUNKS)]

    own_d.wait()

    @pl.loop(0, devices)
    def _(other):
        @pl.when(other != me)
        def _():
            remote(grow_scr.at[0], gd_scr.at[other], d_send.at[other], d_recv.at[other], other).wait_recv()

        @pl.when(other % per_group != place)
        def _():
            remote(gb_scr.at[other], gb_scr.at[other], f_send.at[0, 1], f_recv.at[other], other).wait_recv()

    for copy in own_x:
        copy.wait()

    def fill(part):
        @pl.loop(0, devices)
        def _(to):
            levels = []
            for slot in range(OWNER_SLOTS):
                source = pick_scr[to * OWNER_SLOTS + slot]
                table_scr[part, to, slot * chunk:(slot + 1) * chunk] = slot_scr[part, source, :chunk]
                levels.append(slot_scr[part, source, chunk:].astype(jnp.int32)[:SCALE_ROWS // OWNER_SLOTS])
            table_scr[part, to, OWNER_SLOTS * chunk:] = jnp.concatenate(levels, 0).astype(jnp.int16)

    def near_state():
        for part in range(CHUNKS):
            if part > 0:
                for other in range(middle - 1 - relays, middle):
                    arrived(part, other)
            state_at_middle(part)

    for part in range(CHUNKS):
        @pl.loop(0, devices)
        def _(other):
            if part == 0:
                arrived(part, other)
            else:
                @pl.when(jnp.logical_not(near(other)))
                def _():
                    arrived(part, other)

        states(part)
        fill(part)
        if part == 0:
            near_state()
        others(lambda to: out_copy(part, to).start())
        own_out[part].start()

    @pl.when(me == middle)
    def _():
        for part in range(CHUNKS):
            own_mid[part].wait()

            @pl.loop(0, devices)
            def _(other):
                @pl.when(other != me)
                def _():
                    remote(mid_scr.at[part], in_ref.at[part, other], mid_send.at[part], mid_recv.at[part, other],
                           other).wait_recv()

        for step in range(1, steps - 2, 2):
            rec_scr[step] = in_ref[...]

    for step in range(2, steps):
        hand_over(step)

    @pl.when((me % 2 != (steps - 1) % 2) & receives)
    def _():
        for part in range(CHUNKS):
            hand_copy(steps - 1, part).wait_recv()

    loads[3].wait()

    def gated_copy(group):
        cols = pl.ds(pl.multiple_of(group * (inner // groups), inner // groups), inner // groups)
        return pltpu.make_async_copy(gated_scr.at[:, cols], gated_hbm.at[:, cols], gated_sem.at[group])

    @pl.loop(0, groups)
    def _(group):
        scan_group(groups, group, skip_ref, xs_scr, gate_scr, in_ref, b_scr, c_scr, rows_ref, cols_ref, start_ref,
                   norm_ref, gated_scr, v_scr)
        gated_copy(group).start()

    @pl.when(me < devices - 1)
    def _():
        for k in range(2):
            rim_copy(k).wait_send()

    @pl.when(sends)
    def _():
        for step in range(steps - 2, steps):
            @pl.when(me % 2 == step % 2)
            def _():
                for part in range(CHUNKS):
                    hand_copy(step, part).wait_send()

    @pl.when(me != middle)
    def _():
        for part in range(CHUNKS):
            mid_copy(part).wait_send()

    for group in range(groups):
        @pl.when(quarter != group)
        def _():
            b_copy(group).wait_send()

    for frm_quarter in range(groups):
        for by in range(1, per_group):
            f_copy(frm_quarter * per_group + place, by).wait_send()

    @pl.loop(0, groups)
    def _(group):
        gated_copy(group).wait()

    for part in range(CHUNKS):
        own_out[part].wait()

    @pl.loop(0, devices)
    def _(other):
        @pl.when(other != me)
        def _():
            d_copy(other).wait_send()
            for part in range(CHUNKS):
                x_copy(part, other).wait_send()
                out_copy(part, other).wait_send()
                remote(table_scr.at[part, 0], out_ref.at[part, other], out_send.at[part, other],
                       out_recv.at[part, other], other).wait_recv()


def scan_group(groups, group, skip_ref, xs_ref, gate_ref, in_ref, b_ref, c_ref, rows_ref, cols_ref, start_ref,
               norm_ref, out_ref, v_scr):
    length, inner = xs_ref.shape
    state_dim = b_ref.shape[1] // groups
    all_heads = rows_ref.shape[0] // 2
    group_heads = all_heads // groups
    group_width = inner // groups
    blocks = group_heads // BLOCK_HEADS
    width = group_width // blocks
    head_dim = width // BLOCK_HEADS
    per_block = in_ref.shape[1] // (groups * blocks)
    chunk = in_ref.shape[2] - SCALE_ROWS
    state_cols = pl.ds(pl.multiple_of(group * state_dim, state_dim), state_dim)
    c_val = c_ref[:, state_cols]
    contract = (((1,), (1,)), ((), ()))
    scores = lax.dot_general(c_val, b_ref[:, state_cols], contract, preferred_element_type=jnp.float32)
    row = lax.broadcasted_iota(jnp.int32, (length, length), 0)
    col = lax.broadcasted_iota(jnp.int32, (length, length), 1)
    causal = (col <= row) & (col >= start_ref[:, :1])
    part = lax.broadcasted_iota(jnp.int32, (length, width), 1) // head_dim
    part_row = lax.broadcasted_iota(jnp.int32, (1, width), 1) // head_dim
    cum_rows = rows_ref[pl.ds(pl.multiple_of(group * group_heads, group_heads), group_heads), :]
    dt_rows = rows_ref[pl.ds(pl.multiple_of(all_heads + group * group_heads, group_heads), group_heads), :]
    columns = cols_ref[group]
    square = jnp.zeros((length, 1), jnp.float32)
    for block in range(blocks):
        here = pl.ds(pl.multiple_of(group * group_width + block * width, width), width)
        xs = xs_ref[:, here]
        weights, split = [], []
        cont = jnp.zeros((length, width), jnp.float32)
        skip = jnp.zeros((1, width), jnp.float32)
        for head in range(BLOCK_HEADS):
            at = block * BLOCK_HEADS + head
            gap = columns[:, at:at + 1] - cum_rows[at:at + 1]
            decay = jnp.exp(jnp.where(causal, gap, -jnp.inf))
            weights.append((scores * decay * dt_rows[at:at + 1]).astype(jnp.bfloat16))
            split.append(jnp.where(part == head, xs, jnp.zeros_like(xs)))
            cont = jnp.where(part == head, columns[:, group_heads + at:group_heads + at + 1], cont)
            skip = jnp.where(part_row == head, skip_ref[group * group_heads + at], skip)
        intra = jnp.dot(jnp.concatenate(weights, 1), jnp.concatenate(split, 0), preferred_element_type=jnp.float32)
        pieces = []
        for piece in range(per_block * CHUNKS):
            at = (group * blocks + block) * per_block + piece // CHUNKS
            pieces.append(decode(in_ref[piece % CHUNKS, at, :chunk], in_ref[piece % CHUNKS, at, chunk:]))
        state = jnp.concatenate(pieces, 0)
        high = state.astype(jnp.bfloat16)
        low = (state - high.astype(jnp.float32)).astype(jnp.bfloat16)
        inter = lax.dot_general(c_val, high, contract, preferred_element_type=jnp.float32)
        inter = inter + lax.dot_general(c_val, low, contract, preferred_element_type=jnp.float32)
        y_sum = intra + inter * cont + skip * xs.astype(jnp.float32)
        gate = gate_ref[:, here].astype(jnp.float32)
        value = y_sum * (gate / (1.0 + jnp.exp(-gate)))
        v_scr[:, block * width:(block + 1) * width] = value
        square = square + jnp.sum(value * value, axis=1, keepdims=True)
    scale = lax.rsqrt(square / group_width + 1e-05)
    whole = pl.ds(pl.multiple_of(group * group_width, group_width), group_width)
    out_ref[:, whole] = (v_scr[...] * scale * norm_ref[:, whole]).astype(jnp.bfloat16)


def deliver_kernel(code_ref, out_ref):
    sources = code_ref.shape[1]
    slots, heads, head_dim, state_dim = out_ref.shape
    chunk = (code_ref.shape[2] - SCALE_ROWS) // slots
    for source in range(sources):
        for part in range(CHUNKS):
            level = code_ref[part, source, slots * chunk:].astype(jnp.int32)
            for slot in range(slots):
                at = slot * (SCALE_ROWS // slots)
                value = decode(code_ref[part, source, slot * chunk:(slot + 1) * chunk], level[at:])
                first = (source * CHUNKS + part) * chunk
                head, row = first // head_dim, first % head_dim
                if chunk >= head_dim:
                    value = value.reshape(chunk // head_dim, head_dim, state_dim)
                    out_ref[slot, head:head + chunk // head_dim] = value
                else:
                    out_ref[slot, head, row:row + chunk] = value


def per_device(
    ssm_input,
    gate_input,
    bc_input,
    dt_raw,
    offsets,
    owners,
    conv_weight,
    convolution_bias,
    a_log,
    dt_bias,
    d_skip,
    norm_weight,
):
    length, inner_dim = ssm_input.shape
    heads = a_log.shape[0]
    head_dim = inner_dim // heads
    groups = heads // GROUP_HEADS
    state_dim = bc_input.shape[1] // (2 * groups)
    devices = lax.axis_size("ctx")
    relays = devices // 8 - 1
    blocks = heads // BLOCK_HEADS
    width = BLOCK_HEADS * head_dim
    group_state = groups * state_dim
    group_width = inner_dim // groups
    device_width = inner_dim // devices
    device_heads = heads // devices
    slice_rows = -(-device_heads // 8) * 8

    vmem = pl.BlockSpec(memory_space=pltpu.VMEM)
    smem = pl.BlockSpec(memory_space=pltpu.SMEM)
    anywhere = pl.BlockSpec(memory_space=pl.ANY)
    dma = pltpu.SemaphoreType.DMA
    per_group = devices // groups
    steps = relays + 2
    docs = owners.shape[0]
    chunk = device_width // CHUNKS
    chunk_heads = max(chunk // head_dim, 1)
    table_rows = OWNER_SLOTS * chunk + SCALE_ROWS
    code = lambda *lead: pltpu.VMEM(lead + (chunk + SCALE_ROWS, state_dim), jnp.int16)
    half = lambda *shape: pltpu.VMEM(shape, jnp.bfloat16)
    full = lambda *shape: pltpu.VMEM(shape, jnp.float32)
    delivered, gated_out = pl.pallas_call(
        functools.partial(whole_kernel, devices, groups, relays),
        in_specs=[smem] * 3 + [vmem] * 5 + [anywhere] * 4,
        out_specs=[anywhere] * 2,
        out_shape=[
            jax.ShapeDtypeStruct((CHUNKS, devices, table_rows, state_dim), jnp.int16),
            jax.ShapeDtypeStruct((length, inner_dim), jnp.bfloat16),
        ],
        scratch_shapes=[
            half(length, inner_dim),
            half(length, 2 * group_state),
            full(KERNEL_WIDTH, inner_dim + 2 * group_state),
            half(RIM, inner_dim),
            half(RIM, 2 * group_state),
            half(length, inner_dim),
            half(length, group_state),
            half(length, group_state),
            half(inner_dim, length),
            half(groups, length, state_dim),
            full(devices * CHUNKS, chunk, state_dim),
            code(CHUNKS, devices),
            code(max(relays, 1), CHUNKS, devices),
            code(CHUNKS, devices),
            half(groups, length, state_dim),
            full(KERNEL_WIDTH - 1, length, state_dim),
            full(blocks, BLOCK_HEADS, length),
            full(devices, slice_rows, state_dim),
            full(devices * CHUNKS, chunk_heads, state_dim),
            full(2 * heads, length),
            full(groups, length, 2 * GROUP_HEADS),
            pltpu.VMEM((length, state_dim), jnp.int32),
            half(CHUNKS, devices, chunk, length),
            half(devices, length, state_dim),
            full(devices, slice_rows, state_dim),
            code(CHUNKS, devices * END_SLOTS + 1),
            pltpu.VMEM((CHUNKS, devices, table_rows, state_dim), jnp.int16),
            code(CHUNKS),
            half(length, inner_dim),
            half(length, inner_dim),
            full(length, group_width),
            pltpu.SMEM((devices,), jnp.int32),
            pltpu.SMEM((docs,), jnp.int32),
            pltpu.SMEM((docs,), jnp.int32),
            pltpu.SMEM((devices * OWNER_SLOTS,), jnp.int32),
            dma((2,)), dma((2,)),
            dma((CHUNKS, devices)), dma((CHUNKS, devices)),
            dma((groups,)), dma((devices,)),
            dma((groups, per_group)), dma((devices,)),
            dma((devices,)), dma((devices,)),
            dma((steps, CHUNKS)), dma((steps, CHUNKS)),
            dma((CHUNKS,)), dma((CHUNKS, devices)),
            dma((CHUNKS, devices)), dma((CHUNKS, devices)),
            dma((2 + 3 * CHUNKS,)), dma((4,)), dma((groups,)),
        ],
        compiler_params=pltpu.CompilerParams(
            collective_id=0, has_side_effects=True, vmem_limit_bytes=VMEM_LIMIT),
        name="layer",
    )(offsets, owners, d_skip, dt_raw.T, convolution_bias[None, :], a_log[None, :], dt_bias[None, :],
      norm_weight[None, :], ssm_input, bc_input, conv_weight, gate_input)

    sources = devices // 4
    decode_states = pl.pallas_call(
        deliver_kernel,
        grid=(4,),
        in_specs=[pl.BlockSpec((CHUNKS, sources, table_rows, state_dim), lambda j: (0, j, 0, 0))],
        out_specs=pl.BlockSpec((OWNER_SLOTS, heads // 4, head_dim, state_dim), lambda j: (0, j, 0, 0)),
        out_shape=jax.ShapeDtypeStruct((OWNER_SLOTS, heads, head_dim, state_dim), jnp.float32),
        name="deliver",
    )(delivered)
    return (gated_out, decode_states)


def solution(mesh):
    in_specs = (
        P(("groups", "ctx"), None),
        P(("groups", "ctx"), None),
        P(("groups", "ctx"), None),
        P(("groups", "ctx"), None),
        P("groups"),
        P("groups"),
        P(),
        P(),
        P(),
        P(),
        P(),
        P(),
    )
    out_specs = (P(("groups", "ctx"), None), P(("groups", "ctx"), None, None, None))
    return jax.shard_map(
        per_device, mesh=mesh, in_specs=in_specs, out_specs=out_specs, check_vma=False
    )
```

```python
import functools
import math
import jax
import jax.numpy as jnp
from jax import lax
from jax.experimental import pallas as pl
from jax.experimental.pallas import tpu as pltpu
from jax.sharding import PartitionSpec as P

GROUP_HEADS = 16
KERNEL_WIDTH = 4
OWNER_SLOTS = 2
BLOCK_HEADS = 4
RIM = 16
SCALE_ROWS = 16
LEVELS = 8.0
CODE_MAX = 32767.0
END_SLOTS = 4
CHUNKS = 2
VMEM_LIMIT = 56 * 1024 * 1024
MESH = pl.DeviceIdType.MESH


def encode(value):
    rows, lanes = value.shape
    parts = value.reshape(rows // SCALE_ROWS, SCALE_ROWS, lanes)
    top = jnp.max(jnp.abs(parts), axis=1)
    level = jnp.ceil(jnp.log(jnp.maximum(top, 1e-30)) * (LEVELS / math.log(2.0)))
    unit = jnp.exp2(level * (-1.0 / LEVELS)) * CODE_MAX
    coded = jnp.clip(jnp.round(parts * unit[:, None, :]), -CODE_MAX, CODE_MAX).reshape(rows, lanes)
    if level.shape[0] < SCALE_ROWS:
        level = jnp.concatenate([level, jnp.zeros((SCALE_ROWS - level.shape[0], lanes), jnp.float32)], 0)
    return coded.astype(jnp.int32).astype(jnp.int16), level.astype(jnp.int32).astype(jnp.int16)


def decode(coded, level):
    rows, lanes = coded.shape
    unit = jnp.exp2(level.astype(jnp.int32).astype(jnp.float32) * (1.0 / LEVELS)) * (1.0 / CODE_MAX)
    unit = unit[:rows // SCALE_ROWS]
    parts = coded.astype(jnp.int32).astype(jnp.float32).reshape(rows // SCALE_ROWS, SCALE_ROWS, lanes)
    return (parts * unit[:, None, :]).reshape(rows, lanes)


def conv_silu(x, rim, mask_ref, weight, bias):
    x = x.astype(jnp.float32)
    padded = jnp.concatenate([rim.astype(jnp.float32), x], 0)
    total = bias
    for tap in range(KERNEL_WIDTH - 1):
        mask = jnp.concatenate([mask_ref[tap]] * (x.shape[1] // mask_ref.shape[2]), 1)
        total = total + weight[tap:tap + 1] * (mask * pltpu.roll(padded, KERNEL_WIDTH - 1 - tap, 0)[RIM:])
    total = total + weight[KERNEL_WIDTH - 1:KERNEL_WIDTH] * x
    return (total / (1.0 + jnp.exp(-total))).astype(jnp.bfloat16)


def spread(k, count):
    half = (k + 1) // 2
    return count // 2 + half * (1 - 2 * (k % 2))


def enter(axis, me, devices):
    barrier = pltpu.get_barrier_semaphore()

    @pl.loop(1, devices)
    def _(by):
        pl.semaphore_signal(barrier, inc=1, device_id={axis: (me + by) % devices}, device_id_type=MESH)

    return barrier


def exact_dot(a, b):
    return jnp.dot(a, b, precision=lax.Precision.HIGHEST, preferred_element_type=jnp.float32)


def whole_kernel(devices, groups, relays, offsets_ref, owners_ref, skip_ref, dt_ref, bias_ref, a_ref, dt_bias_ref,
                 norm_ref, x_hbm, bc_hbm, taps_hbm, gate_hbm, out_ref, gated_hbm,
                 x_ref, bc_ref, taps_ref, rimx_scr, rimbc_scr, xs_scr, b_scr, c_scr, wt_scr, blast_scr, local_scr, code_scr, rec_scr, in_ref,
                 bsend_scr, mask_scr, end_scr, grow_scr, through_scr, rows_ref, cols_ref, start_ref, gx_scr, gb_scr,
                 gd_scr, slot_scr, table_scr, mid_scr, gate_scr, gated_scr, v_scr, first_scr, dest_scr, source_scr,
                 pick_scr,
                 rim_send, rim_recv, x_send, x_recv, b_send, b_recv, f_send, f_recv, d_send, d_recv, hand_send,
                 hand_recv, mid_send, mid_recv, out_send, out_recv, own_sem, load_sem, gated_sem):
    me = lax.axis_index("ctx")
    length, inner = x_ref.shape
    blocks = end_scr.shape[0]
    width = inner // blocks
    state_dim = blast_scr.shape[2]
    all_heads = dt_ref.shape[0]
    head_dim = inner // all_heads
    per_block = devices // blocks
    slice_width = width // per_block
    slice_heads = all_heads // devices
    chunk = slice_width // CHUNKS
    chunk_heads = max(chunk // head_dim, 1)
    per_group = devices // groups
    blocks_per_group = blocks // groups
    group_heads = all_heads // groups
    quarter = me // per_group
    place = me % per_group
    steps = relays + 2
    middle = devices // 2

    def remote(src, dst, send, recv, to):
        return pltpu.make_async_remote_copy(src_ref=src, dst_ref=dst, send_sem=send, recv_sem=recv,
                                            device_id={"ctx": to}, device_id_type=MESH)

    barrier = enter("ctx", me, devices)
    loads = [pltpu.make_async_copy(src, dst, load_sem.at[k]) for k, (src, dst) in enumerate(
        ((bc_hbm, bc_ref), (taps_hbm, taps_ref), (x_hbm, x_ref), (gate_hbm, gate_scr)))]
    for load in loads:
        load.start()

    @pl.when(me == 0)
    def _():
        rimx_scr[...] = jnp.zeros_like(rimx_scr)
        rimbc_scr[...] = jnp.zeros_like(rimbc_scr)
        in_ref[...] = jnp.zeros_like(in_ref)
        rec_scr[...] = jnp.zeros_like(rec_scr)

    base = me * length
    docs = offsets_ref.shape[0] - 1
    token = lax.broadcasted_iota(jnp.int32, (length, state_dim), 0)
    along = lax.broadcasted_iota(jnp.int32, (8, length), 1)

    def bounds(k, carry):
        start, end = carry
        offset = offsets_ref[k] - base
        start = jnp.where(offset <= token, jnp.maximum(start, offset), start)
        end = jnp.where(offset > along, jnp.minimum(end, offset), end)
        return start, end

    start, end = lax.fori_loop(0, docs + 1, bounds, (jnp.full((length, state_dim), -base, jnp.int32),
                                                     jnp.full((8, length), length, jnp.int32)))
    end = end - 1
    start_ref[...] = start
    for tap in range(KERNEL_WIDTH - 1):
        mask_scr[tap] = jnp.where(token + (tap - KERNEL_WIDTH + 1) >= start, 1.0, 0.0).astype(jnp.float32)
    last_start = jnp.max(start, axis=0, keepdims=True)
    last = token >= last_start

    pair = jnp.concatenate([dt_bias_ref[...], a_ref[...]], 1)
    pair = jnp.broadcast_to(pair, (8, 2 * all_heads)).T
    pre = dt_ref[...] + pair[:all_heads, :1]
    dt_rows = jnp.maximum(pre, 0.0) + jnp.log1p(jnp.exp(-jnp.abs(pre)))
    logdec = -dt_rows * jnp.exp(pair[all_heads:, :1])
    one = lax.broadcasted_iota(jnp.int32, (length, length), 0)
    two = lax.broadcasted_iota(jnp.int32, (length, length), 1)
    cum_rows = exact_dot(logdec, jnp.where(one <= two, 1.0, 0.0).astype(jnp.float32))
    cum_end = exact_dot(cum_rows, jnp.where(one == end[:1], 1.0, 0.0).astype(jnp.float32))
    grow = jnp.exp(cum_rows)
    rows_ref[:all_heads] = cum_rows
    rows_ref[all_heads:] = dt_rows
    weight = jnp.exp(cum_end - cum_rows) * dt_rows
    for block in range(blocks):
        end_scr[block] = weight[block * BLOCK_HEADS:(block + 1) * BLOCK_HEADS]
    first_end = jnp.min(end, axis=1, keepdims=True)[:1]
    grow_first = jnp.sum(jnp.where(lax.broadcasted_iota(jnp.int32, grow.shape, 1) == first_end, grow, 0.0), axis=1,
                         keepdims=True)
    carried = jnp.where(start[:1] < 0, jnp.broadcast_to(grow_first, (all_heads, state_dim)), 0.0)
    for device in range(devices):
        grow_scr[device, :slice_heads] = carried[device * slice_heads:(device + 1) * slice_heads]
    grow_last = jnp.sum(jnp.where(lax.broadcasted_iota(jnp.int32, grow.shape, 1) == length - 1, grow, 0.0), axis=1,
                        keepdims=True)
    through = jnp.where(last_start < 0, jnp.broadcast_to(grow_last, (all_heads, state_dim)), 0.0)
    for part in range(devices * CHUNKS):
        at = part * chunk // head_dim
        through_scr[part] = through[at:at + chunk_heads]
    upright = jnp.concatenate([cum_rows, grow], 0).T
    begun = start[:, :group_heads] < 0
    for group in range(groups):
        at = group * group_heads
        cols_ref[group, :, :group_heads] = upright[:, at:at + group_heads]
        cols_ref[group, :, group_heads:] = jnp.where(begun, upright[:, all_heads + at:all_heads + at + group_heads], 0.0)

    pl.semaphore_wait(barrier, devices - 1)

    right = (me + 1) % devices

    def rim_copy(k):
        src, dst = ((bc_hbm, rimbc_scr), (x_hbm, rimx_scr))[k]
        return remote(src.at[pl.ds(length - RIM, RIM)], dst, rim_send.at[k], rim_recv.at[k], right)

    @pl.when(me < devices - 1)
    def _():
        for k in range(2):
            rim_copy(k).start()

    def others(act):
        @pl.loop(0, devices)
        def _(k):
            to = (me + spread(k, devices)) % devices

            @pl.when(to != me)
            def _():
                act(to)

    def d_copy(to):
        return remote(grow_scr.at[to], gd_scr.at[me], d_send.at[to], d_recv.at[me], to)

    others(lambda to: d_copy(to).start())
    own_d = pltpu.make_async_copy(grow_scr.at[me], gd_scr.at[me], own_sem.at[0])
    own_d.start()

    loads[0].wait()
    loads[1].wait()

    @pl.when(me > 0)
    def _():
        rim_copy(0).wait_recv()

    def narrow(part):
        cols = slice(part * state_dim, (part + 1) * state_dim)
        after = slice(inner + part * state_dim, inner + (part + 1) * state_dim)
        return conv_silu(bc_ref[:, cols], rimbc_scr[:, cols], mask_scr, taps_ref[:, after], bias_ref[:, after])

    for part in range(groups):
        value = narrow(part)
        b_scr[:, part * state_dim:(part + 1) * state_dim] = value
        bsend_scr[part] = value
        blast_scr[part] = jnp.where(last, value, jnp.zeros_like(value))

    def b_copy(group):
        return remote(bsend_scr.at[group], gb_scr.at[me], b_send.at[group], b_recv.at[me],
                      group * per_group + place)

    own_b = pltpu.make_async_copy(bsend_scr.at[quarter], gb_scr.at[me], own_sem.at[1])
    own_b.start()
    for group in range(groups):
        @pl.when(quarter != group)
        def _():
            b_copy(group).start()

    def slice_rows(to, part):
        return pl.ds(pl.multiple_of(to * slice_width + part * chunk, chunk), chunk)

    def x_copy(part, to):
        return remote(wt_scr.at[slice_rows(to, part)], gx_scr.at[part, me], x_send.at[part, to], x_recv.at[part, me],
                      to)

    def near(device):
        return (device >= middle - 1 - relays) & (device < middle)

    def one_block(k):
        block = (me // per_block + spread(k, blocks)) % blocks
        cols = pl.ds(pl.multiple_of(block * width, width), width)
        xs = conv_silu(x_ref[:, cols], rimx_scr[:, cols], mask_scr, taps_ref[:, cols], bias_ref[:, cols])
        xs_scr[:, cols] = xs
        x_t = xs.astype(jnp.float32).T.reshape(BLOCK_HEADS, head_dim, length)
        weighted = (x_t * end_scr[block][:, None, :]).astype(jnp.bfloat16).reshape(width, length)
        wt_scr[cols, :] = weighted

        @pl.loop(0, per_block)
        def _(part):
            to = block * per_block + part

            @pl.when(to != me)
            def _():
                x_copy(0, to).start()

                @pl.when(near(me))
                def _():
                    for later in range(1, CHUNKS):
                        x_copy(later, to).start()

        local = jnp.dot(weighted, blast_scr[block // blocks_per_group], preferred_element_type=jnp.float32)
        for part in range(per_block * CHUNKS):
            local_scr[block * per_block * CHUNKS + part] = local[part * chunk:(part + 1) * chunk]

        @pl.when(me % 2 == 0)
        def _():
            for part in range(per_block * CHUNKS):
                at = block * per_block + part // CHUNKS
                coded = encode(local[part * chunk:(part + 1) * chunk])
                code_scr[part % CHUNKS, at, :chunk], code_scr[part % CHUNKS, at, chunk:] = coded

    loads[2].wait()

    @pl.when(me > 0)
    def _():
        rim_copy(1).wait_recv()

    half = blocks // 2

    @pl.loop(0, half)
    def _(k):
        one_block(k)

    def f_copy(frm, by):
        to = quarter * per_group + (place + by) % per_group
        return remote(gb_scr.at[frm], gb_scr.at[frm], f_send.at[frm // per_group, by], f_recv.at[frm], to)

    own_b.wait()
    for frm_quarter in range(groups):
        frm = frm_quarter * per_group + place

        @pl.when(quarter != frm_quarter)
        def _():
            remote(bsend_scr.at[0], gb_scr.at[frm], b_send.at[0], b_recv.at[frm], me).wait_recv()

        for by in range(1, per_group):
            f_copy(frm, by).start()

    @pl.loop(half, blocks)
    def _(k):
        one_block(k)

    for part in range(1, CHUNKS):
        @pl.when(jnp.logical_not(near(me)))
        def _():
            others(lambda to: x_copy(part, to).start())

    for part in range(groups):
        c_scr[:, part * state_dim:(part + 1) * state_dim] = narrow(groups + part)

    own_x = [pltpu.make_async_copy(wt_scr.at[slice_rows(me, part)], gx_scr.at[part, me], own_sem.at[2 + part])
             for part in range(CHUNKS)]
    for copy in own_x:
        copy.start()

    sends = (me < devices - 1) & (me != middle - 1)
    receives = (me > 0) & (me != middle)

    def landing(step):
        return in_ref if step >= steps - 2 else rec_scr.at[step]

    def hand_copy(step, part):
        return remote(code_scr.at[part], landing(step).at[part], hand_send.at[step, part], hand_recv.at[step, part],
                      right)

    def hand_over(step):
        @pl.when(me % 2 == step % 2)
        def _():
            for part in range(CHUNKS):
                if step >= 2:
                    @pl.when(sends)
                    def _():
                        hand_copy(step - 2, part).wait_send()

                if step >= 1:
                    @pl.when(receives)
                    def _():
                        hand_copy(step - 1, part).wait_recv()

                    got = landing(step - 1)

                    @pl.loop(0, devices)
                    def _(at):
                        factor = through_scr[at * CHUNKS + part]
                        factor = jnp.broadcast_to(factor[:, None, :],
                                                  (chunk_heads, chunk // chunk_heads, state_dim))
                        value = decode(got[part, at, :chunk], got[part, at, chunk:])
                        value = factor.reshape(chunk, state_dim) * value + local_scr[at * CHUNKS + part]
                        code_scr[part, at, :chunk], code_scr[part, at, chunk:] = encode(value)

                @pl.when(sends)
                def _():
                    hand_copy(step, part).start()

    for step in range(2):
        hand_over(step)

    docs_here = owners_ref.shape[0]

    @pl.loop(0, devices)
    def _(block):
        first_scr[block] = lax.fori_loop(
            0, docs_here + 1, lambda k, n: n + (offsets_ref[k] <= block * length).astype(jnp.int32), jnp.int32(0))

    @pl.loop(0, docs_here)
    def _(doc):
        owner = owners_ref[doc]
        rank = lax.fori_loop(
            0, docs_here, lambda k, n: n + ((owners_ref[k] == owner) & (k < doc)).astype(jnp.int32), jnp.int32(0))
        end_at = offsets_ref[doc + 1] - 1
        block = lax.fori_loop(
            1, devices, lambda k, n: n + (end_at >= k * length).astype(jnp.int32), jnp.int32(0))
        dest_scr[doc] = owner * OWNER_SLOTS + rank
        slot = jnp.clip(doc + 1 - first_scr[block], 0, END_SLOTS - 1)
        source_scr[doc] = block * END_SLOTS + slot

    @pl.loop(0, devices * OWNER_SLOTS)
    def _(at):
        pick_scr[at] = lax.fori_loop(
            0, docs_here, lambda k, n: jnp.where(dest_scr[k] == at, source_scr[k], n),
            jnp.int32(devices * END_SLOTS))

    for part in range(CHUNKS):
        slot_scr[part, devices * END_SLOTS] = jnp.zeros(slot_scr.shape[2:], jnp.int16)

    row = lax.broadcasted_iota(jnp.int32, (length, state_dim), 0)
    def mid_copy(part):
        return remote(mid_scr.at[part], in_ref.at[part, me], mid_send.at[part], mid_recv.at[part, me], middle)

    own_mid = [pltpu.make_async_copy(mid_scr.at[part], in_ref.at[part, middle], own_sem.at[2 + CHUNKS + part])
               for part in range(CHUNKS)]

    def factor_rows(part, block):
        head = part * chunk // head_dim
        factor = gd_scr[block][head:head + chunk_heads]
        return jnp.broadcast_to(factor[:, None, :],
                                (chunk_heads, chunk // chunk_heads, state_dim)).reshape(chunk, state_dim)

    def block_cuts(block):
        first = block * length
        cuts = [offsets_ref[jnp.minimum(first_scr[block] + k, docs_here)] - first for k in range(END_SLOTS)]
        last_cut = jnp.int32(0)
        for cut in cuts:
            last_cut = jnp.where(cut < length, cut, last_cut)
        return cuts, last_cut

    def state_at_middle(part):
        carry = jnp.zeros((chunk, state_dim), jnp.float32)
        for block in range(middle - 1 - relays, middle):
            cuts, last_cut = block_cuts(block)
            masked = jnp.where(row >= last_cut, gb_scr[block].astype(jnp.float32), 0.0).astype(jnp.bfloat16)
            local = jnp.dot(gx_scr[part, block], masked, preferred_element_type=jnp.float32)
            carry = local + jnp.where(cuts[0] >= length, factor_rows(part, block) * carry, 0.0)
        mid_scr[part, :chunk], mid_scr[part, chunk:] = encode(carry)

        @pl.when(me != middle)
        def _():
            mid_copy(part).start()

        @pl.when(me == middle)
        def _():
            own_mid[part].start()

    def arrived(part, other):
        @pl.when(other != me)
        def _():
            remote(wt_scr.at[pl.ds(0, chunk)], gx_scr.at[part, other], x_send.at[part, other],
                   x_recv.at[part, other], other).wait_recv()

    def states(part):
        def one(block, carry):
            b_val = gb_scr[block].astype(jnp.float32)
            cuts, last_cut = block_cuts(block)
            begin, masked = jnp.int32(0), []
            for cut in cuts:
                masked.append(jnp.where((row >= begin) & (row < cut), b_val, 0.0).astype(jnp.bfloat16))
                begin = cut
            masked.append(jnp.where(row >= last_cut, b_val, 0.0).astype(jnp.bfloat16))
            local = jnp.dot(gx_scr[part, block], jnp.concatenate(masked, 1), preferred_element_type=jnp.float32)
            kept = factor_rows(part, block) * carry
            for k in range(END_SLOTS):
                value = local[:, k * state_dim:(k + 1) * state_dim]
                coded = encode(value + kept if k == 0 else value)
                at_slot = block * END_SLOTS + k
                slot_scr[part, at_slot, :chunk], slot_scr[part, at_slot, chunk:] = coded
            carry = local[:, END_SLOTS * state_dim:] + jnp.where(cuts[0] >= length, kept, 0.0)

            return carry

        lax.fori_loop(0, devices, one, jnp.zeros((chunk, state_dim), jnp.float32))

    def out_copy(part, to):
        return remote(table_scr.at[part, to], out_ref.at[part, me], out_send.at[part, to], out_recv.at[part, me], to)

    own_out = [pltpu.make_async_copy(table_scr.at[part, me], out_ref.at[part, me], own_sem.at[2 + 2 * CHUNKS + part])
               for part in range(CHUNKS)]

    own_d.wait()

    @pl.loop(0, devices)
    def _(other):
        @pl.when(other != me)
        def _():
            remote(grow_scr.at[0], gd_scr.at[other], d_send.at[other], d_recv.at[other], other).wait_recv()

        @pl.when(other % per_group != place)
        def _():
            remote(gb_scr.at[other], gb_scr.at[other], f_send.at[0, 1], f_recv.at[other], other).wait_recv()

    for copy in own_x:
        copy.wait()

    def fill(part):
        @pl.loop(0, devices)
        def _(to):
            levels = []
            for slot in range(OWNER_SLOTS):
                source = pick_scr[to * OWNER_SLOTS + slot]
                table_scr[part, to, slot * chunk:(slot + 1) * chunk] = slot_scr[part, source, :chunk]
                levels.append(slot_scr[part, source, chunk:].astype(jnp.int32)[:SCALE_ROWS // OWNER_SLOTS])
            table_scr[part, to, OWNER_SLOTS * chunk:] = jnp.concatenate(levels, 0).astype(jnp.int16)

    def near_state():
        for part in range(CHUNKS):
            if part > 0:
                for other in range(middle - 1 - relays, middle):
                    arrived(part, other)
            state_at_middle(part)

    for part in range(CHUNKS):
        @pl.loop(0, devices)
        def _(other):
            if part == 0:
                arrived(part, other)
            else:
                @pl.when(jnp.logical_not(near(other)))
                def _():
                    arrived(part, other)

        states(part)
        fill(part)
        if part == 0:
            near_state()
        others(lambda to: out_copy(part, to).start())
        own_out[part].start()

    @pl.when(me == middle)
    def _():
        for part in range(CHUNKS):
            own_mid[part].wait()

            @pl.loop(0, devices)
            def _(other):
                @pl.when(other != me)
                def _():
                    remote(mid_scr.at[part], in_ref.at[part, other], mid_send.at[part], mid_recv.at[part, other],
                           other).wait_recv()

        for step in range(1, steps - 2, 2):
            rec_scr[step] = in_ref[...]

    for step in range(2, steps):
        hand_over(step)

    @pl.when((me % 2 != (steps - 1) % 2) & receives)
    def _():
        for part in range(CHUNKS):
            hand_copy(steps - 1, part).wait_recv()

    loads[3].wait()

    def gated_copy(group):
        cols = pl.ds(pl.multiple_of(group * (inner // groups), inner // groups), inner // groups)
        return pltpu.make_async_copy(gated_scr.at[:, cols], gated_hbm.at[:, cols], gated_sem.at[group])

    @pl.loop(0, groups)
    def _(group):
        scan_group(groups, group, skip_ref, xs_scr, gate_scr, in_ref, b_scr, c_scr, rows_ref, cols_ref, start_ref,
                   norm_ref, gated_scr, v_scr)
        gated_copy(group).start()

    @pl.when(me < devices - 1)
    def _():
        for k in range(2):
            rim_copy(k).wait_send()

    @pl.when(sends)
    def _():
        for step in range(steps - 2, steps):
            @pl.when(me % 2 == step % 2)
            def _():
                for part in range(CHUNKS):
                    hand_copy(step, part).wait_send()

    @pl.when(me != middle)
    def _():
        for part in range(CHUNKS):
            mid_copy(part).wait_send()

    for group in range(groups):
        @pl.when(quarter != group)
        def _():
            b_copy(group).wait_send()

    for frm_quarter in range(groups):
        for by in range(1, per_group):
            f_copy(frm_quarter * per_group + place, by).wait_send()

    @pl.loop(0, groups)
    def _(group):
        gated_copy(group).wait()

    for part in range(CHUNKS):
        own_out[part].wait()

    @pl.loop(0, devices)
    def _(other):
        @pl.when(other != me)
        def _():
            d_copy(other).wait_send()
            for part in range(CHUNKS):
                x_copy(part, other).wait_send()
                out_copy(part, other).wait_send()
                remote(table_scr.at[part, 0], out_ref.at[part, other], out_send.at[part, other],
                       out_recv.at[part, other], other).wait_recv()


def scan_group(groups, group, skip_ref, xs_ref, gate_ref, in_ref, b_ref, c_ref, rows_ref, cols_ref, start_ref,
               norm_ref, out_ref, v_scr):
    length, inner = xs_ref.shape
    state_dim = b_ref.shape[1] // groups
    all_heads = rows_ref.shape[0] // 2
    group_heads = all_heads // groups
    group_width = inner // groups
    blocks = group_heads // BLOCK_HEADS
    width = group_width // blocks
    head_dim = width // BLOCK_HEADS
    per_block = in_ref.shape[1] // (groups * blocks)
    chunk = in_ref.shape[2] - SCALE_ROWS
    state_cols = pl.ds(pl.multiple_of(group * state_dim, state_dim), state_dim)
    c_val = c_ref[:, state_cols]
    contract = (((1,), (1,)), ((), ()))
    scores = lax.dot_general(c_val, b_ref[:, state_cols], contract, preferred_element_type=jnp.float32)
    row = lax.broadcasted_iota(jnp.int32, (length, length), 0)
    col = lax.broadcasted_iota(jnp.int32, (length, length), 1)
    causal = (col <= row) & (col >= start_ref[:, :1])
    part = lax.broadcasted_iota(jnp.int32, (length, width), 1) // head_dim
    part_row = lax.broadcasted_iota(jnp.int32, (1, width), 1) // head_dim
    cum_rows = rows_ref[pl.ds(pl.multiple_of(group * group_heads, group_heads), group_heads), :]
    dt_rows = rows_ref[pl.ds(pl.multiple_of(all_heads + group * group_heads, group_heads), group_heads), :]
    columns = cols_ref[group]
    square = jnp.zeros((length, 1), jnp.float32)
    for block in range(blocks):
        here = pl.ds(pl.multiple_of(group * group_width + block * width, width), width)
        xs = xs_ref[:, here]
        weights, split = [], []
        cont = jnp.zeros((length, width), jnp.float32)
        skip = jnp.zeros((1, width), jnp.float32)
        for head in range(BLOCK_HEADS):
            at = block * BLOCK_HEADS + head
            gap = columns[:, at:at + 1] - cum_rows[at:at + 1]
            decay = jnp.exp(jnp.where(causal, gap, -jnp.inf))
            weights.append((scores * decay * dt_rows[at:at + 1]).astype(jnp.bfloat16))
            split.append(jnp.where(part == head, xs, jnp.zeros_like(xs)))
            cont = jnp.where(part == head, columns[:, group_heads + at:group_heads + at + 1], cont)
            skip = jnp.where(part_row == head, skip_ref[group * group_heads + at], skip)
        intra = jnp.dot(jnp.concatenate(weights, 1), jnp.concatenate(split, 0), preferred_element_type=jnp.float32)
        pieces = []
        for piece in range(per_block * CHUNKS):
            at = (group * blocks + block) * per_block + piece // CHUNKS
            pieces.append(decode(in_ref[piece % CHUNKS, at, :chunk], in_ref[piece % CHUNKS, at, chunk:]))
        state = jnp.concatenate(pieces, 0)
        high = state.astype(jnp.bfloat16)
        low = (state - high.astype(jnp.float32)).astype(jnp.bfloat16)
        inter = lax.dot_general(c_val, high, contract, preferred_element_type=jnp.float32)
        inter = inter + lax.dot_general(c_val, low, contract, preferred_element_type=jnp.float32)
        y_sum = intra + inter * cont + skip * xs.astype(jnp.float32)
        gate = gate_ref[:, here].astype(jnp.float32)
        value = y_sum * (gate / (1.0 + jnp.exp(-gate)))
        v_scr[:, block * width:(block + 1) * width] = value
        square = square + jnp.sum(value * value, axis=1, keepdims=True)
    scale = lax.rsqrt(square / group_width + 1e-05)
    whole = pl.ds(pl.multiple_of(group * group_width, group_width), group_width)
    out_ref[:, whole] = (v_scr[...] * scale * norm_ref[:, whole]).astype(jnp.bfloat16)


def deliver_kernel(code_ref, gated_ref, out_ref, final_ref):
    final_ref[...] = gated_ref[...]
    sources = code_ref.shape[1]
    slots, heads, head_dim, state_dim = out_ref.shape
    chunk = (code_ref.shape[2] - SCALE_ROWS) // slots
    for source in range(sources):
        for part in range(CHUNKS):
            level = code_ref[part, source, slots * chunk:].astype(jnp.int32)
            for slot in range(slots):
                at = slot * (SCALE_ROWS // slots)
                value = decode(code_ref[part, source, slot * chunk:(slot + 1) * chunk], level[at:])
                first = (source * CHUNKS + part) * chunk
                head, row = first // head_dim, first % head_dim
                if chunk >= head_dim:
                    value = value.reshape(chunk // head_dim, head_dim, state_dim)
                    out_ref[slot, head:head + chunk // head_dim] = value
                else:
                    out_ref[slot, head, row:row + chunk] = value


def per_device(
    ssm_input,
    gate_input,
    bc_input,
    dt_raw,
    offsets,
    owners,
    conv_weight,
    convolution_bias,
    a_log,
    dt_bias,
    d_skip,
    norm_weight,
):
    length, inner_dim = ssm_input.shape
    heads = a_log.shape[0]
    head_dim = inner_dim // heads
    groups = heads // GROUP_HEADS
    state_dim = bc_input.shape[1] // (2 * groups)
    devices = lax.axis_size("ctx")
    relays = devices // 8 - 1
    blocks = heads // BLOCK_HEADS
    width = BLOCK_HEADS * head_dim
    group_state = groups * state_dim
    group_width = inner_dim // groups
    device_width = inner_dim // devices
    device_heads = heads // devices
    slice_rows = -(-device_heads // 8) * 8

    vmem = pl.BlockSpec(memory_space=pltpu.VMEM)
    smem = pl.BlockSpec(memory_space=pltpu.SMEM)
    anywhere = pl.BlockSpec(memory_space=pl.ANY)
    dma = pltpu.SemaphoreType.DMA
    per_group = devices // groups
    steps = relays + 2
    docs = owners.shape[0]
    chunk = device_width // CHUNKS
    chunk_heads = max(chunk // head_dim, 1)
    table_rows = OWNER_SLOTS * chunk + SCALE_ROWS
    code = lambda *lead: pltpu.VMEM(lead + (chunk + SCALE_ROWS, state_dim), jnp.int16)
    half = lambda *shape: pltpu.VMEM(shape, jnp.bfloat16)
    full = lambda *shape: pltpu.VMEM(shape, jnp.float32)
    delivered, gated_out = pl.pallas_call(
        functools.partial(whole_kernel, devices, groups, relays),
        in_specs=[smem] * 3 + [vmem] * 5 + [anywhere] * 4,
        out_specs=[anywhere] * 2,
        out_shape=[
            jax.ShapeDtypeStruct((CHUNKS, devices, table_rows, state_dim), jnp.int16),
            jax.ShapeDtypeStruct((length, inner_dim), jnp.bfloat16),
        ],
        scratch_shapes=[
            half(length, inner_dim),
            half(length, 2 * group_state),
            full(KERNEL_WIDTH, inner_dim + 2 * group_state),
            half(RIM, inner_dim),
            half(RIM, 2 * group_state),
            half(length, inner_dim),
            half(length, group_state),
            half(length, group_state),
            half(inner_dim, length),
            half(groups, length, state_dim),
            full(devices * CHUNKS, chunk, state_dim),
            code(CHUNKS, devices),
            code(max(relays, 1), CHUNKS, devices),
            code(CHUNKS, devices),
            half(groups, length, state_dim),
            full(KERNEL_WIDTH - 1, length, state_dim),
            full(blocks, BLOCK_HEADS, length),
            full(devices, slice_rows, state_dim),
            full(devices * CHUNKS, chunk_heads, state_dim),
            full(2 * heads, length),
            full(groups, length, 2 * GROUP_HEADS),
            pltpu.VMEM((length, state_dim), jnp.int32),
            half(CHUNKS, devices, chunk, length),
            half(devices, length, state_dim),
            full(devices, slice_rows, state_dim),
            code(CHUNKS, devices * END_SLOTS + 1),
            pltpu.VMEM((CHUNKS, devices, table_rows, state_dim), jnp.int16),
            code(CHUNKS),
            half(length, inner_dim),
            half(length, inner_dim),
            full(length, group_width),
            pltpu.SMEM((devices,), jnp.int32),
            pltpu.SMEM((docs,), jnp.int32),
            pltpu.SMEM((docs,), jnp.int32),
            pltpu.SMEM((devices * OWNER_SLOTS,), jnp.int32),
            dma((2,)), dma((2,)),
            dma((CHUNKS, devices)), dma((CHUNKS, devices)),
            dma((groups,)), dma((devices,)),
            dma((groups, per_group)), dma((devices,)),
            dma((devices,)), dma((devices,)),
            dma((steps, CHUNKS)), dma((steps, CHUNKS)),
            dma((CHUNKS,)), dma((CHUNKS, devices)),
            dma((CHUNKS, devices)), dma((CHUNKS, devices)),
            dma((2 + 3 * CHUNKS,)), dma((4,)), dma((groups,)),
        ],
        compiler_params=pltpu.CompilerParams(
            collective_id=0, has_side_effects=True, vmem_limit_bytes=VMEM_LIMIT),
        name="layer",
    )(offsets, owners, d_skip, dt_raw.T, convolution_bias[None, :], a_log[None, :], dt_bias[None, :],
      norm_weight[None, :], ssm_input, bc_input, conv_weight, gate_input)

    sources = devices // 2
    row_half = pl.BlockSpec((length // 2, inner_dim), lambda j: (j, 0))
    decode_states, final = pl.pallas_call(
        deliver_kernel,
        grid=(2,),
        in_specs=[pl.BlockSpec((CHUNKS, sources, table_rows, state_dim), lambda j: (0, j, 0, 0)), row_half],
        out_specs=[pl.BlockSpec((OWNER_SLOTS, heads // 2, head_dim, state_dim), lambda j: (0, j, 0, 0)), row_half],
        out_shape=[
            jax.ShapeDtypeStruct((OWNER_SLOTS, heads, head_dim, state_dim), jnp.float32),
            jax.ShapeDtypeStruct((length, inner_dim), jnp.bfloat16),
        ],
        compiler_params=pltpu.CompilerParams(vmem_limit_bytes=VMEM_LIMIT),
        name="deliver",
    )(delivered, gated_out)
    return (final, decode_states)


def solution(mesh):
    in_specs = (
        P(("groups", "ctx"), None),
        P(("groups", "ctx"), None),
        P(("groups", "ctx"), None),
        P(("groups", "ctx"), None),
        P("groups"),
        P("groups"),
        P(),
        P(),
        P(),
        P(),
        P(),
        P(),
    )
    out_specs = (P(("groups", "ctx"), None), P(("groups", "ctx"), None, None, None))
    return jax.shard_map(
        per_device, mesh=mesh, in_specs=in_specs, out_specs=out_specs, check_vma=False
    )
```

```python
import functools
import math
import jax
import jax.numpy as jnp
from jax import lax
from jax.experimental import pallas as pl
from jax.experimental.pallas import tpu as pltpu
from jax.sharding import PartitionSpec as P

GROUP_HEADS = 16
KERNEL_WIDTH = 4
OWNER_SLOTS = 2
BLOCK_HEADS = 4
RIM = 16
SCALE_ROWS = 16
LEVELS = 8.0
CODE_MAX = 32767.0
END_SLOTS = 4
CHUNKS = 2
VMEM_LIMIT = 56 * 1024 * 1024
MESH = pl.DeviceIdType.MESH


def encode(value):
    rows, lanes = value.shape
    parts = value.reshape(rows // SCALE_ROWS, SCALE_ROWS, lanes)
    top = jnp.max(jnp.abs(parts), axis=1)
    level = jnp.ceil(jnp.log(jnp.maximum(top, 1e-30)) * (LEVELS / math.log(2.0)))
    unit = jnp.exp2(level * (-1.0 / LEVELS)) * CODE_MAX
    coded = jnp.clip(jnp.round(parts * unit[:, None, :]), -CODE_MAX, CODE_MAX).reshape(rows, lanes)
    if level.shape[0] < SCALE_ROWS:
        level = jnp.concatenate([level, jnp.zeros((SCALE_ROWS - level.shape[0], lanes), jnp.float32)], 0)
    return coded.astype(jnp.int32).astype(jnp.int16), level.astype(jnp.int32).astype(jnp.int16)


def decode(coded, level):
    rows, lanes = coded.shape
    unit = jnp.exp2(level.astype(jnp.int32).astype(jnp.float32) * (1.0 / LEVELS)) * (1.0 / CODE_MAX)
    unit = unit[:rows // SCALE_ROWS]
    parts = coded.astype(jnp.int32).astype(jnp.float32).reshape(rows // SCALE_ROWS, SCALE_ROWS, lanes)
    return (parts * unit[:, None, :]).reshape(rows, lanes)


def conv_silu(x, rim, mask_ref, weight, bias):
    x = x.astype(jnp.float32)
    padded = jnp.concatenate([rim.astype(jnp.float32), x], 0)
    total = bias
    for tap in range(KERNEL_WIDTH - 1):
        mask = jnp.concatenate([mask_ref[tap]] * (x.shape[1] // mask_ref.shape[2]), 1)
        total = total + weight[tap:tap + 1] * (mask * pltpu.roll(padded, KERNEL_WIDTH - 1 - tap, 0)[RIM:])
    total = total + weight[KERNEL_WIDTH - 1:KERNEL_WIDTH] * x
    return (total / (1.0 + jnp.exp(-total))).astype(jnp.bfloat16)


def spread(k, count):
    half = (k + 1) // 2
    return count // 2 + half * (1 - 2 * (k % 2))


def enter(axis, me, devices):
    barrier = pltpu.get_barrier_semaphore()

    @pl.loop(1, devices)
    def _(by):
        pl.semaphore_signal(barrier, inc=1, device_id={axis: (me + by) % devices}, device_id_type=MESH)

    return barrier


def exact_dot(a, b):
    return jnp.dot(a, b, precision=lax.Precision.HIGHEST, preferred_element_type=jnp.float32)


def whole_kernel(devices, groups, relays, offsets_ref, owners_ref, skip_ref, dt_ref, bias_ref, a_ref, dt_bias_ref,
                 norm_ref, x_hbm, bc_hbm, taps_hbm, gate_hbm, out_ref, gated_hbm,
                 x_ref, bc_ref, taps_ref, rimx_scr, rimbc_scr, xs_scr, b_scr, c_scr, wt_scr, blast_scr, local_scr, code_scr, rec_scr, in_ref,
                 bsend_scr, mask_scr, end_scr, grow_scr, through_scr, rows_ref, cols_ref, start_ref, gx_scr, gb_scr,
                 gd_scr, slot_scr, table_scr, mid_scr, gate_scr, gated_scr, v_scr, first_scr, dest_scr, source_scr,
                 pick_scr,
                 rim_send, rim_recv, x_send, x_recv, b_send, b_recv, f_send, f_recv, d_send, d_recv, hand_send,
                 hand_recv, mid_send, mid_recv, out_send, out_recv, own_sem, load_sem, gated_sem):
    me = lax.axis_index("ctx")
    length, inner = x_ref.shape
    blocks = end_scr.shape[0]
    width = inner // blocks
    state_dim = blast_scr.shape[2]
    all_heads = dt_ref.shape[0]
    head_dim = inner // all_heads
    per_block = devices // blocks
    slice_width = width // per_block
    slice_heads = all_heads // devices
    chunk = slice_width // CHUNKS
    chunk_heads = max(chunk // head_dim, 1)
    per_group = devices // groups
    blocks_per_group = blocks // groups
    group_heads = all_heads // groups
    quarter = me // per_group
    place = me % per_group
    steps = relays + 2
    middle = devices // 2

    def remote(src, dst, send, recv, to):
        return pltpu.make_async_remote_copy(src_ref=src, dst_ref=dst, send_sem=send, recv_sem=recv,
                                            device_id={"ctx": to}, device_id_type=MESH)

    barrier = enter("ctx", me, devices)
    loads = [pltpu.make_async_copy(src, dst, load_sem.at[k]) for k, (src, dst) in enumerate(
        ((bc_hbm, bc_ref), (taps_hbm, taps_ref), (x_hbm, x_ref), (gate_hbm, gate_scr)))]
    for load in loads:
        load.start()

    @pl.when(me == 0)
    def _():
        rimx_scr[...] = jnp.zeros_like(rimx_scr)
        rimbc_scr[...] = jnp.zeros_like(rimbc_scr)

    base = me * length
    docs = offsets_ref.shape[0] - 1
    token = lax.broadcasted_iota(jnp.int32, (length, state_dim), 0)
    along = lax.broadcasted_iota(jnp.int32, (8, length), 1)

    def bounds(k, carry):
        start, end = carry
        offset = offsets_ref[k] - base
        start = jnp.where(offset <= token, jnp.maximum(start, offset), start)
        end = jnp.where(offset > along, jnp.minimum(end, offset), end)
        return start, end

    start, end = lax.fori_loop(0, docs + 1, bounds, (jnp.full((length, state_dim), -base, jnp.int32),
                                                     jnp.full((8, length), length, jnp.int32)))
    end = end - 1
    start_ref[...] = start
    for tap in range(KERNEL_WIDTH - 1):
        mask_scr[tap] = jnp.where(token + (tap - KERNEL_WIDTH + 1) >= start, 1.0, 0.0).astype(jnp.float32)
    last_start = jnp.max(start, axis=0, keepdims=True)
    last = token >= last_start

    pair = jnp.concatenate([dt_bias_ref[...], a_ref[...]], 1)
    pair = jnp.broadcast_to(pair, (8, 2 * all_heads)).T
    pre = dt_ref[...] + pair[:all_heads, :1]
    dt_rows = jnp.maximum(pre, 0.0) + jnp.log1p(jnp.exp(-jnp.abs(pre)))
    logdec = -dt_rows * jnp.exp(pair[all_heads:, :1])
    one = lax.broadcasted_iota(jnp.int32, (length, length), 0)
    two = lax.broadcasted_iota(jnp.int32, (length, length), 1)
    cum_rows = exact_dot(logdec, jnp.where(one <= two, 1.0, 0.0).astype(jnp.float32))
    cum_end = exact_dot(cum_rows, jnp.where(one == end[:1], 1.0, 0.0).astype(jnp.float32))
    grow = jnp.exp(cum_rows)
    rows_ref[:all_heads] = cum_rows
    rows_ref[all_heads:] = dt_rows
    weight = jnp.exp(cum_end - cum_rows) * dt_rows
    for block in range(blocks):
        end_scr[block] = weight[block * BLOCK_HEADS:(block + 1) * BLOCK_HEADS]
    first_end = jnp.min(end, axis=1, keepdims=True)[:1]
    grow_first = jnp.sum(jnp.where(lax.broadcasted_iota(jnp.int32, grow.shape, 1) == first_end, grow, 0.0), axis=1,
                         keepdims=True)
    carried = jnp.where(start[:1] < 0, jnp.broadcast_to(grow_first, (all_heads, state_dim)), 0.0)
    for device in range(devices):
        grow_scr[device, :slice_heads] = carried[device * slice_heads:(device + 1) * slice_heads]
    pl.semaphore_wait(barrier, devices - 1)

    right = (me + 1) % devices

    def rim_copy(k):
        src, dst = ((bc_hbm, rimbc_scr), (x_hbm, rimx_scr))[k]
        return remote(src.at[pl.ds(length - RIM, RIM)], dst, rim_send.at[k], rim_recv.at[k], right)

    @pl.when(me < devices - 1)
    def _():
        for k in range(2):
            rim_copy(k).start()

    def others(act):
        @pl.loop(0, devices)
        def _(k):
            to = (me + spread(k, devices)) % devices

            @pl.when(to != me)
            def _():
                act(to)

    def d_copy(to):
        return remote(grow_scr.at[to], gd_scr.at[me], d_send.at[to], d_recv.at[me], to)

    others(lambda to: d_copy(to).start())
    own_d = pltpu.make_async_copy(grow_scr.at[me], gd_scr.at[me], own_sem.at[0])
    own_d.start()

    loads[0].wait()
    loads[1].wait()

    @pl.when(me > 0)
    def _():
        rim_copy(0).wait_recv()

    def narrow(part):
        cols = slice(part * state_dim, (part + 1) * state_dim)
        after = slice(inner + part * state_dim, inner + (part + 1) * state_dim)
        return conv_silu(bc_ref[:, cols], rimbc_scr[:, cols], mask_scr, taps_ref[:, after], bias_ref[:, after])

    for part in range(groups):
        value = narrow(part)
        b_scr[:, part * state_dim:(part + 1) * state_dim] = value
        bsend_scr[part] = value
        blast_scr[part] = jnp.where(last, value, jnp.zeros_like(value))

    def b_copy(group):
        return remote(bsend_scr.at[group], gb_scr.at[me], b_send.at[group], b_recv.at[me],
                      group * per_group + place)

    own_b = pltpu.make_async_copy(bsend_scr.at[quarter], gb_scr.at[me], own_sem.at[1])
    own_b.start()
    for group in range(groups):
        @pl.when(quarter != group)
        def _():
            b_copy(group).start()

    def slice_rows(to, part):
        return pl.ds(pl.multiple_of(to * slice_width + part * chunk, chunk), chunk)

    def x_copy(part, to):
        return remote(wt_scr.at[slice_rows(to, part)], gx_scr.at[part, me], x_send.at[part, to], x_recv.at[part, me],
                      to)

    def near(device):
        return (device >= middle - 1 - relays) & (device < middle)

    def one_block(k):
        block = (me // per_block + spread(k, blocks)) % blocks
        cols = pl.ds(pl.multiple_of(block * width, width), width)
        xs = conv_silu(x_ref[:, cols], rimx_scr[:, cols], mask_scr, taps_ref[:, cols], bias_ref[:, cols])
        xs_scr[:, cols] = xs
        x_t = xs.astype(jnp.float32).T.reshape(BLOCK_HEADS, head_dim, length)
        weighted = (x_t * end_scr[block][:, None, :]).astype(jnp.bfloat16).reshape(width, length)
        wt_scr[cols, :] = weighted

        @pl.loop(0, per_block)
        def _(part):
            to = block * per_block + part

            @pl.when(to != me)
            def _():
                x_copy(0, to).start()

                @pl.when(near(me))
                def _():
                    for later in range(1, CHUNKS):
                        x_copy(later, to).start()

        local = jnp.dot(weighted, blast_scr[block // blocks_per_group], preferred_element_type=jnp.float32)
        for part in range(per_block * CHUNKS):
            local_scr[block * per_block * CHUNKS + part] = local[part * chunk:(part + 1) * chunk]

        @pl.when(me % 2 == 0)
        def _():
            for part in range(per_block * CHUNKS):
                at = block * per_block + part // CHUNKS
                coded = encode(local[part * chunk:(part + 1) * chunk])
                code_scr[part % CHUNKS, at, :chunk], code_scr[part % CHUNKS, at, chunk:] = coded

    loads[2].wait()

    @pl.when(me > 0)
    def _():
        rim_copy(1).wait_recv()

    half = blocks // 2

    @pl.loop(0, half)
    def _(k):
        one_block(k)

    def f_copy(frm, by):
        to = quarter * per_group + (place + by) % per_group
        return remote(gb_scr.at[frm], gb_scr.at[frm], f_send.at[frm // per_group, by], f_recv.at[frm], to)

    own_b.wait()
    for frm_quarter in range(groups):
        frm = frm_quarter * per_group + place

        @pl.when(quarter != frm_quarter)
        def _():
            remote(bsend_scr.at[0], gb_scr.at[frm], b_send.at[0], b_recv.at[frm], me).wait_recv()

        for by in range(1, per_group):
            f_copy(frm, by).start()

    @pl.loop(half, blocks)
    def _(k):
        one_block(k)

    for part in range(1, CHUNKS):
        @pl.when(jnp.logical_not(near(me)))
        def _():
            others(lambda to: x_copy(part, to).start())

    cum_rows = rows_ref[:all_heads]
    grow = jnp.exp(cum_rows)
    start = start_ref[...]
    last_start = jnp.max(start, axis=0, keepdims=True)
    grow_last = jnp.sum(jnp.where(lax.broadcasted_iota(jnp.int32, grow.shape, 1) == length - 1, grow, 0.0), axis=1,
                        keepdims=True)
    through = jnp.where(last_start < 0, jnp.broadcast_to(grow_last, (all_heads, state_dim)), 0.0)
    for part in range(devices * CHUNKS):
        at = part * chunk // head_dim
        through_scr[part] = through[at:at + chunk_heads]
    upright = jnp.concatenate([cum_rows, grow], 0).T
    begun = start[:, :group_heads] < 0
    for group in range(groups):
        at = group * group_heads
        cols_ref[group, :, :group_heads] = upright[:, at:at + group_heads]
        cols_ref[group, :, group_heads:] = jnp.where(begun, upright[:, all_heads + at:all_heads + at + group_heads], 0.0)

    for part in range(groups):
        c_scr[:, part * state_dim:(part + 1) * state_dim] = narrow(groups + part)

    own_x = [pltpu.make_async_copy(wt_scr.at[slice_rows(me, part)], gx_scr.at[part, me], own_sem.at[2 + part])
             for part in range(CHUNKS)]
    for copy in own_x:
        copy.start()

    sends = (me < devices - 1) & (me != middle - 1)
    receives = (me > 0) & (me != middle)

    def landing(step):
        return in_ref if step >= steps - 2 else rec_scr.at[step]

    def hand_copy(step, part):
        return remote(code_scr.at[part], landing(step).at[part], hand_send.at[step, part], hand_recv.at[step, part],
                      right)

    def hand_over(step):
        @pl.when(me % 2 == step % 2)
        def _():
            for part in range(CHUNKS):
                if step >= 2:
                    @pl.when(sends)
                    def _():
                        hand_copy(step - 2, part).wait_send()

                if step >= 1:
                    @pl.when(receives)
                    def _():
                        hand_copy(step - 1, part).wait_recv()

                    got = landing(step - 1)

                    @pl.loop(0, devices)
                    def _(at):
                        factor = through_scr[at * CHUNKS + part]
                        factor = jnp.broadcast_to(factor[:, None, :],
                                                  (chunk_heads, chunk // chunk_heads, state_dim))
                        value = decode(got[part, at, :chunk], got[part, at, chunk:])
                        value = factor.reshape(chunk, state_dim) * value + local_scr[at * CHUNKS + part]
                        code_scr[part, at, :chunk], code_scr[part, at, chunk:] = encode(value)

                @pl.when(sends)
                def _():
                    hand_copy(step, part).start()

    @pl.when(me == 0)
    def _():
        in_ref[...] = jnp.zeros_like(in_ref)
        rec_scr[...] = jnp.zeros_like(rec_scr)

    for step in range(2):
        hand_over(step)

    docs_here = owners_ref.shape[0]

    @pl.loop(0, devices)
    def _(block):
        first_scr[block] = lax.fori_loop(
            0, docs_here + 1, lambda k, n: n + (offsets_ref[k] <= block * length).astype(jnp.int32), jnp.int32(0))

    @pl.loop(0, docs_here)
    def _(doc):
        owner = owners_ref[doc]
        rank = lax.fori_loop(
            0, docs_here, lambda k, n: n + ((owners_ref[k] == owner) & (k < doc)).astype(jnp.int32), jnp.int32(0))
        end_at = offsets_ref[doc + 1] - 1
        block = lax.fori_loop(
            1, devices, lambda k, n: n + (end_at >= k * length).astype(jnp.int32), jnp.int32(0))
        dest_scr[doc] = owner * OWNER_SLOTS + rank
        slot = jnp.clip(doc + 1 - first_scr[block], 0, END_SLOTS - 1)
        source_scr[doc] = block * END_SLOTS + slot

    @pl.loop(0, devices * OWNER_SLOTS)
    def _(at):
        pick_scr[at] = lax.fori_loop(
            0, docs_here, lambda k, n: jnp.where(dest_scr[k] == at, source_scr[k], n),
            jnp.int32(devices * END_SLOTS))

    for part in range(CHUNKS):
        slot_scr[part, devices * END_SLOTS] = jnp.zeros(slot_scr.shape[2:], jnp.int16)

    row = lax.broadcasted_iota(jnp.int32, (length, state_dim), 0)
    def mid_copy(part):
        return remote(mid_scr.at[part], in_ref.at[part, me], mid_send.at[part], mid_recv.at[part, me], middle)

    own_mid = [pltpu.make_async_copy(mid_scr.at[part], in_ref.at[part, middle], own_sem.at[2 + CHUNKS + part])
               for part in range(CHUNKS)]

    def factor_rows(part, block):
        head = part * chunk // head_dim
        factor = gd_scr[block][head:head + chunk_heads]
        return jnp.broadcast_to(factor[:, None, :],
                                (chunk_heads, chunk // chunk_heads, state_dim)).reshape(chunk, state_dim)

    def block_cuts(block):
        first = block * length
        cuts = [offsets_ref[jnp.minimum(first_scr[block] + k, docs_here)] - first for k in range(END_SLOTS)]
        last_cut = jnp.int32(0)
        for cut in cuts:
            last_cut = jnp.where(cut < length, cut, last_cut)
        return cuts, last_cut

    def state_at_middle(part):
        carry = jnp.zeros((chunk, state_dim), jnp.float32)
        for block in range(middle - 1 - relays, middle):
            cuts, last_cut = block_cuts(block)
            masked = jnp.where(row >= last_cut, gb_scr[block].astype(jnp.float32), 0.0).astype(jnp.bfloat16)
            local = jnp.dot(gx_scr[part, block], masked, preferred_element_type=jnp.float32)
            carry = local + jnp.where(cuts[0] >= length, factor_rows(part, block) * carry, 0.0)
        mid_scr[part, :chunk], mid_scr[part, chunk:] = encode(carry)

        @pl.when(me != middle)
        def _():
            mid_copy(part).start()

        @pl.when(me == middle)
        def _():
            own_mid[part].start()

    def arrived(part, other):
        @pl.when(other != me)
        def _():
            remote(wt_scr.at[pl.ds(0, chunk)], gx_scr.at[part, other], x_send.at[part, other],
                   x_recv.at[part, other], other).wait_recv()

    def states(part):
        def one(block, carry):
            b_val = gb_scr[block].astype(jnp.float32)
            cuts, last_cut = block_cuts(block)
            begin, masked = jnp.int32(0), []
            for cut in cuts:
                masked.append(jnp.where((row >= begin) & (row < cut), b_val, 0.0).astype(jnp.bfloat16))
                begin = cut
            masked.append(jnp.where(row >= last_cut, b_val, 0.0).astype(jnp.bfloat16))
            local = jnp.dot(gx_scr[part, block], jnp.concatenate(masked, 1), preferred_element_type=jnp.float32)
            kept = factor_rows(part, block) * carry
            for k in range(END_SLOTS):
                value = local[:, k * state_dim:(k + 1) * state_dim]
                coded = encode(value + kept if k == 0 else value)
                at_slot = block * END_SLOTS + k
                slot_scr[part, at_slot, :chunk], slot_scr[part, at_slot, chunk:] = coded
            carry = local[:, END_SLOTS * state_dim:] + jnp.where(cuts[0] >= length, kept, 0.0)

            return carry

        lax.fori_loop(0, devices, one, jnp.zeros((chunk, state_dim), jnp.float32))

    def out_copy(part, to):
        return remote(table_scr.at[part, to], out_ref.at[part, me], out_send.at[part, to], out_recv.at[part, me], to)

    own_out = [pltpu.make_async_copy(table_scr.at[part, me], out_ref.at[part, me], own_sem.at[2 + 2 * CHUNKS + part])
               for part in range(CHUNKS)]

    own_d.wait()

    @pl.loop(0, devices)
    def _(other):
        @pl.when(other != me)
        def _():
            remote(grow_scr.at[0], gd_scr.at[other], d_send.at[other], d_recv.at[other], other).wait_recv()

        @pl.when(other % per_group != place)
        def _():
            remote(gb_scr.at[other], gb_scr.at[other], f_send.at[0, 1], f_recv.at[other], other).wait_recv()

    for copy in own_x:
        copy.wait()

    def fill(part):
        @pl.loop(0, devices)
        def _(to):
            levels = []
            for slot in range(OWNER_SLOTS):
                source = pick_scr[to * OWNER_SLOTS + slot]
                table_scr[part, to, slot * chunk:(slot + 1) * chunk] = slot_scr[part, source, :chunk]
                levels.append(slot_scr[part, source, chunk:].astype(jnp.int32)[:SCALE_ROWS // OWNER_SLOTS])
            table_scr[part, to, OWNER_SLOTS * chunk:] = jnp.concatenate(levels, 0).astype(jnp.int16)

    def near_state():
        for part in range(CHUNKS):
            if part > 0:
                for other in range(middle - 1 - relays, middle):
                    arrived(part, other)
            state_at_middle(part)

    for part in range(CHUNKS):
        @pl.loop(0, devices)
        def _(other):
            if part == 0:
                arrived(part, other)
            else:
                @pl.when(jnp.logical_not(near(other)))
                def _():
                    arrived(part, other)

        states(part)
        fill(part)
        if part == 0:
            near_state()
        others(lambda to: out_copy(part, to).start())
        own_out[part].start()

    @pl.when(me == middle)
    def _():
        for part in range(CHUNKS):
            own_mid[part].wait()

            @pl.loop(0, devices)
            def _(other):
                @pl.when(other != me)
                def _():
                    remote(mid_scr.at[part], in_ref.at[part, other], mid_send.at[part], mid_recv.at[part, other],
                           other).wait_recv()

        for step in range(1, steps - 2, 2):
            rec_scr[step] = in_ref[...]

    for step in range(2, steps):
        hand_over(step)

    @pl.when((me % 2 != (steps - 1) % 2) & receives)
    def _():
        for part in range(CHUNKS):
            hand_copy(steps - 1, part).wait_recv()

    loads[3].wait()

    def gated_copy(group):
        cols = pl.ds(pl.multiple_of(group * (inner // groups), inner // groups), inner // groups)
        return pltpu.make_async_copy(gated_scr.at[:, cols], gated_hbm.at[:, cols], gated_sem.at[group])

    @pl.loop(0, groups)
    def _(group):
        scan_group(groups, group, skip_ref, xs_scr, gate_scr, in_ref, b_scr, c_scr, rows_ref, cols_ref, start_ref,
                   norm_ref, gated_scr, v_scr)
        gated_copy(group).start()

    @pl.when(me < devices - 1)
    def _():
        for k in range(2):
            rim_copy(k).wait_send()

    @pl.when(sends)
    def _():
        for step in range(steps - 2, steps):
            @pl.when(me % 2 == step % 2)
            def _():
                for part in range(CHUNKS):
                    hand_copy(step, part).wait_send()

    @pl.when(me != middle)
    def _():
        for part in range(CHUNKS):
            mid_copy(part).wait_send()

    for group in range(groups):
        @pl.when(quarter != group)
        def _():
            b_copy(group).wait_send()

    for frm_quarter in range(groups):
        for by in range(1, per_group):
            f_copy(frm_quarter * per_group + place, by).wait_send()

    @pl.loop(0, groups)
    def _(group):
        gated_copy(group).wait()

    for part in range(CHUNKS):
        own_out[part].wait()

    @pl.loop(0, devices)
    def _(other):
        @pl.when(other != me)
        def _():
            d_copy(other).wait_send()
            for part in range(CHUNKS):
                x_copy(part, other).wait_send()
                out_copy(part, other).wait_send()
                remote(table_scr.at[part, 0], out_ref.at[part, other], out_send.at[part, other],
                       out_recv.at[part, other], other).wait_recv()


def scan_group(groups, group, skip_ref, xs_ref, gate_ref, in_ref, b_ref, c_ref, rows_ref, cols_ref, start_ref,
               norm_ref, out_ref, v_scr):
    length, inner = xs_ref.shape
    state_dim = b_ref.shape[1] // groups
    all_heads = rows_ref.shape[0] // 2
    group_heads = all_heads // groups
    group_width = inner // groups
    blocks = group_heads // BLOCK_HEADS
    width = group_width // blocks
    head_dim = width // BLOCK_HEADS
    per_block = in_ref.shape[1] // (groups * blocks)
    chunk = in_ref.shape[2] - SCALE_ROWS
    state_cols = pl.ds(pl.multiple_of(group * state_dim, state_dim), state_dim)
    c_val = c_ref[:, state_cols]
    contract = (((1,), (1,)), ((), ()))
    scores = lax.dot_general(c_val, b_ref[:, state_cols], contract, preferred_element_type=jnp.float32)
    row = lax.broadcasted_iota(jnp.int32, (length, length), 0)
    col = lax.broadcasted_iota(jnp.int32, (length, length), 1)
    causal = (col <= row) & (col >= start_ref[:, :1])
    part = lax.broadcasted_iota(jnp.int32, (length, width), 1) // head_dim
    part_row = lax.broadcasted_iota(jnp.int32, (1, width), 1) // head_dim
    cum_rows = rows_ref[pl.ds(pl.multiple_of(group * group_heads, group_heads), group_heads), :]
    dt_rows = rows_ref[pl.ds(pl.multiple_of(all_heads + group * group_heads, group_heads), group_heads), :]
    columns = cols_ref[group]
    square = jnp.zeros((length, 1), jnp.float32)
    for block in range(blocks):
        here = pl.ds(pl.multiple_of(group * group_width + block * width, width), width)
        xs = xs_ref[:, here]
        weights, split = [], []
        cont = jnp.zeros((length, width), jnp.float32)
        skip = jnp.zeros((1, width), jnp.float32)
        for head in range(BLOCK_HEADS):
            at = block * BLOCK_HEADS + head
            gap = columns[:, at:at + 1] - cum_rows[at:at + 1]
            decay = jnp.exp(jnp.where(causal, gap, -jnp.inf))
            weights.append((scores * decay * dt_rows[at:at + 1]).astype(jnp.bfloat16))
            split.append(jnp.where(part == head, xs, jnp.zeros_like(xs)))
            cont = jnp.where(part == head, columns[:, group_heads + at:group_heads + at + 1], cont)
            skip = jnp.where(part_row == head, skip_ref[group * group_heads + at], skip)
        intra = jnp.dot(jnp.concatenate(weights, 1), jnp.concatenate(split, 0), preferred_element_type=jnp.float32)
        pieces = []
        for piece in range(per_block * CHUNKS):
            at = (group * blocks + block) * per_block + piece // CHUNKS
            pieces.append(decode(in_ref[piece % CHUNKS, at, :chunk], in_ref[piece % CHUNKS, at, chunk:]))
        state = jnp.concatenate(pieces, 0)
        high = state.astype(jnp.bfloat16)
        low = (state - high.astype(jnp.float32)).astype(jnp.bfloat16)
        inter = lax.dot_general(c_val, high, contract, preferred_element_type=jnp.float32)
        inter = inter + lax.dot_general(c_val, low, contract, preferred_element_type=jnp.float32)
        y_sum = intra + inter * cont + skip * xs.astype(jnp.float32)
        gate = gate_ref[:, here].astype(jnp.float32)
        value = y_sum * (gate / (1.0 + jnp.exp(-gate)))
        v_scr[:, block * width:(block + 1) * width] = value
        square = square + jnp.sum(value * value, axis=1, keepdims=True)
    scale = lax.rsqrt(square / group_width + 1e-05)
    whole = pl.ds(pl.multiple_of(group * group_width, group_width), group_width)
    out_ref[:, whole] = (v_scr[...] * scale * norm_ref[:, whole]).astype(jnp.bfloat16)


def deliver_kernel(code_ref, gated_ref, out_ref, final_ref):
    final_ref[...] = gated_ref[...]
    sources = code_ref.shape[1]
    slots, heads, head_dim, state_dim = out_ref.shape
    chunk = (code_ref.shape[2] - SCALE_ROWS) // slots
    for source in range(sources):
        for part in range(CHUNKS):
            level = code_ref[part, source, slots * chunk:].astype(jnp.int32)
            for slot in range(slots):
                at = slot * (SCALE_ROWS // slots)
                value = decode(code_ref[part, source, slot * chunk:(slot + 1) * chunk], level[at:])
                first = (source * CHUNKS + part) * chunk
                head, row = first // head_dim, first % head_dim
                if chunk >= head_dim:
                    value = value.reshape(chunk // head_dim, head_dim, state_dim)
                    out_ref[slot, head:head + chunk // head_dim] = value
                else:
                    out_ref[slot, head, row:row + chunk] = value


def per_device(
    ssm_input,
    gate_input,
    bc_input,
    dt_raw,
    offsets,
    owners,
    conv_weight,
    convolution_bias,
    a_log,
    dt_bias,
    d_skip,
    norm_weight,
):
    length, inner_dim = ssm_input.shape
    heads = a_log.shape[0]
    head_dim = inner_dim // heads
    groups = heads // GROUP_HEADS
    state_dim = bc_input.shape[1] // (2 * groups)
    devices = lax.axis_size("ctx")
    relays = devices // 8 - 1
    blocks = heads // BLOCK_HEADS
    width = BLOCK_HEADS * head_dim
    group_state = groups * state_dim
    group_width = inner_dim // groups
    device_width = inner_dim // devices
    device_heads = heads // devices
    slice_rows = -(-device_heads // 8) * 8

    vmem = pl.BlockSpec(memory_space=pltpu.VMEM)
    smem = pl.BlockSpec(memory_space=pltpu.SMEM)
    anywhere = pl.BlockSpec(memory_space=pl.ANY)
    dma = pltpu.SemaphoreType.DMA
    per_group = devices // groups
    steps = relays + 2
    docs = owners.shape[0]
    chunk = device_width // CHUNKS
    chunk_heads = max(chunk // head_dim, 1)
    table_rows = OWNER_SLOTS * chunk + SCALE_ROWS
    code = lambda *lead: pltpu.VMEM(lead + (chunk + SCALE_ROWS, state_dim), jnp.int16)
    half = lambda *shape: pltpu.VMEM(shape, jnp.bfloat16)
    full = lambda *shape: pltpu.VMEM(shape, jnp.float32)
    delivered, gated_out = pl.pallas_call(
        functools.partial(whole_kernel, devices, groups, relays),
        in_specs=[smem] * 3 + [vmem] * 5 + [anywhere] * 4,
        out_specs=[anywhere] * 2,
        out_shape=[
            jax.ShapeDtypeStruct((CHUNKS, devices, table_rows, state_dim), jnp.int16),
            jax.ShapeDtypeStruct((length, inner_dim), jnp.bfloat16),
        ],
        scratch_shapes=[
            half(length, inner_dim),
            half(length, 2 * group_state),
            full(KERNEL_WIDTH, inner_dim + 2 * group_state),
            half(RIM, inner_dim),
            half(RIM, 2 * group_state),
            half(length, inner_dim),
            half(length, group_state),
            half(length, group_state),
            half(inner_dim, length),
            half(groups, length, state_dim),
            full(devices * CHUNKS, chunk, state_dim),
            code(CHUNKS, devices),
            code(max(relays, 1), CHUNKS, devices),
            code(CHUNKS, devices),
            half(groups, length, state_dim),
            full(KERNEL_WIDTH - 1, length, state_dim),
            full(blocks, BLOCK_HEADS, length),
            full(devices, slice_rows, state_dim),
            full(devices * CHUNKS, chunk_heads, state_dim),
            full(2 * heads, length),
            full(groups, length, 2 * GROUP_HEADS),
            pltpu.VMEM((length, state_dim), jnp.int32),
            half(CHUNKS, devices, chunk, length),
            half(devices, length, state_dim),
            full(devices, slice_rows, state_dim),
            code(CHUNKS, devices * END_SLOTS + 1),
            pltpu.VMEM((CHUNKS, devices, table_rows, state_dim), jnp.int16),
            code(CHUNKS),
            half(length, inner_dim),
            half(length, inner_dim),
            full(length, group_width),
            pltpu.SMEM((devices,), jnp.int32),
            pltpu.SMEM((docs,), jnp.int32),
            pltpu.SMEM((docs,), jnp.int32),
            pltpu.SMEM((devices * OWNER_SLOTS,), jnp.int32),
            dma((2,)), dma((2,)),
            dma((CHUNKS, devices)), dma((CHUNKS, devices)),
            dma((groups,)), dma((devices,)),
            dma((groups, per_group)), dma((devices,)),
            dma((devices,)), dma((devices,)),
            dma((steps, CHUNKS)), dma((steps, CHUNKS)),
            dma((CHUNKS,)), dma((CHUNKS, devices)),
            dma((CHUNKS, devices)), dma((CHUNKS, devices)),
            dma((2 + 3 * CHUNKS,)), dma((4,)), dma((groups,)),
        ],
        compiler_params=pltpu.CompilerParams(
            collective_id=0, has_side_effects=True, vmem_limit_bytes=VMEM_LIMIT),
        name="layer",
    )(offsets, owners, d_skip, dt_raw.T, convolution_bias[None, :], a_log[None, :], dt_bias[None, :],
      norm_weight[None, :], ssm_input, bc_input, conv_weight, gate_input)

    sources = devices // 2
    row_half = pl.BlockSpec((length // 2, inner_dim), lambda j: (j, 0))
    decode_states, final = pl.pallas_call(
        deliver_kernel,
        grid=(2,),
        in_specs=[pl.BlockSpec((CHUNKS, sources, table_rows, state_dim), lambda j: (0, j, 0, 0)), row_half],
        out_specs=[pl.BlockSpec((OWNER_SLOTS, heads // 2, head_dim, state_dim), lambda j: (0, j, 0, 0)), row_half],
        out_shape=[
            jax.ShapeDtypeStruct((OWNER_SLOTS, heads, head_dim, state_dim), jnp.float32),
            jax.ShapeDtypeStruct((length, inner_dim), jnp.bfloat16),
        ],
        compiler_params=pltpu.CompilerParams(vmem_limit_bytes=VMEM_LIMIT),
        name="deliver",
    )(delivered, gated_out)
    return (final, decode_states)


def solution(mesh):
    in_specs = (
        P(("groups", "ctx"), None),
        P(("groups", "ctx"), None),
        P(("groups", "ctx"), None),
        P(("groups", "ctx"), None),
        P("groups"),
        P("groups"),
        P(),
        P(),
        P(),
        P(),
        P(),
        P(),
    )
    out_specs = (P(("groups", "ctx"), None), P(("groups", "ctx"), None, None, None))
    return jax.shard_map(
        per_device, mesh=mesh, in_specs=in_specs, out_specs=out_specs, check_vma=False
    )
```
